32 devices in a mesh: grp: 2 (over y), gy: 4 (over z), gx: 2 (over x), ch: 2 (over core).
Axes of the slice: x: 2, y: 2, z: 4, core: 2. Of those that a mesh axis runs over, the one named last changes fastest.
Arguments:
- cells: bfloat16 [128, 128, 512], P(('grp', 'gy'), 'gx'), parts along dimension 0, may hold values from -6 to 6
- w_expand: bfloat16 [512, 2048], P(None, 'ch'), may hold values from -0.25 to 0.25
- b_expand: float32 [2048], P('ch'), may hold values from -3 to 3
- w_depth: bfloat16 [3, 3, 2048], P(None, None, 'ch'), may hold values from -2 to 2
- b_depth: float32 [2048], P('ch'), may hold values from -3 to 3
- w_project: bfloat16 [2048, 512], P('ch'), may hold values from -0.125 to 0.125
- b_project: float32 [512], replicated, may hold values from -3 to 3
- ln_gain: float32 [512], replicated, may hold values from 0.5 to 1.5
- w_qkv: bfloat16 [512, 3, 512], P(None, None, 'ch'), as said below
- w_out: bfloat16 [512, 512], P('ch'), may hold values from -0.25 to 0.25
- b_out: float32 [512], P('ch'), may hold values from -3 to 3
Outputs:
- result: bfloat16 [128, 128, 512], P(('grp', 'gy'), 'gx', 'ch'), parts along dimension 0
The draws below stay inside these ranges and needn't reach their ends.
There are 2 independent parts, one for each index of `grp`. The reference program is written for one: setup_inputs(seed, part) draws one part's arguments, and reference() takes and returns one part's arrays. A program takes and returns all parts, laid end to end along the dimension named above; an argument that names none is the same for every part. Nothing has to cross between parts.
Inputs may be any that keep to these rules, and one draw needn't show every extreme that they name: `w_qkv`: dense projection weights of every head.
All inputs are finite; a program needn't handle non-finite values.
Results may differ from the reference program's by a relative error of at most 0.01.
Values may be sent and summed in bfloat16 or wider, within the bound.
A program may use at most 64 MiB of HBM per device.

```python
import jax
import jax.numpy as jnp
from jax import lax

C = 512
EXP = 2048
HEADS = 16
HEAD_DIM = 32
GRID = 8
ROWS = 64
COLS = 128


def draw_w_qkv(key, part):
    key_base = jax.random.fold_in(key, 11)
    weight_scale = C ** (-0.5)
    return (jax.random.normal(key_base, (C, 3, C), jnp.float32) * weight_scale).astype(jnp.bfloat16)


def levels(own_key, dims, pieces, least, high):
    gain = 1.0
    for position, blocks in pieces:
        draws = jax.random.uniform(jax.random.fold_in(jax.random.fold_in(own_key, 6), position), (blocks,), jnp.float32, least / len(pieces), high / len(pieces))
        gain = gain * jnp.repeat(jnp.exp(draws), dims[position] // blocks).reshape((-1,) + (1,) * (len(dims) - 1 - position))
    return gain


def normal_values(stream_key, extent, scale, bound, split=(), kind=jnp.bfloat16):
    gain = levels(stream_key, extent, split, -0.22, 0.18) if split else 1.0
    values = jax.random.normal(stream_key, extent, jnp.float32) * scale * gain
    return jnp.minimum(jnp.maximum(values, -bound), bound).astype(kind)


def setup_inputs(seed: int = 0, part: int = 0) -> dict:
    splits = jax.random.split(jax.random.key(seed), 12)
    part_splits = jax.random.split(jax.random.fold_in(splits[11], part), 12)
    return {
        "cells": normal_values(part_splits[0], (ROWS, COLS, C), 1.0, 6.0, ((0, 4), (1, 2))),
        "w_expand": normal_values(splits[1], (C, EXP), C ** -0.5, 0.25, ((1, 2),)),
        "b_expand": normal_values(splits[2], (EXP,), 0.5, 3.0, ((0, 2),), jnp.float32),
        "w_depth": normal_values(splits[3], (3, 3, EXP), 9 ** -0.5, 2.0, ((2, 2),)),
        "b_depth": normal_values(splits[4], (EXP,), 0.5, 3.0, ((0, 2),), jnp.float32),
        "w_project": normal_values(splits[5], (EXP, C), EXP ** -0.5, 0.125, ((0, 2),)),
        "b_project": normal_values(splits[6], (C,), 0.5, 3.0, (), jnp.float32),
        "ln_gain": jnp.clip(jax.random.uniform(splits[7], (C,), jnp.float32, 0.5, 1.5), 0.5, 1.5),
        "w_qkv": draw_w_qkv(jax.random.fold_in(splits[11], 71), part),
        "w_out": normal_values(splits[9], (C, C), C ** -0.5, 0.25, ((0, 2),)),
        "b_out": normal_values(splits[10], (C,), 0.5, 3.0, ((0, 2),), jnp.float32),
    }


def gelu_exact(values):
    return jax.nn.gelu(values, approximate=False)

def normalize(source, ln_gain):
    values = source.astype(jnp.float32)
    centre = lax.optimization_barrier(jnp.mean(values, axis=-1, keepdims=True))
    centered = values - centre
    spread = lax.optimization_barrier(jnp.mean(centered * centered, axis=-1, keepdims=True))
    return (centered * lax.rsqrt(spread + 1e-05) * ln_gain).astype(jnp.bfloat16)

def reference(cells, w_expand, b_expand, w_depth, b_depth, w_project, b_project, ln_gain, w_qkv, w_out, b_out):
    rows, cols, width = cells.shape
    blocks = 8
    piece = EXP // blocks
    expand_blocks = w_expand.reshape(width, blocks, piece).transpose(1, 0, 2)
    bias_blocks = b_expand.reshape(blocks, piece)
    depth_blocks = w_depth.reshape(3, 3, blocks, piece).transpose(2, 0, 1, 3)
    depth_bias = b_depth.reshape(blocks, piece)
    project_blocks = w_project.reshape(blocks, piece, width)
    flat_cells = cells.reshape(rows * cols, width)

    def add_block(total, parts):
        w_e, b_e, w_d, b_d, w_p = parts
        pre = jnp.dot(flat_cells, w_e, preferred_element_type=jnp.float32).reshape(rows, cols, piece)
        expanded = gelu_exact(pre + b_e).astype(jnp.bfloat16)
        padded = jnp.pad(expanded, ((1, 1), (1, 1), (0, 0)))
        summed = jnp.zeros((rows, cols, piece), jnp.float32)
        for row_off in range(3):
            for col_off in range(3):
                summed = summed + padded[row_off:row_off + rows, col_off:col_off + cols].astype(jnp.float32) * w_d[row_off, col_off].astype(jnp.float32)
        depth = gelu_exact(summed + b_d).astype(jnp.bfloat16)
        term = jnp.dot(depth.reshape(rows * cols, piece), w_p, preferred_element_type=jnp.float32)
        return (total + term.reshape(rows, cols, width), None)
    total, _ = lax.scan(add_block, jnp.zeros((rows, cols, width), jnp.float32), (expand_blocks, bias_blocks, depth_blocks, depth_bias, project_blocks))
    mixed = (cells.astype(jnp.float32) + total + b_project).astype(jnp.bfloat16)
    stride_h = rows // GRID
    stride_w = cols // GRID
    windows = mixed.reshape(GRID, stride_h, GRID, stride_w, width).transpose(1, 3, 0, 2, 4)
    windows = windows.reshape(stride_h * stride_w, GRID * GRID, width)
    count = stride_h * stride_w
    tokens = GRID * GRID
    normed = normalize(windows, ln_gain).reshape(count * tokens, width)

    def project_heads(index):
        projected = jnp.dot(normed, w_qkv[:, index, :], preferred_element_type=jnp.float32).astype(jnp.bfloat16)
        return projected.reshape(count, tokens, HEADS, HEAD_DIM).transpose(2, 0, 1, 3)
    query = project_heads(0)
    keyset = project_heads(1)
    valueset = project_heads(2)

    def one_head(parts):
        head_q, head_k, head_v = parts
        scores = jnp.einsum('wqd,wkd->wqk', head_q.astype(jnp.float32), head_k.astype(jnp.float32)) * HEAD_DIM ** (-0.5)
        weights = jax.nn.softmax(scores, axis=-1).astype(jnp.bfloat16)
        return jnp.einsum('wqk,wkd->wqd', weights.astype(jnp.float32), head_v.astype(jnp.float32)).astype(jnp.bfloat16)
    heads_out = lax.map(one_head, (query, keyset, valueset))
    attended = heads_out.transpose(1, 2, 0, 3).reshape(count * tokens, width)
    projected_out = jnp.dot(attended, w_out, preferred_element_type=jnp.float32).reshape(count, tokens, width)
    outcome = (windows.astype(jnp.float32) + projected_out + b_out).astype(jnp.bfloat16)
    outcome = outcome.reshape(stride_h, stride_w, GRID, GRID, width).transpose(2, 0, 3, 1, 4)
    return outcome.reshape(rows, cols, width)
```

```python
import functools

import jax
import jax.numpy as jnp
import numpy as np
from jax import lax
from jax.experimental import pallas as pl
from jax.experimental.pallas import tpu as pltpu
from jax.sharding import PartitionSpec as P

HEAD_DIM = 32
GRID = 8
WINDOWS = 2
MESH = pl.DeviceIdType.MESH
F32 = jnp.float32
BF16 = jnp.bfloat16


def gelu(v):
    return v * (0.5 * (1.0 + lax.erf(v * np.float32(np.sqrt(0.5)))))


def dot(a, b):
    return jnp.dot(a, b, preferred_element_type=F32)


class Plan:
    def __init__(self, mesh_shape, tile_h, tile_w):
        self.n_rows, self.n_cols = mesh_shape["gy"], mesh_shape["gx"]
        self.tile_h, self.tile_w = tile_h, tile_w
        stride_h = tile_h * self.n_rows // GRID
        stride_w = tile_w * self.n_cols // GRID
        self.depth_h, self.depth_w = min(tile_h, stride_h), min(tile_w, stride_w)
        self.steps_h, self.steps_w = stride_h // self.depth_h, stride_w // self.depth_w
        self.n_i, self.n_j = tile_h // self.depth_h, tile_w // self.depth_w
        self.ph, self.pw = GRID // self.n_i, GRID // self.n_j
        self.n_t = self.n_i * self.n_j
        self.sources = self.ph * self.pw
        half_w = self.depth_w // 2
        self.slab = self.depth_w * self.n_t
        self.part = self.slab // 2
        self.pairs = half_w // WINDOWS
        self.slabs = self.sources * WINDOWS // half_w
        self.batches = self.depth_h // self.slabs
        self.piece = WINDOWS * self.n_t
        assert self.pairs % self.pw == 0 and self.pairs // self.pw * self.slabs == self.ph
        assert self.depth_h % self.slabs == 0 and self.depth_h >= 4

    def permutation(self):
        out = np.zeros((self.slab, self.slab), np.float32)
        for b in range(self.depth_w):
            for i in range(self.n_i):
                for j in range(self.n_j):
                    row = b * self.n_t + i * self.n_j + j
                    out[row, i * self.tile_w + j * self.depth_w + b] = 1
        return out

    def picks(self):
        out = np.zeros((2 * self.tile_h, self.tile_h * 16), np.float32)
        for r in range(self.tile_h):
            out[r, r * 16] = 1
            out[self.tile_h + r, r * 16 + 15] = 1
        return out

    def score_bias(self):
        rows = np.arange(self.sources * self.piece)
        window = (rows % self.piece) // self.n_t
        return np.where(window[:, None] == window[None, :], 0.0, -1e30).astype(np.float32)


def kernel(
    plan, cells_h, w_exp_h, b_exp, w_dep_in, b_dep, w_proj_h, b_proj, gain, w_qkv_h, w_out_h,
    b_out, perm, perm_t, bias_s, pick, out,
    cells, ordered, w_exp, w_proj, w_qkv, w_out, w_dep,
    exp, halo, edge, colin, edge_x, colin_x, colexp, dbuf, dperm, psend, precv, acc, fsend, frecv,
    wq_other, wo_other, bo_full, osend, oin,
    in_s, halo_s, halo_r, col_s, col_r, w_s, w_r, p_s, p_r, f_s, f_r, o_s, o_r,
):
    tile_h, tile_w = plan.tile_h, plan.tile_w
    depth_h, n_i, n_j, n_t = plan.depth_h, plan.n_i, plan.n_j, plan.n_t
    width = cells.shape[2]
    inner = w_exp.shape[1]
    slab, part, pw, slabs = plan.slab, plan.part, plan.pw, plan.slabs
    half = width // 2
    z, x, c = lax.axis_index("gy"), lax.axis_index("gx"), lax.axis_index("ch")
    zs, xs = lax.rem(z, plan.steps_h), lax.rem(x, plan.steps_w)
    mp, mq = lax.div(z, plan.steps_h), lax.div(x, plan.steps_w)
    my_s = mp * pw + mq
    my_slab = lax.rem(mp, slabs)
    my_pair = lax.div(mp, slabs) * pw + mq
    flip = (mp < plan.ph // 2).astype(jnp.int32)
    last_z, last_x = plan.n_rows - 1, plan.n_cols - 1
    partner = {"ch": 1 - c}
    has_top, has_bot = z > 0, z < last_z
    has_left, has_right = x > 0, x < last_x

    def peer(s, core):
        p, q = lax.div(s, pw), lax.rem(s, pw)
        return {"gy": p * plan.steps_h + zs, "gx": q * plan.steps_w + xs, "ch": core}

    def owner(ah, pair):
        return (lax.div(pair, pw) * slabs + ah) * pw + lax.rem(pair, pw)

    def remote(src, dst, send, recv, device):
        return pltpu.make_async_remote_copy(
            src_ref=src, dst_ref=dst, send_sem=send, recv_sem=recv,
            device_id=device, device_id_type=MESH,
        )

    loads = [
        pltpu.make_async_copy(src, dst, in_s.at[n])
        for n, (src, dst) in enumerate((
            (cells_h, cells), (w_exp_h, w_exp), (w_proj_h, w_proj), (w_qkv_h, w_qkv),
            (w_out_h, w_out),
        ))
    ]
    for load in loads:
        load.start()

    barrier = pltpu.get_barrier_semaphore()
    around = (
        (has_top, {"gy": jnp.maximum(z - 1, 0)}),
        (has_bot, {"gy": jnp.minimum(z + 1, last_z)}),
        (has_left, {"gx": jnp.maximum(x - 1, 0)}),
        (has_right, {"gx": jnp.minimum(x + 1, last_x)}),
    )
    count = jnp.int32(2 * plan.sources - 1)
    for there, device in around:
        @pl.when(there)
        def _():
            pl.semaphore_signal(barrier, inc=1, device_id=device, device_id_type=MESH)
        count = count + there.astype(jnp.int32)

    @pl.loop(0, 2 * plan.sources)
    def _(t):
        s, core = lax.div(t, 2), lax.rem(t, 2)

        @pl.when(jnp.logical_not((s == my_s) & (core == c)))
        def _():
            pl.semaphore_signal(barrier, inc=1, device_id=peer(s, core), device_id_type=MESH)

    down = remote(cells_h.at[tile_h - 1], halo.at[0], halo_s.at[0], halo_r.at[0], around[1][1])
    up = remote(cells_h.at[0], halo.at[1], halo_s.at[1], halo_r.at[1], around[0][1])
    rightward = remote(edge.at[1], colin.at[0], col_s.at[0], col_r.at[0], around[3][1])
    leftward = remote(edge.at[0], colin.at[1], col_s.at[1], col_r.at[1], around[2][1])
    rightward_x = remote(edge_x.at[1], colin_x.at[0], col_s.at[2], col_r.at[2], around[3][1])
    leftward_x = remote(edge_x.at[0], colin_x.at[1], col_s.at[3], col_r.at[3], around[2][1])
    weights = (
        remote(w_qkv_h, wq_other, w_s.at[0], w_r.at[0], partner),
        remote(w_out_h, wo_other, w_s.at[1], w_r.at[1], partner),
        remote(b_out, bo_full.at[c], w_s.at[2], w_r.at[2], partner),
    )

    for di in range(3):
        w_dep[3 * di : 3 * di + 3] = w_dep_in[di].astype(F32)
    bo_full[c] = b_out[...]
    loads[0].wait()

    for side, first in ((0, 0), (1, tile_w - 16)):
        border = cells[:, first : first + 16, :].reshape(tile_h * 16, width)
        edge[side] = dot(pick[side * tile_h : (side + 1) * tile_h], border).astype(BF16)

    def place(e, rows):
        ordered[e] = dot(perm[...], jnp.concatenate(rows, axis=0)).astype(BF16)

    def place_own(e):
        place(e, [cells[i * depth_h + e - 1] for i in range(n_i)])

    lanes_e = 256

    def expand(source, lanes):
        return gelu(dot(source, w_exp[:, lanes]) + b_exp[:, lanes])

    def expand_slab(e, mask=None):
        for n in range(inner // lanes_e):
            lanes = slice(n * lanes_e, (n + 1) * lanes_e)
            value = expand(ordered[e], lanes)
            exp[e, n_t : n_t + slab, lanes] = value if mask is None else value * mask

    def expand_own(e):
        place_own(e)
        expand_slab(e)

    ok_top, ok_bot = has_top.astype(F32), has_bot.astype(F32)
    ok_left, ok_right = has_left.astype(F32), has_right.astype(F32)

    def border_columns(e, rows):
        at = lax.broadcasted_iota(jnp.int32, (n_t, inner), 0)
        left = exp[e, slab : slab + n_t, :]
        right = exp[e, n_t : 2 * n_t, :]
        if n_t > 1:
            left = pltpu.roll(left, 1, 0)
            right = pltpu.roll(right, n_t - 1, 0)
        for i, (row, ok) in enumerate(rows):
            left = jnp.where(at == i * n_j, colexp[0, pl.ds(row, 1), :] * (ok_left * ok), left)
            right = jnp.where(
                at == i * n_j + n_j - 1, colexp[1, pl.ds(row, 1), :] * (ok_right * ok), right
            )
        exp[e, 0:n_t, :] = left
        exp[e, n_t + slab : 2 * n_t + slab, :] = right

    def border_own(e):
        border_columns(e, [(i * depth_h + e - 1, jnp.float32(1)) for i in range(n_i)])

    pl.semaphore_wait(barrier, count)

    @pl.when(has_right)
    def _():
        rightward.start()

    @pl.when(has_left)
    def _():
        leftward.start()

    @pl.when(has_bot)
    def _():
        down.start()

    @pl.when(has_top)
    def _():
        up.start()

    for copy in weights:
        copy.start()

    loads[1].wait()

    @pl.loop(1, 4)
    def _(e):
        expand_own(e)

    def await_or_zero(pairs):
        for buffer, index, there, copy in pairs:
            @pl.when(there)
            def _():
                copy.wait_recv()

            @pl.when(jnp.logical_not(there))
            def _():
                buffer[index] = jnp.zeros(buffer.shape[1:], BF16)

    await_or_zero(((colin, 0, has_left, rightward), (colin, 1, has_right, leftward)))

    def expand_columns(source, first):
        rows = source.shape[1]
        flat = source[...].reshape(2 * rows, width)
        for n in range(inner // lanes_e):
            lanes = slice(n * lanes_e, (n + 1) * lanes_e)
            value = expand(flat, lanes)
            colexp[0, first : first + rows, lanes] = value[:rows]
            colexp[1, first : first + rows, lanes] = value[rows:]

    expand_columns(colin, 0)

    @pl.loop(1, 4)
    def _(e):
        border_own(e)

    lanes_d = 128
    strips = 2
    strip = slab // strips

    def partial_copy(u):
        return remote(psend.at[u], precv.at[u], p_s.at[u], p_r.at[u], partner)

    def depth_slab(u):
        a = lax.rem(u + 1, depth_h)

        @pl.loop(0, inner // lanes_d)
        def _(chunk):
            lanes = pl.ds(pl.multiple_of(chunk * lanes_d, lanes_d), lanes_d)
            for n in range(strips):
                total = None
                for di in range(3):
                    rows = exp[a + di, n * strip : (n + 1) * strip + 2 * n_t, lanes]
                    for dj in range(3):
                        k = 3 * di + dj
                        term = rows[dj * n_t : dj * n_t + strip] * w_dep[k : k + 1, lanes]
                        total = term if total is None else total + term
                value = gelu(total + b_dep[:, lanes]).astype(BF16)
                dbuf[n * strip : (n + 1) * strip, lanes] = value

        projected = dot(dbuf[...], w_proj[...])
        dperm[0] = projected[:part]
        dperm[1] = projected[part:]
        psend[u] = dperm[1 - c].astype(BF16)
        partial_copy(u).start()
        own = ordered[a + 1, pl.ds(pl.multiple_of(c * part, part), part)]
        acc[u] = dperm[c] + own.astype(F32) + b_proj[...]

    def forward_copy(u, pair):
        m, ah = lax.div(u, slabs), lax.rem(u, slabs)
        s = owner(ah, pair)
        return s, remote(
            fsend.at[u, pair], frecv.at[m, my_s], f_s.at[u, pair], f_r.at[m, my_s], peer(s, c)
        )

    def finish(u):
        m = lax.div(u, slabs)
        partial_copy(u).wait_recv()
        mixed = (acc[u] + precv[u].astype(F32)).astype(BF16)
        for pair in range(plan.pairs):
            fsend[u, pair] = mixed[pair * plan.piece : (pair + 1) * plan.piece]

        @pl.loop(0, plan.pairs)
        def _(t):
            pair = lax.rem(t + flip * (plan.pairs // 2), plan.pairs)
            s, copy = forward_copy(u, pair)

            @pl.when(s == my_s)
            def _():
                frecv[m, my_s] = fsend[u, pair]

            @pl.when(s != my_s)
            def _():
                copy.start()

    loads[2].wait()

    early = depth_h - 3
    middle = (early + 1) // 2

    def step(u):
        @pl.when(u > 0)
        def _():
            expand_own(u + 3)
            border_own(u + 3)

        depth_slab(u)

        @pl.when(u > 0)
        def _():
            finish(u - 1)

    pl.loop(0, middle)(step)

    await_or_zero(((halo, 0, has_top, down), (halo, 1, has_bot, up)))
    place(0, [halo[0]] + [cells[i * depth_h - 1] for i in range(1, n_i)])
    place(depth_h + 1, [cells[i * depth_h] for i in range(1, n_i)] + [halo[1]])
    rows_x = edge_x.shape[1]
    at_row = lax.broadcasted_iota(jnp.int32, (rows_x, width), 0)
    for side, col in ((0, 0), (1, tile_w - 1)):
        top = halo[0].astype(F32)[col : col + 1]
        bottom = halo[1].astype(F32)[col : col + 1]
        edge_x[side] = jnp.where(at_row == 0, top, bottom).astype(BF16)

    @pl.when(has_right)
    def _():
        rightward_x.start()

    @pl.when(has_left)
    def _():
        leftward_x.start()

    pl.loop(middle, depth_h - 4)(step)

    token_row = lax.broadcasted_iota(jnp.int32, (slab, 1), 0)
    token_i = lax.rem(lax.div(token_row, n_j), n_i)
    await_or_zero(((colin_x, 0, has_left, rightward_x), (colin_x, 1, has_right, leftward_x)))
    expand_columns(colin_x, tile_h)

    one = jnp.float32(1)
    top_rows = [(tile_h, ok_top)] + [(i * depth_h - 1, one) for i in range(1, n_i)]
    bot_rows = [(i * depth_h, one) for i in range(1, n_i)] + [(tile_h + 1, ok_bot)]

    def step_late(u):
        @pl.when(u == depth_h - 4)
        def _():
            expand_own(u + 3)
            border_own(u + 3)

        @pl.when(u == depth_h - 3)
        def _():
            expand_own(u + 3)
            border_own(u + 3)

        @pl.when(u == depth_h - 2)
        def _():
            expand_slab(depth_h + 1, jnp.where(token_i == n_i - 1, ok_bot, one))
            border_columns(depth_h + 1, bot_rows)

        @pl.when(u == depth_h - 1)
        def _():
            expand_slab(0, jnp.where(token_i == 0, ok_top, one))
            border_columns(0, top_rows)

        depth_slab(u)
        finish(u - 1)

    pl.loop(depth_h - 4, depth_h)(step_late)
    finish(jnp.int32(depth_h - 1))
    loads[3].wait()
    loads[4].wait()

    for copy in weights:
        copy.wait_recv()

    def await_batch(m):
        @pl.loop(0, plan.sources)
        def _(s):
            @pl.when(s != my_s)
            def _():
                remote(
                    fsend.at[0, 0], frecv.at[m, s], f_s.at[0, 0], f_r.at[m, s], partner
                ).wait_recv()

    tokens = plan.sources * plan.piece
    heads = half // HEAD_DIM
    lane = lax.broadcasted_iota(jnp.int32, (1, half), 1)
    head_masks = [
        ((lane >= h * HEAD_DIM) & (lane < (h + 1) * HEAD_DIM)).astype(F32) for h in range(heads)
    ]

    def return_copy(m, s, side):
        return remote(
            osend.at[side, m, s], oin.at[m, my_slab, c, my_pair],
            o_s.at[side, m, s], o_r.at[m, my_slab, c, my_pair], peer(s, side),
        )

    @pl.loop(0, plan.batches)
    def _(m):
        await_batch(m)
        mixed = frecv[m].astype(F32).reshape(tokens, width)
        centered = mixed - jnp.mean(mixed, axis=-1, keepdims=True)
        spread = jnp.mean(centered * centered, axis=-1, keepdims=True)
        normed = (centered * lax.rsqrt(spread + 1e-05) * gain[...]).astype(BF16)
        total = mixed
        for wq, wo in ((w_qkv, w_out), (wq_other, wo_other)):
            query = dot(normed, wq[0]).astype(BF16)
            keyset = dot(normed, wq[1]).astype(BF16)
            valueset = dot(normed, wq[2]).astype(BF16)
            stacked = jnp.concatenate([query * n.astype(BF16) for n in head_masks], axis=0)
            scores = lax.dot_general(
                stacked, keyset, (((1,), (1,)), ((), ())), preferred_element_type=F32
            )
            scores = scores.reshape(heads, tokens, tokens) * HEAD_DIM ** (-0.5) + bias_s[...]
            top = jnp.max(scores, axis=-1, keepdims=True)
            weights_e = jnp.exp(scores - top)
            weights_e = weights_e / jnp.sum(weights_e, axis=-1, keepdims=True)
            mixed_v = dot(weights_e.astype(BF16).reshape(heads * tokens, tokens), valueset)
            attended = mixed_v[:tokens] * head_masks[0]
            for h in range(1, heads):
                attended = attended + mixed_v[h * tokens : (h + 1) * tokens] * head_masks[h]
            total = total + dot(attended.astype(BF16), wo[...])
        for side in range(2):
            lanes = slice(side * half, (side + 1) * half)
            value = (total[:, lanes] + bo_full[side]).astype(BF16)
            osend[side, m] = value.reshape(plan.sources, plan.piece, half)

        @pl.loop(0, 2 * plan.sources)
        def _(t):
            s = lax.rem(lax.div(t, 2) + flip * (plan.sources // 2), plan.sources)
            side = lax.rem(t, 2)
            mine = (s == my_s) & (side == c)

            @pl.when(mine)
            def _():
                oin[m, my_slab, c, my_pair] = osend[c, m, my_s]

            @pl.when(jnp.logical_not(mine))
            def _():
                return_copy(m, s, side).start()

    @pl.loop(0, depth_h)
    def _(u):
        m, ah = lax.div(u, slabs), lax.rem(u, slabs)
        a = lax.rem(u + 1, depth_h)

        @pl.loop(0, 2 * plan.pairs)
        def _(t):
            core, pair = lax.rem(t, 2), lax.div(t, 2)

            @pl.when(jnp.logical_not((owner(ah, pair) == my_s) & (core == c)))
            def _():
                remote(
                    osend.at[0, 0, 0], oin.at[m, ah, core, pair],
                    o_s.at[0, 0, 0], o_r.at[m, ah, core, pair], partner,
                ).wait_recv()

        arrived = oin[m, ah].astype(F32).reshape(slab, half).astype(BF16)
        placed = dot(perm_t[...], arrived).astype(BF16)
        for i in range(n_i):
            out[i * depth_h + a] = placed[i * tile_w : (i + 1) * tile_w]

    @pl.when(has_bot)
    def _():
        down.wait_send()

    @pl.when(has_top)
    def _():
        up.wait_send()

    @pl.when(has_right)
    def _():
        rightward.wait_send()
        rightward_x.wait_send()

    @pl.when(has_left)
    def _():
        leftward.wait_send()
        leftward_x.wait_send()

    for copy in weights:
        copy.wait_send()

    @pl.loop(0, depth_h)
    def _(u):
        partial_copy(u).wait_send()

        @pl.loop(0, plan.pairs)
        def _(pair):
            s, copy = forward_copy(u, pair)

            @pl.when(s != my_s)
            def _():
                copy.wait_send()

    @pl.loop(0, 2 * plan.sources)
    def _(t):
        s, side = lax.div(t, 2), lax.rem(t, 2)

        @pl.when(jnp.logical_not((s == my_s) & (side == c)))
        def _():
            for m in range(plan.batches):
                return_copy(m, s, side).wait_send()


def per_device(
    mesh_shape, cells, w_expand, b_expand, w_depth, b_depth, w_project, b_project, ln_gain,
    w_qkv, w_out, b_out,
):
    tile_h, tile_w, width = cells.shape
    plan = Plan(mesh_shape, tile_h, tile_w)
    inner = w_expand.shape[1]
    half = width // 2
    perm = plan.permutation()
    args = (
        cells, w_expand, b_expand[None], w_depth, b_depth[None],
        w_project, b_project[None], ln_gain[None], w_qkv.transpose(1, 0, 2), w_out, b_out[None],
        jnp.asarray(perm, BF16), jnp.asarray(perm.T, BF16),
        jnp.asarray(plan.score_bias()), jnp.asarray(plan.picks(), BF16),
    )
    dma = pltpu.SemaphoreType.DMA
    vmem = pltpu.VMEM
    n = plan
    rows_x = 16
    return pl.pallas_call(
        functools.partial(kernel, plan),
        out_shape=jax.ShapeDtypeStruct((tile_h, tile_w, half), BF16),
        in_specs=[
            pl.BlockSpec(memory_space=pl.ANY if at in (0, 1, 5, 8, 9) else pltpu.VMEM)
            for at in range(len(args))
        ],
        out_specs=pl.BlockSpec(memory_space=pltpu.VMEM),
        scratch_shapes=[
            vmem(cells.shape, BF16), vmem((n.depth_h + 2, n.slab, width), BF16),
            vmem(w_expand.shape, BF16), vmem(w_project.shape, BF16),
            vmem((3, width, half), BF16), vmem((half, width), BF16), vmem((9, inner), F32),
            vmem((n.depth_h + 2, n.slab + 2 * n.n_t, inner), F32),
            vmem((2, tile_w, width), BF16),
            vmem((2, tile_h, width), BF16),
            vmem((2, tile_h, width), BF16),
            vmem((2, rows_x, width), BF16),
            vmem((2, rows_x, width), BF16),
            vmem((2, tile_h + rows_x, inner), F32),
            vmem((n.slab, inner), BF16),
            vmem((2, n.part, width), F32),
            vmem((n.depth_h, n.part, width), BF16),
            vmem((n.depth_h, n.part, width), BF16),
            vmem((n.depth_h, n.part, width), F32),
            vmem((n.depth_h, n.pairs, n.piece, width), BF16),
            vmem((n.batches, n.sources, n.piece, width), BF16),
            vmem((3, width, half), BF16),
            vmem((half, width), BF16),
            vmem((2, 1, half), F32),
            vmem((2, n.batches, n.sources, n.piece, half), BF16),
            vmem((n.batches, n.slabs, 2, n.pairs, n.piece, half), BF16),
            dma((5,)),
            dma((2,)), dma((2,)), dma((4,)), dma((4,)), dma((3,)), dma((3,)),
            dma((n.depth_h,)), dma((n.depth_h,)),
            dma((n.depth_h, n.pairs)), dma((n.batches, n.sources)),
            dma((2, n.batches, n.sources)), dma((n.batches, n.slabs, 2, n.pairs)),
        ],
        compiler_params=pltpu.CompilerParams(
            collective_id=0, has_side_effects=True, vmem_limit_bytes=60 << 20
        ),
    )(*args)


def solution(mesh):
    placed = (
        P(("grp", "gy"), "gx", None),
        P(None, "ch"),
        P("ch"),
        P(None, None, "ch"),
        P("ch"),
        P("ch", None),
        P(),
        P(),
        P(None, None, "ch"),
        P("ch", None),
        P("ch"),
    )
    return jax.shard_map(
        functools.partial(per_device, dict(mesh.shape)),
        mesh=mesh,
        in_specs=placed,
        out_specs=P(("grp", "gy"), "gx", "ch"),
        check_vma=False,
    )
```

```python
import functools

import jax
import jax.numpy as jnp
import numpy as np
from jax import lax
from jax.experimental import pallas as pl
from jax.experimental.pallas import tpu as pltpu
from jax.sharding import PartitionSpec as P

HEAD_DIM = 32
GRID = 8
WINDOWS = 2
MESH = pl.DeviceIdType.MESH
F32 = jnp.float32
BF16 = jnp.bfloat16


HALF_ROOT = np.float32(np.sqrt(0.5))


def gelu_scaled(t):
    return t * (HALF_ROOT + HALF_ROOT * lax.erf(t))


def dot(a, b):
    return jnp.dot(a, b, preferred_element_type=F32)


def dot_t(a, b):
    return lax.dot_general(a, b, (((1,), (1,)), ((), ())), preferred_element_type=F32)


class Plan:
    def __init__(self, mesh_shape, tile_h, tile_w):
        self.n_rows, self.n_cols = mesh_shape["gy"], mesh_shape["gx"]
        self.tile_h, self.tile_w = tile_h, tile_w
        stride_h = tile_h * self.n_rows // GRID
        stride_w = tile_w * self.n_cols // GRID
        self.depth_h, self.depth_w = min(tile_h, stride_h), min(tile_w, stride_w)
        self.steps_h, self.steps_w = stride_h // self.depth_h, stride_w // self.depth_w
        self.n_i, self.n_j = tile_h // self.depth_h, tile_w // self.depth_w
        self.ph, self.pw = GRID // self.n_i, GRID // self.n_j
        self.n_t = self.n_i * self.n_j
        self.sources = self.ph * self.pw
        half_w = self.depth_w // 2
        self.slab = self.depth_w * self.n_t
        self.part = self.slab // 2
        self.pairs = half_w // WINDOWS
        self.slabs = self.sources * WINDOWS // half_w
        self.batches = self.depth_h // self.slabs
        self.piece = WINDOWS * self.n_t
        assert self.pairs % self.pw == 0 and self.pairs // self.pw * self.slabs == self.ph
        assert self.depth_h % self.slabs == 0 and self.depth_h >= 4

    def permutation(self):
        out = np.zeros((self.slab, self.slab), np.float32)
        for b in range(self.depth_w):
            for i in range(self.n_i):
                for j in range(self.n_j):
                    row = b * self.n_t + i * self.n_j + j
                    out[row, i * self.tile_w + j * self.depth_w + b] = 1
        return out

    def picks(self):
        out = np.zeros((2 * self.tile_h, self.tile_h * 16), np.float32)
        for r in range(self.tile_h):
            out[r, r * 16] = 1
            out[self.tile_h + r, r * 16 + 15] = 1
        return out


def kernel(
    plan, cells_h, w_exp_h, b_exp, w_dep_in, b_dep, w_proj_h, b_proj, gain, w_qkv_h, w_out_h,
    b_out, perm, perm_t, pick, out,
    cells, ordered, w_exp, w_proj, w_qkv, w_out, w_dep,
    exp, halo, edge, colin, edge_x, colin_x, colexp, dbuf, psend, precv, acc, fsend, frecv,
    b_exp_s, b_dep_s, wq_other, wo_other, w_vt, bo_full, osend, oin,
    in_s, halo_s, halo_r, col_s, col_r, w_s, w_r, p_s, p_r, f_s, f_r, o_s, o_r,
):
    tile_h, tile_w = plan.tile_h, plan.tile_w
    depth_h, n_i, n_j, n_t = plan.depth_h, plan.n_i, plan.n_j, plan.n_t
    width = cells.shape[2]
    inner = w_exp.shape[1]
    slab, part, pw, slabs = plan.slab, plan.part, plan.pw, plan.slabs
    half = width // 2
    z, x, c = lax.axis_index("gy"), lax.axis_index("gx"), lax.axis_index("ch")
    zs, xs = lax.rem(z, plan.steps_h), lax.rem(x, plan.steps_w)
    mp, mq = lax.div(z, plan.steps_h), lax.div(x, plan.steps_w)
    my_s = mp * pw + mq
    my_slab = lax.rem(mp, slabs)
    my_pair = lax.div(mp, slabs) * pw + mq
    flip = (mp < plan.ph // 2).astype(jnp.int32)
    last_z, last_x = plan.n_rows - 1, plan.n_cols - 1
    partner = {"ch": 1 - c}
    has_top, has_bot = z > 0, z < last_z
    has_left, has_right = x > 0, x < last_x

    def peer(s, core):
        p, q = lax.div(s, pw), lax.rem(s, pw)
        return {"gy": p * plan.steps_h + zs, "gx": q * plan.steps_w + xs, "ch": core}

    def owner(ah, pair):
        return (lax.div(pair, pw) * slabs + ah) * pw + lax.rem(pair, pw)

    def remote(src, dst, send, recv, device):
        return pltpu.make_async_remote_copy(
            src_ref=src, dst_ref=dst, send_sem=send, recv_sem=recv,
            device_id=device, device_id_type=MESH,
        )

    loads = [
        pltpu.make_async_copy(src, dst, in_s.at[n])
        for n, (src, dst) in enumerate((
            (cells_h, cells), (w_exp_h, w_exp), (w_proj_h, w_proj), (w_qkv_h, w_qkv),
            (w_out_h, w_out),
        ))
    ]
    for load in loads[:2]:
        load.start()

    barrier = pltpu.get_barrier_semaphore()
    around = (
        (has_top, {"gy": jnp.maximum(z - 1, 0)}),
        (has_bot, {"gy": jnp.minimum(z + 1, last_z)}),
        (has_left, {"gx": jnp.maximum(x - 1, 0)}),
        (has_right, {"gx": jnp.minimum(x + 1, last_x)}),
    )
    count = jnp.int32(2 * plan.sources - 1)
    for there, device in around:
        @pl.when(there)
        def _():
            pl.semaphore_signal(barrier, inc=1, device_id=device, device_id_type=MESH)
        count = count + there.astype(jnp.int32)

    @pl.loop(0, 2 * plan.sources)
    def _(t):
        s, core = lax.div(t, 2), lax.rem(t, 2)

        @pl.when(jnp.logical_not((s == my_s) & (core == c)))
        def _():
            pl.semaphore_signal(barrier, inc=1, device_id=peer(s, core), device_id_type=MESH)

    down = remote(cells_h.at[tile_h - 1], halo.at[0], halo_s.at[0], halo_r.at[0], around[1][1])
    up = remote(cells_h.at[0], halo.at[1], halo_s.at[1], halo_r.at[1], around[0][1])
    rightward = remote(edge.at[1], colin.at[0], col_s.at[0], col_r.at[0], around[3][1])
    leftward = remote(edge.at[0], colin.at[1], col_s.at[1], col_r.at[1], around[2][1])
    rightward_x = remote(edge_x.at[1], colin_x.at[0], col_s.at[2], col_r.at[2], around[3][1])
    leftward_x = remote(edge_x.at[0], colin_x.at[1], col_s.at[3], col_r.at[3], around[2][1])
    weights = (
        remote(w_qkv_h, wq_other, w_s.at[0], w_r.at[0], partner),
        remote(w_out_h, wo_other, w_s.at[1], w_r.at[1], partner),
        remote(b_out, bo_full.at[c], w_s.at[2], w_r.at[2], partner),
    )

    for di in range(3):
        w_dep[3 * di : 3 * di + 3] = w_dep_in[di].astype(F32) * HALF_ROOT
    b_exp_s[...] = b_exp[...] * HALF_ROOT
    b_dep_s[...] = b_dep[...] * HALF_ROOT
    bo_full[c] = b_out[...]
    loads[0].wait()
    loads[2].start()

    for side, first in ((0, 0), (1, tile_w - 16)):
        border = cells[:, first : first + 16, :].reshape(tile_h * 16, width)
        edge[side] = dot(pick[side * tile_h : (side + 1) * tile_h], border).astype(BF16)

    def place(e, rows):
        ordered[e] = dot(perm[...], jnp.concatenate(rows, axis=0)).astype(BF16)

    @pl.loop(1, depth_h + 1)
    def _(e):
        place(e, [cells[i * depth_h + e - 1] for i in range(n_i)])

    lanes_e = 256

    def expand(source, lanes):
        return gelu_scaled(dot(source, w_exp[:, lanes]) * HALF_ROOT + b_exp_s[:, lanes])

    def expand_chunk(e, lanes, mask=None):
        value = expand(ordered[e], lanes)
        exp[e, n_t : n_t + slab, lanes] = value if mask is None else value * mask

    ok_top, ok_bot = has_top.astype(F32), has_bot.astype(F32)
    ok_left, ok_right = has_left.astype(F32), has_right.astype(F32)

    def border_columns(e):
        at = lax.broadcasted_iota(jnp.int32, (n_t, inner), 0)
        left = exp[e, slab : slab + n_t, :]
        right = exp[e, n_t : 2 * n_t, :]
        if n_t > 1:
            left = pltpu.roll(left, 1, 0)
            right = pltpu.roll(right, n_t - 1, 0)
        for i in range(n_i):
            row = i * depth_h + e - 1
            above, below = row < 0, row >= tile_h
            ok = jnp.where(above, ok_top, jnp.where(below, ok_bot, jnp.float32(1)))
            row = jnp.where(above, tile_h, jnp.where(below, tile_h + 1, row))
            left = jnp.where(at == i * n_j, colexp[0, pl.ds(row, 1), :] * (ok_left * ok), left)
            right = jnp.where(
                at == i * n_j + n_j - 1, colexp[1, pl.ds(row, 1), :] * (ok_right * ok), right
            )
        exp[e, 0:n_t, :] = left
        exp[e, n_t + slab : 2 * n_t + slab, :] = right

    pl.semaphore_wait(barrier, count)

    @pl.when(has_right)
    def _():
        rightward.start()

    @pl.when(has_left)
    def _():
        leftward.start()

    @pl.when(has_bot)
    def _():
        down.start()

    @pl.when(has_top)
    def _():
        up.start()

    for copy in weights:
        copy.start()

    loads[1].wait()
    loads[3].start()
    loads[4].start()

    @pl.loop(1, 4)
    def _(e):
        for n in range(inner // lanes_e):
            expand_chunk(e, slice(n * lanes_e, (n + 1) * lanes_e))

    def await_or_zero(pairs):
        for buffer, index, there, copy in pairs:
            @pl.when(there)
            def _():
                copy.wait_recv()

            @pl.when(jnp.logical_not(there))
            def _():
                buffer[index] = jnp.zeros(buffer.shape[1:], BF16)

    await_or_zero(((colin, 0, has_left, rightward), (colin, 1, has_right, leftward)))

    def expand_columns(source, first):
        rows = source.shape[1]
        flat = source[...].reshape(2 * rows, width)
        for n in range(inner // lanes_e):
            lanes = slice(n * lanes_e, (n + 1) * lanes_e)
            value = expand(flat, lanes)
            colexp[0, first : first + rows, lanes] = value[:rows]
            colexp[1, first : first + rows, lanes] = value[rows:]

    expand_columns(colin, 0)

    @pl.loop(1, 4)
    def _(e):
        border_columns(e)

    lanes_d = 128

    def partial_copy(u):
        return remote(psend.at[u], precv.at[u], p_s.at[u], p_r.at[u], partner)

    def depth_slab(u, ahead=True, mask_of=None):
        a = lax.rem(u + 1, depth_h)
        e = lax.rem(u + 4, depth_h + 2)
        mask = None if mask_of is None else mask_of(e)

        @pl.loop(0, inner // lanes_e)
        def _(chunk):
            for n in range(2):
                for sub in range(lanes_e // lanes_d):
                    lanes = pl.ds(
                        pl.multiple_of(chunk * lanes_e + sub * lanes_d, lanes_d), lanes_d
                    )
                    total = None
                    for di in range(3):
                        rows = exp[a + di, n * part : (n + 1) * part + 2 * n_t, lanes]
                        for dj in range(3):
                            k = 3 * di + dj
                            term = rows[dj * n_t : dj * n_t + part] * w_dep[k : k + 1, lanes]
                            total = term if total is None else total + term
                    value = gelu_scaled(total + b_dep_s[:, lanes]).astype(BF16)
                    first = pl.multiple_of(jnp.where(c == n, part, 0), part)
                    dbuf[pl.ds(first, part), lanes] = value
            if ahead:
                expand_chunk(e, pl.ds(pl.multiple_of(chunk * lanes_e, lanes_e), lanes_e), mask)

        if ahead:
            border_columns(e)
        projected = dot(dbuf[...], w_proj[...])
        psend[u] = projected[:part].astype(BF16)
        partial_copy(u).start()
        own = ordered[a + 1, pl.ds(pl.multiple_of(c * part, part), part)]
        acc[u] = projected[part:] + own.astype(F32) + b_proj[...]

    def forward_copy(u, pair):
        m, ah = lax.div(u, slabs), lax.rem(u, slabs)
        s = owner(ah, pair)
        return s, remote(
            fsend.at[u, pair], frecv.at[m, my_s], f_s.at[u, pair], f_r.at[m, my_s], peer(s, c)
        )

    def finish(u):
        m = lax.div(u, slabs)
        partial_copy(u).wait_recv()
        mixed = (acc[u] + precv[u].astype(F32)).astype(BF16)
        for pair in range(plan.pairs):
            fsend[u, pair] = mixed[pair * plan.piece : (pair + 1) * plan.piece]

        @pl.loop(0, plan.pairs)
        def _(t):
            pair = lax.rem(t + flip * (plan.pairs // 2), plan.pairs)
            s, copy = forward_copy(u, pair)

            @pl.when(s == my_s)
            def _():
                frecv[m, my_s] = fsend[u, pair]

            @pl.when(s != my_s)
            def _():
                copy.start()

    loads[2].wait()

    def step(u):
        depth_slab(u)

        @pl.when(u > 0)
        def _():
            finish(u - 1)

    middle = (depth_h - 3) // 2 + 1
    pl.loop(0, middle)(step)

    await_or_zero(((halo, 0, has_top, down), (halo, 1, has_bot, up)))
    place(0, [halo[0]] + [cells[i * depth_h - 1] for i in range(1, n_i)])
    place(depth_h + 1, [cells[i * depth_h] for i in range(1, n_i)] + [halo[1]])
    rows_x = edge_x.shape[1]
    at_row = lax.broadcasted_iota(jnp.int32, (rows_x, width), 0)
    for side, col in ((0, 0), (1, tile_w - 1)):
        top = halo[0].astype(F32)[col : col + 1]
        bottom = halo[1].astype(F32)[col : col + 1]
        edge_x[side] = jnp.where(at_row == 0, top, bottom).astype(BF16)

    @pl.when(has_right)
    def _():
        rightward_x.start()

    @pl.when(has_left)
    def _():
        leftward_x.start()

    pl.loop(middle, depth_h - 3)(step)

    await_or_zero(((colin_x, 0, has_left, rightward_x), (colin_x, 1, has_right, leftward_x)))
    expand_columns(colin_x, tile_h)
    token_row = lax.broadcasted_iota(jnp.int32, (slab, 1), 0)
    token_i = lax.rem(lax.div(token_row, n_j), n_i)

    def mask_of(e):
        outside = jnp.where(
            e == 0,
            jnp.where(token_i == 0, 1 - ok_top, 0.0),
            jnp.where(token_i == n_i - 1, 1 - ok_bot, 0.0),
        )
        return 1 - outside

    @pl.loop(depth_h - 3, depth_h - 1)
    def _(u):
        depth_slab(u, mask_of=mask_of)
        finish(u - 1)

    depth_slab(jnp.int32(depth_h - 1), ahead=False)
    finish(jnp.int32(depth_h - 2))
    finish(jnp.int32(depth_h - 1))
    loads[3].wait()
    loads[4].wait()

    for copy in weights:
        copy.wait_recv()

    eye = (
        lax.broadcasted_iota(jnp.int32, (half, half), 0)
        == lax.broadcasted_iota(jnp.int32, (half, half), 1)
    ).astype(F32).astype(BF16)
    for n, wq in enumerate((w_qkv, wq_other)):
        w_vt[n] = dot_t(eye, wq[2]).astype(BF16)

    def await_batch(m):
        @pl.loop(0, plan.sources)
        def _(s):
            @pl.when(s != my_s)
            def _():
                remote(
                    fsend.at[0, 0], frecv.at[m, s], f_s.at[0, 0], f_r.at[m, s], partner
                ).wait_recv()

    keys = plan.sources * n_t
    tokens = WINDOWS * keys
    group = 128
    n_g = half // group
    n_h = group // HEAD_DIM
    lane = lax.broadcasted_iota(jnp.int32, (1, WINDOWS * half), 1)
    head_masks = [
        (lax.rem(lax.div(lane, HEAD_DIM), n_h) == h).astype(F32).astype(BF16) for h in range(n_h)
    ]
    lane_w = lax.div(lax.broadcasted_iota(jnp.int32, (1, tokens), 1), keys)
    window_masks = [(lane_w == w).astype(F32).astype(BF16) for w in range(WINDOWS)]
    scale = np.float32(HEAD_DIM ** (-0.5) * np.log2(np.e))

    def attend(normed, wq, wvt):
        query = (dot(normed, wq[0]) * scale).astype(BF16)
        keyset = dot(normed, wq[1]).astype(BF16)
        values = dot_t(wvt, normed).astype(BF16)
        blank = jnp.zeros((keys, group), BF16)
        blocks = [(w, g) for w in range(WINDOWS) for g in range(n_g)]
        right = jnp.concatenate([
            jnp.concatenate([
                query[w * keys : (w + 1) * keys, g * group : (g + 1) * group]
                if block == (w, g) else blank
                for block in blocks
            ], axis=1)
            for g in range(n_g) for w in range(WINDOWS)
        ], axis=0)
        left = jnp.concatenate([keyset[w * keys : (w + 1) * keys] for w in range(WINDOWS)], axis=1)
        left = jnp.concatenate([left * mask for mask in head_masks], axis=0)
        scores = dot_t(left, right).reshape(n_h, keys, n_g * tokens)
        top = jnp.max(scores, axis=1, keepdims=True)
        weights_e = jnp.exp2(scores - top)
        share = 1.0 / jnp.sum(weights_e, axis=1, keepdims=True)
        weights_e = weights_e.astype(BF16)
        nothing = jnp.zeros((HEAD_DIM, tokens), BF16)
        parts = []
        for g in range(n_g):
            lanes = slice(g * tokens, (g + 1) * tokens)
            spread = jnp.concatenate(
                [weights_e[h, :, lanes] * mask for h in range(n_h) for mask in window_masks], axis=0
            )
            mine = values[g * group : (g + 1) * group]
            stacked = jnp.concatenate([
                jnp.concatenate([
                    mine[h * HEAD_DIM : (h + 1) * HEAD_DIM] if h == at else nothing
                    for at in range(n_h)
                ], axis=1)
                for h in range(n_h)
            ], axis=0)
            found = dot(stacked, spread).reshape(n_h, HEAD_DIM, tokens) * share[:, :, lanes]
            parts.append(found.reshape(group, tokens).astype(BF16))
        found = jnp.concatenate(parts, axis=0)
        return dot_t(eye[:tokens, :tokens], found).astype(BF16)

    def return_copy(m, s, side):
        return remote(
            osend.at[side, m, s], oin.at[m, my_slab, c, my_pair],
            o_s.at[side, m, s], o_r.at[m, my_slab, c, my_pair], peer(s, side),
        )

    @pl.loop(0, plan.batches)
    def _(m):
        await_batch(m)
        came = frecv[m].astype(F32)
        mixed = jnp.concatenate([
            came[:, w * n_t : (w + 1) * n_t].reshape(keys, width) for w in range(WINDOWS)
        ], axis=0)
        centered = mixed - jnp.mean(mixed, axis=-1, keepdims=True)
        spread = jnp.mean(centered * centered, axis=-1, keepdims=True)
        normed = (centered * lax.rsqrt(spread + 1e-05) * gain[...]).astype(BF16)
        attended = [
            attend(normed, wq, w_vt[n]) for n, wq in enumerate((w_qkv, wq_other))
        ]
        total = mixed + dot(attended[0], w_out[...]) + dot(attended[1], wo_other[...])
        for side in range(2):
            lanes = slice(side * half, (side + 1) * half)
            value = total[:, lanes] + bo_full[side]
            value = jnp.concatenate([
                value[w * keys : (w + 1) * keys].reshape(plan.sources, n_t, half)
                for w in range(WINDOWS)
            ], axis=1)
            osend[side, m] = value.astype(BF16)

        @pl.loop(0, 2 * plan.sources)
        def _(t):
            s = lax.rem(lax.div(t, 2) + flip * (plan.sources // 2), plan.sources)
            side = lax.rem(t, 2)
            mine = (s == my_s) & (side == c)

            @pl.when(mine)
            def _():
                oin[m, my_slab, c, my_pair] = osend[c, m, my_s]

            @pl.when(jnp.logical_not(mine))
            def _():
                return_copy(m, s, side).start()

    @pl.loop(0, depth_h)
    def _(u):
        m, ah = lax.div(u, slabs), lax.rem(u, slabs)
        a = lax.rem(u + 1, depth_h)

        @pl.loop(0, 2 * plan.pairs)
        def _(t):
            core, pair = lax.rem(t, 2), lax.div(t, 2)

            @pl.when(jnp.logical_not((owner(ah, pair) == my_s) & (core == c)))
            def _():
                remote(
                    osend.at[0, 0, 0], oin.at[m, ah, core, pair],
                    o_s.at[0, 0, 0], o_r.at[m, ah, core, pair], partner,
                ).wait_recv()

        arrived = oin[m, ah].astype(F32).reshape(slab, half).astype(BF16)
        placed = dot(perm_t[...], arrived).astype(BF16)
        for i in range(n_i):
            out[i * depth_h + a] = placed[i * tile_w : (i + 1) * tile_w]

    @pl.when(has_bot)
    def _():
        down.wait_send()

    @pl.when(has_top)
    def _():
        up.wait_send()

    @pl.when(has_right)
    def _():
        rightward.wait_send()
        rightward_x.wait_send()

    @pl.when(has_left)
    def _():
        leftward.wait_send()
        leftward_x.wait_send()

    for copy in weights:
        copy.wait_send()

    @pl.loop(0, depth_h)
    def _(u):
        partial_copy(u).wait_send()

        @pl.loop(0, plan.pairs)
        def _(pair):
            s, copy = forward_copy(u, pair)

            @pl.when(s != my_s)
            def _():
                copy.wait_send()

    @pl.loop(0, 2 * plan.sources)
    def _(t):
        s, side = lax.div(t, 2), lax.rem(t, 2)

        @pl.when(jnp.logical_not((s == my_s) & (side == c)))
        def _():
            for m in range(plan.batches):
                return_copy(m, s, side).wait_send()


def per_device(
    mesh_shape, cells, w_expand, b_expand, w_depth, b_depth, w_project, b_project, ln_gain,
    w_qkv, w_out, b_out,
):
    tile_h, tile_w, width = cells.shape
    plan = Plan(mesh_shape, tile_h, tile_w)
    inner = w_expand.shape[1]
    half = width // 2
    perm = plan.permutation()
    args = (
        cells, w_expand, b_expand[None], w_depth, b_depth[None],
        w_project, b_project[None], ln_gain[None], w_qkv.transpose(1, 0, 2), w_out, b_out[None],
        jnp.asarray(perm, BF16), jnp.asarray(perm.T, BF16),
        jnp.asarray(plan.picks(), BF16),
    )
    dma = pltpu.SemaphoreType.DMA
    vmem = pltpu.VMEM
    n = plan
    rows_x = 16
    return pl.pallas_call(
        functools.partial(kernel, plan),
        out_shape=jax.ShapeDtypeStruct((tile_h, tile_w, half), BF16),
        in_specs=[
            pl.BlockSpec(memory_space=pl.ANY if at in (0, 1, 5, 8, 9) else pltpu.VMEM)
            for at in range(len(args))
        ],
        out_specs=pl.BlockSpec(memory_space=pltpu.VMEM),
        scratch_shapes=[
            vmem(cells.shape, BF16), vmem((n.depth_h + 2, n.slab, width), BF16),
            vmem(w_expand.shape, BF16), vmem(w_project.shape, BF16),
            vmem((3, width, half), BF16), vmem((half, width), BF16), vmem((9, inner), F32),
            vmem((n.depth_h + 2, n.slab + 2 * n.n_t, inner), F32),
            vmem((2, tile_w, width), BF16),
            vmem((2, tile_h, width), BF16),
            vmem((2, tile_h, width), BF16),
            vmem((2, rows_x, width), BF16),
            vmem((2, rows_x, width), BF16),
            vmem((2, tile_h + rows_x, inner), F32),
            vmem((n.slab, inner), BF16),
            vmem((n.depth_h, n.part, width), BF16),
            vmem((n.depth_h, n.part, width), BF16),
            vmem((n.depth_h, n.part, width), F32),
            vmem((n.depth_h, n.pairs, n.piece, width), BF16),
            vmem((n.batches, n.sources, n.piece, width), BF16),
            vmem((1, inner), F32), vmem((1, inner), F32),
            vmem((3, width, half), BF16),
            vmem((half, width), BF16),
            vmem((2, half, width), BF16),
            vmem((2, 1, half), F32),
            vmem((2, n.batches, n.sources, n.piece, half), BF16),
            vmem((n.batches, n.slabs, 2, n.pairs, n.piece, half), BF16),
            dma((5,)),
            dma((2,)), dma((2,)), dma((4,)), dma((4,)), dma((3,)), dma((3,)),
            dma((n.depth_h,)), dma((n.depth_h,)),
            dma((n.depth_h, n.pairs)), dma((n.batches, n.sources)),
            dma((2, n.batches, n.sources)), dma((n.batches, n.slabs, 2, n.pairs)),
        ],
        compiler_params=pltpu.CompilerParams(
            collective_id=0, has_side_effects=True, vmem_limit_bytes=60 << 20
        ),
    )(*args)


def solution(mesh):
    placed = (
        P(("grp", "gy"), "gx", None),
        P(None, "ch"),
        P("ch"),
        P(None, None, "ch"),
        P("ch"),
        P("ch", None),
        P(),
        P(),
        P(None, None, "ch"),
        P("ch", None),
        P("ch"),
    )
    return jax.shard_map(
        functools.partial(per_device, dict(mesh.shape)),
        mesh=mesh,
        in_specs=placed,
        out_specs=P(("grp", "gy"), "gx", "ch"),
        check_vma=False,
    )
```

```python
import functools

import jax
import jax.numpy as jnp
import numpy as np
from jax import lax
from jax.experimental import pallas as pl
from jax.experimental.pallas import tpu as pltpu
from jax.sharding import PartitionSpec as P

HEAD_DIM = 32
GRID = 8
WINDOWS = 2
MESH = pl.DeviceIdType.MESH
F32 = jnp.float32
BF16 = jnp.bfloat16


HALF_ROOT = np.float32(np.sqrt(0.5))


def gelu_scaled(t):
    return t * (HALF_ROOT + HALF_ROOT * lax.erf(t))


def dot(a, b):
    return jnp.dot(a, b, preferred_element_type=F32)


def dot_t(a, b):
    return lax.dot_general(a, b, (((1,), (1,)), ((), ())), preferred_element_type=F32)


class Plan:
    def __init__(self, mesh_shape, tile_h, tile_w):
        self.n_rows, self.n_cols = mesh_shape["gy"], mesh_shape["gx"]
        self.tile_h, self.tile_w = tile_h, tile_w
        stride_h = tile_h * self.n_rows // GRID
        stride_w = tile_w * self.n_cols // GRID
        self.depth_h, self.depth_w = min(tile_h, stride_h), min(tile_w, stride_w)
        self.steps_h, self.steps_w = stride_h // self.depth_h, stride_w // self.depth_w
        self.n_i, self.n_j = tile_h // self.depth_h, tile_w // self.depth_w
        self.ph, self.pw = GRID // self.n_i, GRID // self.n_j
        self.n_t = self.n_i * self.n_j
        self.sources = self.ph * self.pw
        half_w = self.depth_w // 2
        self.slab = self.depth_w * self.n_t
        self.part = self.slab // 2
        self.pairs = half_w // WINDOWS
        self.slabs = self.sources * WINDOWS // half_w
        self.batches = self.depth_h // self.slabs
        self.piece = WINDOWS * self.n_t
        assert self.pairs % self.pw == 0 and self.pairs // self.pw * self.slabs == self.ph
        assert self.depth_h % self.slabs == 0 and self.depth_h >= 4


def kernel(
    plan, cells_h, w_exp_h, b_exp_h, w_dep_h, b_dep_h, w_proj_h, b_proj_h, gain_h, w_qkv_h, w_out_h,
    b_out_h, out,
    b_exp, w_dep_in, b_dep, b_proj, gain, cells, ordered, w_exp, w_proj, w_qkv, w_out, w_dep,
    exp, halo, edge, colin, edge_x, colin_x, colexp, dbuf, psend, precv, acc, fsend, frecv,
    b_exp_s, b_dep_s, w_vt, bo_full, osend, oin,
    in_s, halo_s, halo_r, col_s, col_r, w_s, w_r, p_s, p_r, f_s, f_r, o_s, o_r,
):
    tile_h, tile_w = plan.tile_h, plan.tile_w
    depth_h, n_i, n_j, n_t = plan.depth_h, plan.n_i, plan.n_j, plan.n_t
    width = cells.shape[2]
    inner = w_exp.shape[1]
    slab, part, pw, slabs = plan.slab, plan.part, plan.pw, plan.slabs
    half = width // 2
    z, x, c = lax.axis_index("gy"), lax.axis_index("gx"), lax.axis_index("ch")
    zs, xs = lax.rem(z, plan.steps_h), lax.rem(x, plan.steps_w)
    mp, mq = lax.div(z, plan.steps_h), lax.div(x, plan.steps_w)
    my_s = mp * pw + mq
    my_slab = lax.rem(mp, slabs)
    my_pair = lax.div(mp, slabs) * pw + mq
    flip = (mp < plan.ph // 2).astype(jnp.int32)
    last_z, last_x = plan.n_rows - 1, plan.n_cols - 1
    partner = {"ch": 1 - c}
    has_top, has_bot = z > 0, z < last_z
    has_left, has_right = x > 0, x < last_x

    def peer(s, core):
        p, q = lax.div(s, pw), lax.rem(s, pw)
        return {"gy": p * plan.steps_h + zs, "gx": q * plan.steps_w + xs, "ch": core}

    def owner(ah, pair):
        return (lax.div(pair, pw) * slabs + ah) * pw + lax.rem(pair, pw)

    def remote(src, dst, send, recv, device):
        return pltpu.make_async_remote_copy(
            src_ref=src, dst_ref=dst, send_sem=send, recv_sem=recv,
            device_id=device, device_id_type=MESH,
        )

    mine = pl.ds(pl.multiple_of(c * half, half), half)
    loads = [
        pltpu.make_async_copy(src, dst, in_s.at[n])
        for n, (src, dst) in enumerate((
            (cells_h, cells), (w_exp_h, w_exp), (w_proj_h, w_proj),
            (w_qkv_h, w_qkv.at[:, :, mine]), (w_out_h, w_out.at[mine]),
            (b_exp_h, b_exp), (w_dep_h, w_dep_in), (b_dep_h, b_dep), (b_proj_h, b_proj),
            (gain_h, gain), (b_out_h, bo_full.at[c]),
        ))
    ]
    small = loads[5:]
    for load in loads[:2] + small + loads[2:3]:
        load.start()

    barrier = pltpu.get_barrier_semaphore()
    around = (
        (has_top, {"gy": jnp.maximum(z - 1, 0)}),
        (has_bot, {"gy": jnp.minimum(z + 1, last_z)}),
        (has_left, {"gx": jnp.maximum(x - 1, 0)}),
        (has_right, {"gx": jnp.minimum(x + 1, last_x)}),
    )
    count = jnp.int32(2 * plan.sources - 1)
    for there, device in around:
        @pl.when(there)
        def _():
            pl.semaphore_signal(barrier, inc=1, device_id=device, device_id_type=MESH)
        count = count + there.astype(jnp.int32)

    @pl.loop(0, 2 * plan.sources)
    def _(t):
        s, core = lax.div(t, 2), lax.rem(t, 2)

        @pl.when(jnp.logical_not((s == my_s) & (core == c)))
        def _():
            pl.semaphore_signal(barrier, inc=1, device_id=peer(s, core), device_id_type=MESH)

    down = remote(cells_h.at[tile_h - 1], halo.at[0], halo_s.at[0], halo_r.at[0], around[1][1])
    up = remote(cells_h.at[0], halo.at[1], halo_s.at[1], halo_r.at[1], around[0][1])
    rightward = remote(edge.at[1], colin.at[0], col_s.at[0], col_r.at[0], around[3][1])
    leftward = remote(edge.at[0], colin.at[1], col_s.at[1], col_r.at[1], around[2][1])
    rightward_x = remote(edge_x.at[1], colin_x.at[0], col_s.at[2], col_r.at[2], around[3][1])
    leftward_x = remote(edge_x.at[0], colin_x.at[1], col_s.at[3], col_r.at[3], around[2][1])
    weights = (
        remote(w_qkv_h, w_qkv.at[:, :, mine], w_s.at[0], w_r.at[0], partner),
        remote(w_out_h, w_out.at[mine], w_s.at[1], w_r.at[1], partner),
        remote(b_out_h, bo_full.at[c], w_s.at[2], w_r.at[2], partner),
    )

    def one_hot(rows, columns, source):
        row = lax.broadcasted_iota(jnp.int32, (rows, columns), 0)
        column = lax.broadcasted_iota(jnp.int32, (rows, columns), 1)
        return source(row, column).astype(F32).astype(BF16)

    def cell_of(row):
        b, i, j = lax.div(row, n_t), lax.div(lax.rem(row, n_t), n_j), lax.rem(row, n_j)
        return i * tile_w + j * plan.depth_w + b

    perm = one_hot(slab, slab, lambda row, column: cell_of(row) == column)
    picks = [
        one_hot(tile_h, tile_h * 16, lambda row, column: row * 16 + at == column) for at in (0, 15)
    ]
    loads[0].wait()

    for side, first in ((0, 0), (1, tile_w - 16)):
        border = cells[:, first : first + 16, :].reshape(tile_h * 16, width)
        edge[side] = dot(picks[side], border).astype(BF16)

    def place(e, rows):
        ordered[e] = dot(perm, jnp.concatenate(rows, axis=0)).astype(BF16)

    @pl.loop(1, depth_h + 1)
    def _(e):
        place(e, [cells[i * depth_h + e - 1] for i in range(n_i)])

    lanes_e = 256

    def expand(source, lanes):
        return gelu_scaled(dot(source, w_exp[:, lanes]) * HALF_ROOT + b_exp_s[:, lanes])

    def expand_slabs(e, count):
        source = ordered[pl.ds(e, count)].reshape(count * slab, width)
        for n in range(inner // lanes_e):
            lanes = slice(n * lanes_e, (n + 1) * lanes_e)
            value = expand(source, lanes)
            for k in range(count):
                exp[e + k, n_t : n_t + slab, lanes] = value[k * slab : (k + 1) * slab]

    ok_top, ok_bot = has_top.astype(F32), has_bot.astype(F32)
    ok_left, ok_right = has_left.astype(F32), has_right.astype(F32)

    def border_columns(e):
        at = lax.broadcasted_iota(jnp.int32, (n_t, inner), 0)
        left = exp[e, slab : slab + n_t, :]
        right = exp[e, n_t : 2 * n_t, :]
        if n_t > 1:
            left = pltpu.roll(left, 1, 0)
            right = pltpu.roll(right, n_t - 1, 0)
        for i in range(n_i):
            row = i * depth_h + e - 1
            above, below = row < 0, row >= tile_h
            ok = jnp.where(above, ok_top, jnp.where(below, ok_bot, jnp.float32(1)))
            row = jnp.where(above, tile_h, jnp.where(below, tile_h + 1, row))
            left = jnp.where(at == i * n_j, colexp[0, pl.ds(row, 1), :] * (ok_left * ok), left)
            right = jnp.where(
                at == i * n_j + n_j - 1, colexp[1, pl.ds(row, 1), :] * (ok_right * ok), right
            )
        exp[e, 0:n_t, :] = left
        exp[e, n_t + slab : 2 * n_t + slab, :] = right

    pl.semaphore_wait(barrier, count)

    @pl.when(has_right)
    def _():
        rightward.start()

    @pl.when(has_left)
    def _():
        leftward.start()

    @pl.when(has_bot)
    def _():
        down.start()

    @pl.when(has_top)
    def _():
        up.start()

    for copy in weights:
        copy.start()

    for load in small:
        load.wait()
    for di in range(3):
        w_dep[3 * di : 3 * di + 3] = w_dep_in[di].astype(F32) * HALF_ROOT
    b_exp_s[...] = b_exp[...] * HALF_ROOT
    b_dep_s[...] = b_dep[...] * HALF_ROOT
    loads[1].wait()
    loads[3].start()
    loads[4].start()
    expand_slabs(1, 3)

    def await_or_zero(pairs):
        for buffer, index, there, copy in pairs:
            @pl.when(there)
            def _():
                copy.wait_recv()

            @pl.when(jnp.logical_not(there))
            def _():
                buffer[index] = jnp.zeros(buffer.shape[1:], BF16)

    await_or_zero(((colin, 0, has_left, rightward), (colin, 1, has_right, leftward)))

    def expand_columns(source, first):
        rows = source.shape[1]
        flat = source[...].reshape(2 * rows, width)
        for n in range(inner // lanes_e):
            lanes = slice(n * lanes_e, (n + 1) * lanes_e)
            value = expand(flat, lanes)
            colexp[0, first : first + rows, lanes] = value[:rows]
            colexp[1, first : first + rows, lanes] = value[rows:]

    expand_columns(colin, 0)

    @pl.loop(1, 4)
    def _(e):
        border_columns(e)

    lanes_d = 128
    strip = min(32, part)

    def partial_copy(u):
        return remote(psend.at[u], precv.at[u], p_s.at[u], p_r.at[u], partner)

    def depth_slab(a):
        for chunk in range(inner // lanes_d):
            lanes = slice(chunk * lanes_d, (chunk + 1) * lanes_d)
            for n in range(slab // strip):
                total = None
                for di in range(3):
                    rows = exp[a + di, n * strip : (n + 1) * strip + 2 * n_t, lanes]
                    for dj in range(3):
                        k = 3 * di + dj
                        term = rows[dj * n_t : dj * n_t + strip] * w_dep[k : k + 1, lanes]
                        total = term if total is None else total + term
                value = gelu_scaled(total + b_dep_s[:, lanes]).astype(BF16)
                core, place_in = divmod(n * strip, part)
                first = pl.multiple_of(jnp.where(c == core, part, 0) + place_in, strip)
                dbuf[pl.ds(first, strip), lanes] = value

    def project_slab(u, a):
        projected = dot(dbuf[...], w_proj[...])
        psend[u] = projected[:part].astype(BF16)
        partial_copy(u).start()
        own = ordered[a + 1, pl.ds(pl.multiple_of(c * part, part), part)]
        acc[u] = projected[part:] + own.astype(F32) + b_proj[...]

    def forward_copy(u, pair):
        m, ah = lax.div(u, slabs), lax.rem(u, slabs)
        s = owner(ah, pair)
        return s, remote(
            fsend.at[u, pair], frecv.at[m, my_s], f_s.at[u, pair], f_r.at[m, my_s], peer(s, c)
        )

    def finish(u):
        m = lax.div(u, slabs)
        partial_copy(u).wait_recv()
        mixed = (acc[u] + precv[u].astype(F32)).astype(BF16)
        for pair in range(plan.pairs):
            fsend[u, pair] = mixed[pair * plan.piece : (pair + 1) * plan.piece]

        @pl.loop(0, plan.pairs)
        def _(t):
            pair = lax.rem(t + flip * (plan.pairs // 2), plan.pairs)
            s, copy = forward_copy(u, pair)

            @pl.when(s == my_s)
            def _():
                frecv[m, my_s] = fsend[u, pair]

            @pl.when(s != my_s)
            def _():
                copy.start()

    loads[2].wait()
    token_row = lax.broadcasted_iota(jnp.int32, (slab, 1), 0)
    token_i = lax.rem(lax.div(token_row, n_j), n_i)

    @pl.loop(0, depth_h)
    def _(u):
        a = lax.rem(u + 1, depth_h)
        e = lax.rem(u + 4, depth_h + 2)

        @pl.when(u == (depth_h - 3) // 2 + 1)
        def _():
            await_or_zero(((halo, 0, has_top, down), (halo, 1, has_bot, up)))
            place(0, [halo[0]] + [cells[i * depth_h - 1] for i in range(1, n_i)])
            place(depth_h + 1, [cells[i * depth_h] for i in range(1, n_i)] + [halo[1]])
            at_row = lax.broadcasted_iota(jnp.int32, edge_x.shape[1:], 0)
            for side, col in ((0, 0), (1, tile_w - 1)):
                top = halo[0].astype(F32)[col : col + 1]
                bottom = halo[1].astype(F32)[col : col + 1]
                edge_x[side] = jnp.where(at_row == 0, top, bottom).astype(BF16)

            @pl.when(has_right)
            def _():
                rightward_x.start()

            @pl.when(has_left)
            def _():
                leftward_x.start()

        depth_slab(a)
        project_slab(u, a)

        @pl.when(u == depth_h - 3)
        def _():
            await_or_zero(((colin_x, 0, has_left, rightward_x), (colin_x, 1, has_right, leftward_x)))
            expand_columns(colin_x, tile_h)

        @pl.when(u < depth_h - 1)
        def _():
            expand_slabs(e, 1)

            @pl.when((e == 0) | (e == depth_h + 1))
            def _():
                outside = jnp.where(
                    e == 0,
                    jnp.where(token_i == 0, 1 - ok_top, 0.0),
                    jnp.where(token_i == n_i - 1, 1 - ok_bot, 0.0),
                )
                exp[e, n_t : n_t + slab] = exp[e, n_t : n_t + slab] * (1 - outside)

            border_columns(e)

        @pl.when(u > 0)
        def _():
            finish(u - 1)

    loads[3].wait()
    loads[4].wait()

    for copy in weights:
        copy.wait_recv()

    eye = (
        lax.broadcasted_iota(jnp.int32, (half, half), 0)
        == lax.broadcasted_iota(jnp.int32, (half, half), 1)
    ).astype(F32).astype(BF16)
    w_vt[:half] = dot_t(eye, w_qkv[2, :, :half]).astype(BF16)
    w_vt[half:] = dot_t(eye, w_qkv[2, :, half:]).astype(BF16)
    finish(jnp.int32(depth_h - 1))

    def await_batch(m):
        @pl.loop(0, plan.sources)
        def _(s):
            @pl.when(s != my_s)
            def _():
                remote(
                    fsend.at[0, 0], frecv.at[m, s], f_s.at[0, 0], f_r.at[m, s], partner
                ).wait_recv()

    keys = plan.sources * n_t
    tokens = WINDOWS * keys
    group = 128
    n_h = group // HEAD_DIM
    lane = lax.broadcasted_iota(jnp.int32, (1, WINDOWS * 2 * group), 1)
    head_masks = [
        (lax.rem(lax.div(lane, HEAD_DIM), n_h) == h).astype(F32).astype(BF16) for h in range(n_h)
    ]
    lane_w = lax.div(lax.broadcasted_iota(jnp.int32, (1, tokens), 1), keys)
    window_masks = [(lane_w == w).astype(F32).astype(BF16) for w in range(WINDOWS)]
    scale = np.float32(HEAD_DIM ** (-0.5) * np.log2(np.e))
    duos = width // (2 * group)
    eye_t = eye[:tokens, :tokens]

    def attend(normed):
        query = dot(normed, w_qkv[0])
        keyset = dot(normed, w_qkv[1])
        values = dot_t(w_vt[...], normed)
        query = (query * scale).astype(BF16)
        keyset = keyset.astype(BF16)
        values = values.astype(BF16)
        blank = jnp.zeros((keys, group), BF16)
        blocks = [(w, g) for w in range(WINDOWS) for g in range(2)]
        lefts, rights = [], []
        for duo in range(duos):
            rights.append(jnp.concatenate([
                jnp.concatenate([
                    query[w * keys : (w + 1) * keys, (2 * duo + g) * group : (2 * duo + g + 1) * group]
                    if block == (w, g) else blank
                    for block in blocks
                ], axis=1)
                for g in range(2) for w in range(WINDOWS)
            ], axis=0))
            left = jnp.concatenate([
                keyset[w * keys : (w + 1) * keys, 2 * duo * group : (2 * duo + 2) * group]
                for w in range(WINDOWS)
            ], axis=1)
            lefts.append(jnp.concatenate([left * mask for mask in head_masks], axis=0))
        scores = [dot_t(left, right) for left, right in zip(lefts, rights)]
        nothing = jnp.zeros((HEAD_DIM, tokens), BF16)
        stacked, spreads, shares = [], [], []
        for duo in range(duos):
            score = scores[duo].reshape(n_h, keys, 2 * tokens)
            top = jnp.max(score, axis=1, keepdims=True)
            power = jnp.exp2(score - top)
            share = 1.0 / jnp.sum(power, axis=1, keepdims=True)
            power = power.astype(BF16)
            for g in range(2):
                lanes = slice(g * tokens, (g + 1) * tokens)
                shares.append(share[:, :, lanes])
                spreads.append(jnp.concatenate(
                    [power[h, :, lanes] * mask for h in range(n_h) for mask in window_masks], axis=0
                ))
                first = (2 * duo + g) * group
                stacked.append(jnp.concatenate([
                    jnp.concatenate([
                        values[first + h * HEAD_DIM : first + (h + 1) * HEAD_DIM]
                        if h == at else nothing
                        for at in range(n_h)
                    ], axis=1)
                    for h in range(n_h)
                ], axis=0))
        found = [dot(a, b) for a, b in zip(stacked, spreads)]
        found = jnp.concatenate([
            (f.reshape(n_h, HEAD_DIM, tokens) * share).reshape(group, tokens).astype(BF16)
            for f, share in zip(found, shares)
        ], axis=0)
        return dot_t(eye_t, found).astype(BF16)

    def return_copy(m, s, side):
        return remote(
            osend.at[side, m, s], oin.at[m, my_slab, c, my_pair],
            o_s.at[side, m, s], o_r.at[m, my_slab, c, my_pair], peer(s, side),
        )

    @pl.loop(0, plan.batches)
    def _(m):
        await_batch(m)
        came = frecv[m].astype(F32)
        mixed = jnp.concatenate([
            came[:, w * n_t : (w + 1) * n_t].reshape(keys, width) for w in range(WINDOWS)
        ], axis=0)
        centered = mixed - jnp.mean(mixed, axis=-1, keepdims=True)
        spread = jnp.mean(centered * centered, axis=-1, keepdims=True)
        normed = (centered * lax.rsqrt(spread + 1e-05) * gain[...]).astype(BF16)
        total = mixed + dot(attend(normed), w_out[...])
        for side in range(2):
            lanes = slice(side * half, (side + 1) * half)
            value = total[:, lanes] + bo_full[side]
            value = jnp.concatenate([
                value[w * keys : (w + 1) * keys].reshape(plan.sources, n_t, half)
                for w in range(WINDOWS)
            ], axis=1)
            osend[side, m] = value.astype(BF16)

        @pl.loop(0, 2 * plan.sources)
        def _(t):
            s = lax.rem(lax.div(t, 2) + flip * (plan.sources // 2), plan.sources)
            side = lax.rem(t, 2)
            mine = (s == my_s) & (side == c)

            @pl.when(mine)
            def _():
                oin[m, my_slab, c, my_pair] = osend[c, m, my_s]

            @pl.when(jnp.logical_not(mine))
            def _():
                return_copy(m, s, side).start()

    perm_t = one_hot(slab, slab, lambda row, column: cell_of(column) == row)

    @pl.loop(0, depth_h)
    def _(u):
        m, ah = lax.div(u, slabs), lax.rem(u, slabs)
        a = lax.rem(u + 1, depth_h)

        @pl.loop(0, 2 * plan.pairs)
        def _(t):
            core, pair = lax.rem(t, 2), lax.div(t, 2)

            @pl.when(jnp.logical_not((owner(ah, pair) == my_s) & (core == c)))
            def _():
                remote(
                    osend.at[0, 0, 0], oin.at[m, ah, core, pair],
                    o_s.at[0, 0, 0], o_r.at[m, ah, core, pair], partner,
                ).wait_recv()

        arrived = oin[m, ah].astype(F32).reshape(slab, half).astype(BF16)
        placed = dot(perm_t, arrived).astype(BF16)
        for i in range(n_i):
            out[i * depth_h + a] = placed[i * tile_w : (i + 1) * tile_w]

    @pl.when(has_bot)
    def _():
        down.wait_send()

    @pl.when(has_top)
    def _():
        up.wait_send()

    @pl.when(has_right)
    def _():
        rightward.wait_send()
        rightward_x.wait_send()

    @pl.when(has_left)
    def _():
        leftward.wait_send()
        leftward_x.wait_send()

    for copy in weights:
        copy.wait_send()

    @pl.loop(0, depth_h)
    def _(u):
        partial_copy(u).wait_send()

        @pl.loop(0, plan.pairs)
        def _(pair):
            s, copy = forward_copy(u, pair)

            @pl.when(s != my_s)
            def _():
                copy.wait_send()

    @pl.loop(0, 2 * plan.sources)
    def _(t):
        s, side = lax.div(t, 2), lax.rem(t, 2)

        @pl.when(jnp.logical_not((s == my_s) & (side == c)))
        def _():
            for m in range(plan.batches):
                return_copy(m, s, side).wait_send()


def per_device(
    mesh_shape, cells, w_expand, b_expand, w_depth, b_depth, w_project, b_project, ln_gain,
    w_qkv, w_out, b_out,
):
    tile_h, tile_w, width = cells.shape
    plan = Plan(mesh_shape, tile_h, tile_w)
    inner = w_expand.shape[1]
    half = width // 2
    args = (
        cells, w_expand, b_expand[None], w_depth, b_depth[None],
        w_project, b_project[None], ln_gain[None], w_qkv.transpose(1, 0, 2), w_out, b_out[None],
    )
    dma = pltpu.SemaphoreType.DMA
    vmem = pltpu.VMEM
    n = plan
    rows_x = 16
    return pl.pallas_call(
        functools.partial(kernel, plan),
        out_shape=jax.ShapeDtypeStruct((tile_h, tile_w, half), BF16),
        in_specs=[
            pl.BlockSpec(memory_space=pl.ANY) for _ in args
        ],
        out_specs=pl.BlockSpec(memory_space=pltpu.VMEM),
        scratch_shapes=[
            vmem((1, inner), F32), vmem(w_depth.shape, BF16), vmem((1, inner), F32),
            vmem((1, width), F32), vmem((1, width), F32),
            vmem(cells.shape, BF16), vmem((n.depth_h + 2, n.slab, width), BF16),
            vmem(w_expand.shape, BF16), vmem(w_project.shape, BF16),
            vmem((3, width, width), BF16), vmem((width, width), BF16), vmem((9, inner), F32),
            vmem((n.depth_h + 2, n.slab + 2 * n.n_t, inner), F32),
            vmem((2, tile_w, width), BF16),
            vmem((2, tile_h, width), BF16),
            vmem((2, tile_h, width), BF16),
            vmem((2, rows_x, width), BF16),
            vmem((2, rows_x, width), BF16),
            vmem((2, tile_h + rows_x, inner), F32),
            vmem((n.slab, inner), BF16),
            vmem((n.depth_h, n.part, width), BF16),
            vmem((n.depth_h, n.part, width), BF16),
            vmem((n.depth_h, n.part, width), F32),
            vmem((n.depth_h, n.pairs, n.piece, width), BF16),
            vmem((n.batches, n.sources, n.piece, width), BF16),
            vmem((1, inner), F32), vmem((1, inner), F32),
            vmem((width, width), BF16),
            vmem((2, 1, half), F32),
            vmem((2, n.batches, n.sources, n.piece, half), BF16),
            vmem((n.batches, n.slabs, 2, n.pairs, n.piece, half), BF16),
            dma((11,)),
            dma((2,)), dma((2,)), dma((4,)), dma((4,)), dma((3,)), dma((3,)),
            dma((n.depth_h,)), dma((n.depth_h,)),
            dma((n.depth_h, n.pairs)), dma((n.batches, n.sources)),
            dma((2, n.batches, n.sources)), dma((n.batches, n.slabs, 2, n.pairs)),
        ],
        compiler_params=pltpu.CompilerParams(
            collective_id=0, has_side_effects=True, vmem_limit_bytes=60 << 20
        ),
    )(*args)


def solution(mesh):
    placed = (
        P(("grp", "gy"), "gx", None),
        P(None, "ch"),
        P("ch"),
        P(None, None, "ch"),
        P("ch"),
        P("ch", None),
        P(),
        P(),
        P(None, None, "ch"),
        P("ch", None),
        P("ch"),
    )
    return jax.shard_map(
        functools.partial(per_device, dict(mesh.shape)),
        mesh=mesh,
        in_specs=placed,
        out_specs=P(("grp", "gy"), "gx", "ch"),
        check_vma=False,
    )
```

```python
import functools

import jax
import jax.numpy as jnp
import numpy as np
from jax import lax
from jax.experimental import pallas as pl
from jax.experimental.pallas import tpu as pltpu
from jax.sharding import PartitionSpec as P

HEAD_DIM = 32
GRID = 8
WINDOWS = 2
MESH = pl.DeviceIdType.MESH
F32 = jnp.float32
BF16 = jnp.bfloat16


HALF_ROOT = np.float32(np.sqrt(0.5))


def gelu_scaled(t):
    return t * (HALF_ROOT + HALF_ROOT * lax.erf(t))


def dot(a, b):
    return jnp.dot(a, b, preferred_element_type=F32)


def dot_t(a, b):
    return lax.dot_general(a, b, (((1,), (1,)), ((), ())), preferred_element_type=F32)


def quotient(v, n):
    return v >> (n.bit_length() - 1) if n & (n - 1) == 0 else lax.div(v, n)


def remainder(v, n):
    return v & (n - 1) if n & (n - 1) == 0 else lax.rem(v, n)


def farthest_first(n):
    return sorted(range(1, n), key=lambda k: abs(2 * k - n))


class Plan:
    def __init__(self, mesh_shape, tile_h, tile_w):
        self.n_rows, self.n_cols = mesh_shape["gy"], mesh_shape["gx"]
        self.tile_h, self.tile_w = tile_h, tile_w
        stride_h = tile_h * self.n_rows // GRID
        stride_w = tile_w * self.n_cols // GRID
        self.depth_h, self.depth_w = min(tile_h, stride_h), min(tile_w, stride_w)
        self.steps_h, self.steps_w = stride_h // self.depth_h, stride_w // self.depth_w
        self.n_i, self.n_j = tile_h // self.depth_h, tile_w // self.depth_w
        self.ph, self.pw = GRID // self.n_i, GRID // self.n_j
        self.n_t = self.n_i * self.n_j
        self.sources = self.ph * self.pw
        half_w = self.depth_w // 2
        self.slab = self.depth_w * self.n_t
        self.part = self.slab // 2
        self.pairs = half_w // WINDOWS
        self.slabs = self.sources * WINDOWS // half_w
        self.batches = self.depth_h // self.slabs
        self.piece = WINDOWS * self.n_t
        assert self.pairs % self.pw == 0 and self.pairs // self.pw * self.slabs == self.ph
        assert self.depth_h % self.slabs == 0 and self.depth_h >= 4


def kernel(
    plan, cells_h, w_exp_h, b_exp_h, w_dep_h, b_dep_h, w_proj_h, b_proj_h, gain_h, w_qkv_h, w_out_h,
    b_out_h, out,
    b_exp, w_dep_in, b_dep, b_proj, gain, cells, ordered, w_exp, w_proj, w_qkv, w_out, w_dep,
    exp, halo, edge, colin, edge_x, colin_x, colexp, dbuf, psend, precv, acc, fsend, frecv,
    b_exp_s, b_dep_s, w_vt, bo_full, osend, oin,
    in_s, halo_s, halo_r, col_s, col_r, w_s, w_r, p_s, p_r, f_s, f_r, o_s, o_r,
):
    tile_h, tile_w = plan.tile_h, plan.tile_w
    depth_h, n_i, n_j, n_t = plan.depth_h, plan.n_i, plan.n_j, plan.n_t
    width = cells.shape[2]
    inner = w_exp.shape[1]
    slab, part, pw, slabs = plan.slab, plan.part, plan.pw, plan.slabs
    half = width // 2
    z, x, c = lax.axis_index("gy"), lax.axis_index("gx"), lax.axis_index("ch")
    zs, xs = lax.rem(z, plan.steps_h), lax.rem(x, plan.steps_w)
    mp, mq = lax.div(z, plan.steps_h), lax.div(x, plan.steps_w)
    my_s = mp * pw + mq
    my_slab = lax.rem(mp, slabs)
    my_pair = lax.div(mp, slabs) * pw + mq
    last_z, last_x = plan.n_rows - 1, plan.n_cols - 1
    partner = {"ch": 1 - c}
    has_top, has_bot = z > 0, z < last_z
    has_left, has_right = x > 0, x < last_x

    def peer(s, core):
        p, q = lax.div(s, pw), lax.rem(s, pw)
        return {"gy": p * plan.steps_h + zs, "gx": q * plan.steps_w + xs, "ch": core}

    def owner(ah, pair):
        return (lax.div(pair, pw) * slabs + ah) * pw + lax.rem(pair, pw)

    def remote(src, dst, send, recv, device):
        return pltpu.make_async_remote_copy(
            src_ref=src, dst_ref=dst, send_sem=send, recv_sem=recv,
            device_id=device, device_id_type=MESH,
        )

    mine = pl.ds(pl.multiple_of(c * half, half), half)
    loads = [
        pltpu.make_async_copy(src, dst, in_s.at[n])
        for n, (src, dst) in enumerate((
            (cells_h, cells), (w_exp_h, w_exp), (w_proj_h, w_proj),
            (w_qkv_h, w_qkv.at[:, :, mine]), (w_out_h, w_out.at[mine]),
            (b_exp_h, b_exp), (w_dep_h, w_dep_in), (b_dep_h, b_dep), (b_proj_h, b_proj),
            (gain_h, gain), (b_out_h, bo_full.at[c]),
        ))
    ]
    small = loads[5:]
    for load in loads[:2] + small + loads[2:3]:
        load.start()

    barrier = pltpu.get_barrier_semaphore()
    around = (
        (has_top, {"gy": jnp.maximum(z - 1, 0)}),
        (has_bot, {"gy": jnp.minimum(z + 1, last_z)}),
        (has_left, {"gx": jnp.maximum(x - 1, 0)}),
        (has_right, {"gx": jnp.minimum(x + 1, last_x)}),
    )
    count = jnp.int32(2 * plan.sources - 1)
    for there, device in around:
        @pl.when(there)
        def _():
            pl.semaphore_signal(barrier, inc=1, device_id=device, device_id_type=MESH)
        count = count + there.astype(jnp.int32)

    @pl.loop(0, 2 * plan.sources)
    def _(t):
        s, core = lax.div(t, 2), lax.rem(t, 2)

        @pl.when(jnp.logical_not((s == my_s) & (core == c)))
        def _():
            pl.semaphore_signal(barrier, inc=1, device_id=peer(s, core), device_id_type=MESH)

    down = remote(cells_h.at[tile_h - 1], halo.at[0], halo_s.at[0], halo_r.at[0], around[1][1])
    up = remote(cells_h.at[0], halo.at[1], halo_s.at[1], halo_r.at[1], around[0][1])
    rightward = remote(edge.at[1], colin.at[0], col_s.at[0], col_r.at[0], around[3][1])
    leftward = remote(edge.at[0], colin.at[1], col_s.at[1], col_r.at[1], around[2][1])
    rightward_x = remote(edge_x.at[1], colin_x.at[0], col_s.at[2], col_r.at[2], around[3][1])
    leftward_x = remote(edge_x.at[0], colin_x.at[1], col_s.at[3], col_r.at[3], around[2][1])
    weights = (
        remote(w_qkv_h, w_qkv.at[:, :, mine], w_s.at[0], w_r.at[0], partner),
        remote(w_out_h, w_out.at[mine], w_s.at[1], w_r.at[1], partner),
        remote(b_out_h, bo_full.at[c], w_s.at[2], w_r.at[2], partner),
    )

    def one_hot(rows, columns, source):
        row = lax.broadcasted_iota(jnp.int32, (rows, columns), 0)
        column = lax.broadcasted_iota(jnp.int32, (rows, columns), 1)
        return source(row, column).astype(F32).astype(BF16)

    def cell_of(row):
        b, i, j = quotient(row, n_t), quotient(remainder(row, n_t), n_j), remainder(row, n_j)
        return i * tile_w + j * plan.depth_w + b

    perm = one_hot(slab, slab, lambda row, column: cell_of(row) == column)
    picks = [
        one_hot(tile_h, tile_h * 16, lambda row, column: row * 16 + at == column) for at in (0, 15)
    ]
    loads[0].wait()

    for side, first in ((0, 0), (1, tile_w - 16)):
        border = cells[:, first : first + 16, :].reshape(tile_h * 16, width)
        edge[side] = dot(picks[side], border).astype(BF16)

    def place(e, rows):
        ordered[e] = dot(perm, jnp.concatenate(rows, axis=0)).astype(BF16)

    def place_own(e):
        place(e, [cells[i * depth_h + e - 1] for i in range(n_i)])

    for e in range(1, 4):
        place_own(e)

    lanes_e = 256

    def expand(source, lanes):
        return gelu_scaled(dot(source, w_exp[:, lanes]) * HALF_ROOT + b_exp_s[:, lanes])

    def expand_slabs(e, count):
        source = ordered[pl.ds(e, count)].reshape(count * slab, width)
        for n in range(inner // lanes_e):
            lanes = slice(n * lanes_e, (n + 1) * lanes_e)
            value = expand(source, lanes)
            for k in range(count):
                exp[e + k, n_t : n_t + slab, lanes] = value[k * slab : (k + 1) * slab]

    ok_top, ok_bot = has_top.astype(F32), has_bot.astype(F32)
    ok_left, ok_right = has_left.astype(F32), has_right.astype(F32)

    def border_columns(e):
        at = lax.broadcasted_iota(jnp.int32, (n_t, inner), 0)
        left = exp[e, slab : slab + n_t, :]
        right = exp[e, n_t : 2 * n_t, :]
        if n_t > 1:
            left = pltpu.roll(left, 1, 0)
            right = pltpu.roll(right, n_t - 1, 0)
        for i in range(n_i):
            row = i * depth_h + e - 1
            above, below = row < 0, row >= tile_h
            ok = jnp.where(above, ok_top, jnp.where(below, ok_bot, jnp.float32(1)))
            row = jnp.where(above, tile_h, jnp.where(below, tile_h + 1, row))
            left = jnp.where(at == i * n_j, colexp[0, pl.ds(row, 1), :] * (ok_left * ok), left)
            right = jnp.where(
                at == i * n_j + n_j - 1, colexp[1, pl.ds(row, 1), :] * (ok_right * ok), right
            )
        exp[e, 0:n_t, :] = left
        exp[e, n_t + slab : 2 * n_t + slab, :] = right

    pl.semaphore_wait(barrier, count)

    @pl.when(has_right)
    def _():
        rightward.start()

    @pl.when(has_left)
    def _():
        leftward.start()

    @pl.when(has_bot)
    def _():
        down.start()

    @pl.when(has_top)
    def _():
        up.start()

    for copy in weights:
        copy.start()

    for load in small:
        load.wait()
    for di in range(3):
        w_dep[3 * di : 3 * di + 3] = w_dep_in[di].astype(F32) * HALF_ROOT
    b_exp_s[...] = b_exp[...] * HALF_ROOT
    b_dep_s[...] = b_dep[...] * HALF_ROOT
    loads[1].wait()
    loads[3].start()
    loads[4].start()
    expand_slabs(1, 3)

    @pl.loop(4, depth_h + 1)
    def _(e):
        place_own(e)

    def await_or_zero(pairs):
        for buffer, index, there, copy in pairs:
            @pl.when(there)
            def _():
                copy.wait_recv()

            @pl.when(jnp.logical_not(there))
            def _():
                buffer[index] = jnp.zeros(buffer.shape[1:], BF16)

    await_or_zero(((colin, 0, has_left, rightward), (colin, 1, has_right, leftward)))

    def expand_columns(source, first):
        rows = source.shape[1]
        flat = source[...].reshape(2 * rows, width)
        for n in range(inner // lanes_e):
            lanes = slice(n * lanes_e, (n + 1) * lanes_e)
            value = expand(flat, lanes)
            colexp[0, first : first + rows, lanes] = value[:rows]
            colexp[1, first : first + rows, lanes] = value[rows:]

    expand_columns(colin, 0)

    @pl.loop(1, 4)
    def _(e):
        border_columns(e)

    lanes_d = 128
    strip = min(32, part)

    def partial_copy(u):
        return remote(psend.at[u], precv.at[u], p_s.at[u], p_r.at[u], partner)

    def depth_slab(a):
        for chunk in range(inner // lanes_d):
            lanes = slice(chunk * lanes_d, (chunk + 1) * lanes_d)
            for n in range(slab // strip):
                total = None
                for di in range(3):
                    rows = exp[a + di, n * strip : (n + 1) * strip + 2 * n_t, lanes]
                    for dj in range(3):
                        k = 3 * di + dj
                        term = rows[dj * n_t : dj * n_t + strip] * w_dep[k : k + 1, lanes]
                        total = term if total is None else total + term
                value = gelu_scaled(total + b_dep_s[:, lanes]).astype(BF16)
                core, place_in = divmod(n * strip, part)
                first = pl.multiple_of(jnp.where(c == core, part, 0) + place_in, strip)
                dbuf[pl.ds(first, strip), lanes] = value

    def project_slab(u, a):
        projected = dot(dbuf[...], w_proj[...])
        psend[u] = projected[:part].astype(BF16)
        partial_copy(u).start()
        own = ordered[a + 1, pl.ds(pl.multiple_of(c * part, part), part)]
        acc[u] = projected[part:] + own.astype(F32) + b_proj[...]

    def forward_copy(u, pair):
        m, ah = lax.div(u, slabs), lax.rem(u, slabs)
        s = owner(ah, pair)
        return s, remote(
            fsend.at[u, pair], frecv.at[m, my_s], f_s.at[u, pair], f_r.at[m, my_s], peer(s, c)
        )

    def finish(u):
        m = lax.div(u, slabs)
        partial_copy(u).wait_recv()
        mixed = (acc[u] + precv[u].astype(F32)).astype(BF16)
        for pair in range(plan.pairs):
            fsend[u, pair] = mixed[pair * plan.piece : (pair + 1) * plan.piece]

        for k in farthest_first(plan.pairs):
            forward_copy(u, lax.rem(my_pair + k, plan.pairs))[1].start()

        @pl.when(lax.rem(u, slabs) == my_slab)
        def _():
            frecv[m, my_s] = fsend[u, my_pair]

        @pl.when(lax.rem(u, slabs) != my_slab)
        def _():
            forward_copy(u, my_pair)[1].start()

    eye = (
        lax.broadcasted_iota(jnp.int32, (half, half), 0)
        == lax.broadcasted_iota(jnp.int32, (half, half), 1)
    ).astype(F32).astype(BF16)
    def await_weights():
        loads[3].wait()
        loads[4].wait()
        for copy in weights:
            copy.wait_recv()
        w_vt[:half] = dot_t(eye, w_qkv[2, :, :half]).astype(BF16)
        w_vt[half:] = dot_t(eye, w_qkv[2, :, half:]).astype(BF16)

    def await_batch(m):
        @pl.loop(0, plan.sources)
        def _(s):
            @pl.when(s != my_s)
            def _():
                remote(
                    fsend.at[0, 0], frecv.at[m, s], f_s.at[0, 0], f_r.at[m, s], partner
                ).wait_recv()

    keys = plan.sources * n_t
    tokens = WINDOWS * keys
    group = 128
    n_h = group // HEAD_DIM
    lane = lax.broadcasted_iota(jnp.int32, (1, WINDOWS * 2 * group), 1)
    head_masks = [
        (remainder(quotient(lane, HEAD_DIM), n_h) == h).astype(F32).astype(BF16) for h in range(n_h)
    ]
    lane_w = lax.div(lax.broadcasted_iota(jnp.int32, (1, tokens), 1), keys)
    window_masks = [(lane_w == w).astype(F32).astype(BF16) for w in range(WINDOWS)]
    scale = np.float32(HEAD_DIM ** (-0.5) * np.log2(np.e))
    duos = width // (2 * group)
    eye_t = eye[:tokens, :tokens]

    def attend(normed):
        query = dot(normed, w_qkv[0])
        keyset = dot(normed, w_qkv[1])
        values = dot_t(w_vt[...], normed)
        query = (query * scale).astype(BF16)
        keyset = keyset.astype(BF16)
        values = values.astype(BF16)
        blank = jnp.zeros((keys, group), BF16)
        blocks = [(w, g) for w in range(WINDOWS) for g in range(2)]
        lefts, rights = [], []
        for duo in range(duos):
            rights.append(jnp.concatenate([
                jnp.concatenate([
                    query[w * keys : (w + 1) * keys, (2 * duo + g) * group : (2 * duo + g + 1) * group]
                    if block == (w, g) else blank
                    for block in blocks
                ], axis=1)
                for g in range(2) for w in range(WINDOWS)
            ], axis=0))
            left = jnp.concatenate([
                keyset[w * keys : (w + 1) * keys, 2 * duo * group : (2 * duo + 2) * group]
                for w in range(WINDOWS)
            ], axis=1)
            lefts.append(jnp.concatenate([left * mask for mask in head_masks], axis=0))
        scores = [dot_t(left, right) for left, right in zip(lefts, rights)]
        nothing = jnp.zeros((HEAD_DIM, tokens), BF16)
        stacked, spreads, shares = [], [], []
        for duo in range(duos):
            score = scores[duo].reshape(n_h, keys, 2 * tokens)
            top = jnp.max(score, axis=1, keepdims=True)
            power = jnp.exp2(score - top)
            share = 1.0 / jnp.sum(power, axis=1, keepdims=True)
            power = power.astype(BF16)
            for g in range(2):
                lanes = slice(g * tokens, (g + 1) * tokens)
                shares.append(share[:, :, lanes])
                spreads.append(jnp.concatenate(
                    [power[h, :, lanes] * mask for h in range(n_h) for mask in window_masks], axis=0
                ))
                first = (2 * duo + g) * group
                stacked.append(jnp.concatenate([
                    jnp.concatenate([
                        values[first + h * HEAD_DIM : first + (h + 1) * HEAD_DIM]
                        if h == at else nothing
                        for at in range(n_h)
                    ], axis=1)
                    for h in range(n_h)
                ], axis=0))
        found = [dot(a, b) for a, b in zip(stacked, spreads)]
        found = jnp.concatenate([
            (f.reshape(n_h, HEAD_DIM, tokens) * share).reshape(group, tokens).astype(BF16)
            for f, share in zip(found, shares)
        ], axis=0)
        return dot_t(eye_t, found).astype(BF16)

    def return_copy(m, s, side):
        return remote(
            osend.at[side, m, s], oin.at[m, my_slab, c, my_pair],
            o_s.at[side, m, s], o_r.at[m, my_slab, c, my_pair], peer(s, side),
        )

    def attend_batch(m):
        await_batch(m)
        came = frecv[m].astype(F32)
        mixed = jnp.concatenate([
            came[:, w * n_t : (w + 1) * n_t].reshape(keys, width) for w in range(WINDOWS)
        ], axis=0)
        centered = mixed - jnp.mean(mixed, axis=-1, keepdims=True)
        spread = jnp.mean(centered * centered, axis=-1, keepdims=True)
        normed = (centered * lax.rsqrt(spread + 1e-05) * gain[...]).astype(BF16)
        total = mixed + dot(attend(normed), w_out[...])
        for side in range(2):
            lanes = slice(side * half, (side + 1) * half)
            value = total[:, lanes] + bo_full[side]
            value = jnp.concatenate([
                value[w * keys : (w + 1) * keys].reshape(plan.sources, n_t, half)
                for w in range(WINDOWS)
            ], axis=1)
            osend[side, m] = value.astype(BF16)

        oin[m, my_slab, c, my_pair] = osend[c, m, my_s]
        for k in farthest_first(plan.sources):
            for side in range(2):
                return_copy(m, lax.rem(my_s + k, plan.sources), side).start()
        return_copy(m, my_s, 1 - c).start()

    loads[2].wait()
    token_row = lax.broadcasted_iota(jnp.int32, (slab, 1), 0)
    token_i = remainder(quotient(token_row, n_j), n_i)

    def bottleneck(u):
        a = lax.rem(u + 1, depth_h)
        e = lax.rem(u + 4, depth_h + 2)

        @pl.when(u == (depth_h - 3) // 2 + 1)
        def _():
            await_or_zero(((halo, 0, has_top, down), (halo, 1, has_bot, up)))
            place(0, [halo[0]] + [cells[i * depth_h - 1] for i in range(1, n_i)])
            place(depth_h + 1, [cells[i * depth_h] for i in range(1, n_i)] + [halo[1]])
            at_row = lax.broadcasted_iota(jnp.int32, edge_x.shape[1:], 0)
            for side, col in ((0, 0), (1, tile_w - 1)):
                top = halo[0].astype(F32)[col : col + 1]
                bottom = halo[1].astype(F32)[col : col + 1]
                edge_x[side] = jnp.where(at_row == 0, top, bottom).astype(BF16)

            @pl.when(has_right)
            def _():
                rightward_x.start()

            @pl.when(has_left)
            def _():
                leftward_x.start()

        depth_slab(a)
        project_slab(u, a)

        @pl.when(u == depth_h - 3)
        def _():
            await_or_zero(((colin_x, 0, has_left, rightward_x), (colin_x, 1, has_right, leftward_x)))
            expand_columns(colin_x, tile_h)

        @pl.when(u < depth_h - 1)
        def _():
            expand_slabs(e, 1)

            @pl.when((e == 0) | (e == depth_h + 1))
            def _():
                outside = jnp.where(
                    e == 0,
                    jnp.where(token_i == 0, 1 - ok_top, 0.0),
                    jnp.where(token_i == n_i - 1, 1 - ok_bot, 0.0),
                )
                exp[e, n_t : n_t + slab] = exp[e, n_t : n_t + slab] * (1 - outside)

            border_columns(e)

    lag = depth_h - 2

    @pl.loop(0, lag + plan.batches)
    def _(t):
        @pl.when(t < depth_h)
        def _():
            bottleneck(t)

        @pl.when((t > 0) & (t <= depth_h))
        def _():
            finish(t - 1)

        @pl.when(t == lag)
        def _():
            await_weights()

        @pl.when(t >= lag)
        def _():
            attend_batch(t - lag)

    @pl.when(has_bot)
    def _():
        down.wait_send()

    @pl.when(has_top)
    def _():
        up.wait_send()

    @pl.when(has_right)
    def _():
        rightward.wait_send()
        rightward_x.wait_send()

    @pl.when(has_left)
    def _():
        leftward.wait_send()
        leftward_x.wait_send()

    for copy in weights:
        copy.wait_send()

    @pl.loop(0, depth_h)
    def _(u):
        partial_copy(u).wait_send()

        for k in range(1, plan.pairs):
            forward_copy(u, lax.rem(my_pair + k, plan.pairs))[1].wait_send()

        @pl.when(lax.rem(u, slabs) != my_slab)
        def _():
            forward_copy(u, my_pair)[1].wait_send()

    perm_t = one_hot(slab, slab, lambda row, column: cell_of(column) == row)

    @pl.loop(0, depth_h)
    def _(u):
        m, ah = lax.div(u, slabs), lax.rem(u, slabs)
        a = lax.rem(u + 1, depth_h)

        @pl.loop(0, 2 * plan.pairs)
        def _(t):
            core, pair = lax.rem(t, 2), lax.div(t, 2)

            @pl.when(jnp.logical_not((owner(ah, pair) == my_s) & (core == c)))
            def _():
                remote(
                    osend.at[0, 0, 0], oin.at[m, ah, core, pair],
                    o_s.at[0, 0, 0], o_r.at[m, ah, core, pair], partner,
                ).wait_recv()

        arrived = oin[m, ah].astype(F32).reshape(slab, half).astype(BF16)
        placed = dot(perm_t, arrived).astype(BF16)
        for i in range(n_i):
            out[i * depth_h + a] = placed[i * tile_w : (i + 1) * tile_w]

    @pl.loop(0, plan.batches)
    def _(m):
        for k in range(1, plan.sources):
            for side in range(2):
                return_copy(m, lax.rem(my_s + k, plan.sources), side).wait_send()
        return_copy(m, my_s, 1 - c).wait_send()


def per_device(
    mesh_shape, cells, w_expand, b_expand, w_depth, b_depth, w_project, b_project, ln_gain,
    w_qkv, w_out, b_out,
):
    tile_h, tile_w, width = cells.shape
    plan = Plan(mesh_shape, tile_h, tile_w)
    inner = w_expand.shape[1]
    half = width // 2
    args = (
        cells, w_expand, b_expand[None], w_depth, b_depth[None],
        w_project, b_project[None], ln_gain[None], w_qkv.transpose(1, 0, 2), w_out, b_out[None],
    )
    dma = pltpu.SemaphoreType.DMA
    vmem = pltpu.VMEM
    n = plan
    rows_x = 16
    return pl.pallas_call(
        functools.partial(kernel, plan),
        out_shape=jax.ShapeDtypeStruct((tile_h, tile_w, half), BF16),
        in_specs=[
            pl.BlockSpec(memory_space=pl.ANY) for _ in args
        ],
        out_specs=pl.BlockSpec(memory_space=pltpu.VMEM),
        scratch_shapes=[
            vmem((1, inner), F32), vmem(w_depth.shape, BF16), vmem((1, inner), F32),
            vmem((1, width), F32), vmem((1, width), F32),
            vmem(cells.shape, BF16), vmem((n.depth_h + 2, n.slab, width), BF16),
            vmem(w_expand.shape, BF16), vmem(w_project.shape, BF16),
            vmem((3, width, width), BF16), vmem((width, width), BF16), vmem((9, inner), F32),
            vmem((n.depth_h + 2, n.slab + 2 * n.n_t, inner), F32),
            vmem((2, tile_w, width), BF16),
            vmem((2, tile_h, width), BF16),
            vmem((2, tile_h, width), BF16),
            vmem((2, rows_x, width), BF16),
            vmem((2, rows_x, width), BF16),
            vmem((2, tile_h + rows_x, inner), F32),
            vmem((n.slab, inner), BF16),
            vmem((n.depth_h, n.part, width), BF16),
            vmem((n.depth_h, n.part, width), BF16),
            vmem((n.depth_h, n.part, width), F32),
            vmem((n.depth_h, n.pairs, n.piece, width), BF16),
            vmem((n.batches, n.sources, n.piece, width), BF16),
            vmem((1, inner), F32), vmem((1, inner), F32),
            vmem((width, width), BF16),
            vmem((2, 1, half), F32),
            vmem((2, n.batches, n.sources, n.piece, half), BF16),
            vmem((n.batches, n.slabs, 2, n.pairs, n.piece, half), BF16),
            dma((11,)),
            dma((2,)), dma((2,)), dma((4,)), dma((4,)), dma((3,)), dma((3,)),
            dma((n.depth_h,)), dma((n.depth_h,)),
            dma((n.depth_h, n.pairs)), dma((n.batches, n.sources)),
            dma((2, n.batches, n.sources)), dma((n.batches, n.slabs, 2, n.pairs)),
        ],
        compiler_params=pltpu.CompilerParams(
            collective_id=0, has_side_effects=True, vmem_limit_bytes=60 << 20
        ),
    )(*args)


def solution(mesh):
    placed = (
        P(("grp", "gy"), "gx", None),
        P(None, "ch"),
        P("ch"),
        P(None, None, "ch"),
        P("ch"),
        P("ch", None),
        P(),
        P(),
        P(None, None, "ch"),
        P("ch", None),
        P("ch"),
    )
    return jax.shard_map(
        functools.partial(per_device, dict(mesh.shape)),
        mesh=mesh,
        in_specs=placed,
        out_specs=P(("grp", "gy"), "gx", "ch"),
        check_vma=False,
    )
```

```python
import functools

import jax
import jax.numpy as jnp
import numpy as np
from jax import lax
from jax.experimental import pallas as pl
from jax.experimental.pallas import tpu as pltpu
from jax.sharding import PartitionSpec as P

HEAD_DIM = 32
GRID = 8
WINDOWS = 2
MESH = pl.DeviceIdType.MESH
F32 = jnp.float32
BF16 = jnp.bfloat16


HALF_ROOT = np.float32(np.sqrt(0.5))


def gelu_scaled(t):
    return t * (HALF_ROOT + HALF_ROOT * lax.erf(t))


def dot(a, b):
    return jnp.dot(a, b, preferred_element_type=F32)


def dot_t(a, b):
    return lax.dot_general(a, b, (((1,), (1,)), ((), ())), preferred_element_type=F32)


def quotient(v, n):
    return v >> (n.bit_length() - 1) if n & (n - 1) == 0 else lax.div(v, n)


def remainder(v, n):
    return v & (n - 1) if n & (n - 1) == 0 else lax.rem(v, n)


def farthest_first(n):
    return sorted(range(1, n), key=lambda k: abs(2 * k - n))


class Plan:
    def __init__(self, mesh_shape, tile_h, tile_w):
        self.n_rows, self.n_cols = mesh_shape["gy"], mesh_shape["gx"]
        self.tile_h, self.tile_w = tile_h, tile_w
        stride_h = tile_h * self.n_rows // GRID
        stride_w = tile_w * self.n_cols // GRID
        self.depth_h, self.depth_w = min(tile_h, stride_h), min(tile_w, stride_w)
        self.steps_h, self.steps_w = stride_h // self.depth_h, stride_w // self.depth_w
        self.n_i, self.n_j = tile_h // self.depth_h, tile_w // self.depth_w
        self.ph, self.pw = GRID // self.n_i, GRID // self.n_j
        self.n_t = self.n_i * self.n_j
        self.sources = self.ph * self.pw
        half_w = self.depth_w // 2
        self.slab = self.depth_w * self.n_t
        self.part = self.slab // 2
        self.pairs = half_w // WINDOWS
        self.slabs = self.sources * WINDOWS // half_w
        self.batches = self.depth_h // self.slabs
        self.piece = WINDOWS * self.n_t
        assert self.pairs % self.pw == 0 and self.pairs // self.pw * self.slabs == self.ph
        assert self.depth_h % self.slabs == 0 and self.depth_h >= 4


def kernel(
    plan, cells_h, w_exp_h, b_exp_h, w_dep_h, b_dep_h, w_proj_h, b_proj_h, gain_h, w_qkv_h, w_out_h,
    b_out_h, out,
    b_exp, w_dep_in, b_dep, b_proj, gain, cells, ordered, w_exp, w_proj, w_qkv, w_out, w_dep,
    exp, halo, edge, colin, edge_x, colin_x, colexp, dbuf, psend, precv, acc, fsend, frecv,
    b_exp_s, b_dep_s, w_vt, bo_full, osend, oin,
    in_s, halo_s, halo_r, col_s, col_r, w_s, w_r, p_s, p_r, f_s, f_r, o_s, o_r,
):
    tile_h, tile_w = plan.tile_h, plan.tile_w
    depth_h, n_i, n_j, n_t = plan.depth_h, plan.n_i, plan.n_j, plan.n_t
    width = cells.shape[2]
    inner = w_exp.shape[1]
    slab, part, pw, slabs = plan.slab, plan.part, plan.pw, plan.slabs
    half = width // 2
    z, x, c = lax.axis_index("gy"), lax.axis_index("gx"), lax.axis_index("ch")
    zs, xs = lax.rem(z, plan.steps_h), lax.rem(x, plan.steps_w)
    mp, mq = lax.div(z, plan.steps_h), lax.div(x, plan.steps_w)
    my_s = mp * pw + mq
    my_slab = lax.rem(mp, slabs)
    my_pair = lax.div(mp, slabs) * pw + mq
    last_z, last_x = plan.n_rows - 1, plan.n_cols - 1
    partner = {"ch": 1 - c}
    has_top, has_bot = z > 0, z < last_z
    has_left, has_right = x > 0, x < last_x

    def peer(s, core):
        p, q = lax.div(s, pw), lax.rem(s, pw)
        return {"gy": p * plan.steps_h + zs, "gx": q * plan.steps_w + xs, "ch": core}

    def owner(ah, pair):
        return (lax.div(pair, pw) * slabs + ah) * pw + lax.rem(pair, pw)

    def remote(src, dst, send, recv, device):
        return pltpu.make_async_remote_copy(
            src_ref=src, dst_ref=dst, send_sem=send, recv_sem=recv,
            device_id=device, device_id_type=MESH,
        )

    mine = pl.ds(pl.multiple_of(c * half, half), half)
    loads = [
        pltpu.make_async_copy(src, dst, in_s.at[n])
        for n, (src, dst) in enumerate((
            (cells_h, cells), (w_exp_h, w_exp), (w_proj_h, w_proj),
            (w_qkv_h, w_qkv.at[:, :, mine]), (w_out_h, w_out.at[mine]),
            (b_exp_h, b_exp), (w_dep_h, w_dep_in), (b_dep_h, b_dep), (b_proj_h, b_proj),
            (gain_h, gain), (b_out_h, bo_full.at[c]),
        ))
    ]
    small = loads[5:]
    for load in loads[:2] + small + loads[2:3]:
        load.start()

    barrier = pltpu.get_barrier_semaphore()
    around = (
        (has_top, {"gy": jnp.maximum(z - 1, 0)}),
        (has_bot, {"gy": jnp.minimum(z + 1, last_z)}),
        (has_left, {"gx": jnp.maximum(x - 1, 0)}),
        (has_right, {"gx": jnp.minimum(x + 1, last_x)}),
    )
    count = jnp.int32(2 * plan.sources - 1)
    for there, device in around:
        @pl.when(there)
        def _():
            pl.semaphore_signal(barrier, inc=1, device_id=device, device_id_type=MESH)
        count = count + there.astype(jnp.int32)

    @pl.loop(0, 2 * plan.sources)
    def _(t):
        s, core = lax.div(t, 2), lax.rem(t, 2)

        @pl.when(jnp.logical_not((s == my_s) & (core == c)))
        def _():
            pl.semaphore_signal(barrier, inc=1, device_id=peer(s, core), device_id_type=MESH)

    down = remote(cells_h.at[tile_h - 1], halo.at[0], halo_s.at[0], halo_r.at[0], around[1][1])
    up = remote(cells_h.at[0], halo.at[1], halo_s.at[1], halo_r.at[1], around[0][1])
    rightward = remote(edge.at[1], colin.at[0], col_s.at[0], col_r.at[0], around[3][1])
    leftward = remote(edge.at[0], colin.at[1], col_s.at[1], col_r.at[1], around[2][1])
    rightward_x = remote(edge_x.at[1], colin_x.at[0], col_s.at[2], col_r.at[2], around[3][1])
    leftward_x = remote(edge_x.at[0], colin_x.at[1], col_s.at[3], col_r.at[3], around[2][1])
    weights = (
        remote(w_qkv_h, w_qkv.at[:, :, mine], w_s.at[0], w_r.at[0], partner),
        remote(w_out_h, w_out.at[mine], w_s.at[1], w_r.at[1], partner),
        remote(b_out_h, bo_full.at[c], w_s.at[2], w_r.at[2], partner),
    )

    def one_hot(rows, columns, source):
        row = lax.broadcasted_iota(jnp.int32, (rows, columns), 0)
        column = lax.broadcasted_iota(jnp.int32, (rows, columns), 1)
        return source(row, column).astype(F32).astype(BF16)

    def cell_of(row):
        b, i, j = quotient(row, n_t), quotient(remainder(row, n_t), n_j), remainder(row, n_j)
        return i * tile_w + j * plan.depth_w + b

    perm = one_hot(slab, slab, lambda row, column: cell_of(row) == column)
    picks = [
        one_hot(tile_h, tile_h * 16, lambda row, column: row * 16 + at == column) for at in (0, 15)
    ]
    loads[0].wait()

    for side, first in ((0, 0), (1, tile_w - 16)):
        border = cells[:, first : first + 16, :].reshape(tile_h * 16, width)
        edge[side] = dot(picks[side], border).astype(BF16)

    def place(e, rows):
        ordered[e] = dot(perm, jnp.concatenate(rows, axis=0)).astype(BF16)

    def place_own(e):
        place(e, [cells[i * depth_h + e - 1] for i in range(n_i)])

    for e in range(1, 4):
        place_own(e)

    lanes_e = 256

    def expand(source, lanes):
        return gelu_scaled(dot(source, w_exp[:, lanes]) * HALF_ROOT + b_exp_s[:, lanes])

    def expand_slabs(e, count):
        source = ordered[pl.ds(e, count)].reshape(count * slab, width)
        for n in range(inner // lanes_e):
            lanes = slice(n * lanes_e, (n + 1) * lanes_e)
            value = expand(source, lanes)
            for k in range(count):
                exp[e + k, n_t : n_t + slab, lanes] = value[k * slab : (k + 1) * slab]

    ok_top, ok_bot = has_top.astype(F32), has_bot.astype(F32)
    ok_left, ok_right = has_left.astype(F32), has_right.astype(F32)

    def border_columns(e):
        at = lax.broadcasted_iota(jnp.int32, (n_t, inner), 0)
        left = exp[e, slab : slab + n_t, :]
        right = exp[e, n_t : 2 * n_t, :]
        if n_t > 1:
            left = pltpu.roll(left, 1, 0)
            right = pltpu.roll(right, n_t - 1, 0)
        for i in range(n_i):
            row = i * depth_h + e - 1
            above, below = row < 0, row >= tile_h
            ok = jnp.where(above, ok_top, jnp.where(below, ok_bot, jnp.float32(1)))
            row = jnp.where(above, tile_h, jnp.where(below, tile_h + 1, row))
            left = jnp.where(at == i * n_j, colexp[0, pl.ds(row, 1), :] * (ok_left * ok), left)
            right = jnp.where(
                at == i * n_j + n_j - 1, colexp[1, pl.ds(row, 1), :] * (ok_right * ok), right
            )
        exp[e, 0:n_t, :] = left
        exp[e, n_t + slab : 2 * n_t + slab, :] = right

    pl.semaphore_wait(barrier, count)

    @pl.when(has_right)
    def _():
        rightward.start()

    @pl.when(has_left)
    def _():
        leftward.start()

    @pl.when(has_bot)
    def _():
        down.start()

    @pl.when(has_top)
    def _():
        up.start()

    for copy in weights:
        copy.start()

    for load in small:
        load.wait()
    for di in range(3):
        w_dep[3 * di : 3 * di + 3] = w_dep_in[di].astype(F32) * HALF_ROOT
    b_exp_s[...] = b_exp[...] * HALF_ROOT
    b_dep_s[...] = b_dep[...] * HALF_ROOT
    loads[1].wait()
    loads[3].start()
    loads[4].start()
    expand_slabs(1, 3)

    @pl.loop(4, depth_h + 1)
    def _(e):
        place_own(e)

    def await_or_zero(pairs):
        for buffer, index, there, copy in pairs:
            @pl.when(there)
            def _():
                copy.wait_recv()

            @pl.when(jnp.logical_not(there))
            def _():
                buffer[index] = jnp.zeros(buffer.shape[1:], BF16)

    await_or_zero(((colin, 0, has_left, rightward), (colin, 1, has_right, leftward)))

    def expand_columns(source, first):
        rows = source.shape[1]
        flat = source[...].reshape(2 * rows, width)
        for n in range(inner // lanes_e):
            lanes = slice(n * lanes_e, (n + 1) * lanes_e)
            value = expand(flat, lanes)
            colexp[0, first : first + rows, lanes] = value[:rows]
            colexp[1, first : first + rows, lanes] = value[rows:]

    expand_columns(colin, 0)

    @pl.loop(1, 4)
    def _(e):
        border_columns(e)

    lanes_d = 128
    strip = min(32, part)

    def partial_copy(u):
        return remote(psend.at[u], precv.at[u], p_s, p_r.at[u], partner)

    def depth_slab(a):
        for chunk in range(inner // lanes_d):
            lanes = slice(chunk * lanes_d, (chunk + 1) * lanes_d)
            for n in range(slab // strip):
                total = None
                for di in range(3):
                    rows = exp[a + di, n * strip : (n + 1) * strip + 2 * n_t, lanes]
                    for dj in range(3):
                        k = 3 * di + dj
                        term = rows[dj * n_t : dj * n_t + strip] * w_dep[k : k + 1, lanes]
                        total = term if total is None else total + term
                value = gelu_scaled(total + b_dep_s[:, lanes]).astype(BF16)
                core, place_in = divmod(n * strip, part)
                first = pl.multiple_of(jnp.where(c == core, part, 0) + place_in, strip)
                dbuf[pl.ds(first, strip), lanes] = value

    def project_slab(u, a):
        projected = dot(dbuf[...], w_proj[...])
        psend[u] = projected[:part].astype(BF16)
        partial_copy(u).start()
        own = ordered[a + 1, pl.ds(pl.multiple_of(c * part, part), part)]
        acc[u] = projected[part:] + own.astype(F32) + b_proj[...]

    def forward_copy(u, pair):
        m, ah = lax.div(u, slabs), lax.rem(u, slabs)
        s = owner(ah, pair)
        return remote(
            fsend.at[u * plan.pairs + pair], frecv.at[m, my_s], f_s, f_r.at[m], peer(s, c)
        )

    def finish(u):
        m = lax.div(u, slabs)
        partial_copy(u).wait_recv()
        mixed = (acc[u] + precv[u].astype(F32)).astype(BF16)
        for pair in range(plan.pairs):
            fsend[u * plan.pairs + pair] = mixed[pair * plan.piece : (pair + 1) * plan.piece]

        for k in farthest_first(plan.pairs):
            forward_copy(u, lax.rem(my_pair + k, plan.pairs)).start()

        @pl.when(lax.rem(u, slabs) == my_slab)
        def _():
            frecv[m, my_s] = fsend[u * plan.pairs + my_pair]

        @pl.when(lax.rem(u, slabs) != my_slab)
        def _():
            forward_copy(u, my_pair).start()

    eye = (
        lax.broadcasted_iota(jnp.int32, (half, half), 0)
        == lax.broadcasted_iota(jnp.int32, (half, half), 1)
    ).astype(F32).astype(BF16)
    def await_weights():
        loads[3].wait()
        loads[4].wait()
        for copy in weights:
            copy.wait_recv()
        w_vt[:half] = dot_t(eye, w_qkv[2, :, :half]).astype(BF16)
        w_vt[half:] = dot_t(eye, w_qkv[2, :, half:]).astype(BF16)

    def await_batch(m):
        others = frecv.at[m, pl.ds(0, plan.sources - 1)]
        remote(others, others, f_s, f_r.at[m], partner).wait_recv()

    keys = plan.sources * n_t
    tokens = WINDOWS * keys
    group = 128
    n_h = group // HEAD_DIM
    lane = lax.broadcasted_iota(jnp.int32, (1, WINDOWS * 2 * group), 1)
    head_masks = [
        (remainder(quotient(lane, HEAD_DIM), n_h) == h).astype(F32).astype(BF16) for h in range(n_h)
    ]
    lane_w = lax.div(lax.broadcasted_iota(jnp.int32, (1, tokens), 1), keys)
    window_masks = [(lane_w == w).astype(F32).astype(BF16) for w in range(WINDOWS)]
    scale = np.float32(HEAD_DIM ** (-0.5) * np.log2(np.e))
    duos = width // (2 * group)
    eye_t = eye[:tokens, :tokens]

    def attend(normed):
        query = dot(normed, w_qkv[0])
        keyset = dot(normed, w_qkv[1])
        values = dot_t(w_vt[...], normed)
        query = (query * scale).astype(BF16)
        keyset = keyset.astype(BF16)
        values = values.astype(BF16)
        blank = jnp.zeros((keys, group), BF16)
        blocks = [(w, g) for w in range(WINDOWS) for g in range(2)]
        lefts, rights = [], []
        for duo in range(duos):
            rights.append(jnp.concatenate([
                jnp.concatenate([
                    query[w * keys : (w + 1) * keys, (2 * duo + g) * group : (2 * duo + g + 1) * group]
                    if block == (w, g) else blank
                    for block in blocks
                ], axis=1)
                for g in range(2) for w in range(WINDOWS)
            ], axis=0))
            left = jnp.concatenate([
                keyset[w * keys : (w + 1) * keys, 2 * duo * group : (2 * duo + 2) * group]
                for w in range(WINDOWS)
            ], axis=1)
            lefts.append(jnp.concatenate([left * mask for mask in head_masks], axis=0))
        scores = [dot_t(left, right) for left, right in zip(lefts, rights)]
        nothing = jnp.zeros((HEAD_DIM, tokens), BF16)
        stacked, spreads, shares = [], [], []
        for duo in range(duos):
            score = scores[duo].reshape(n_h, keys, 2 * tokens)
            top = jnp.max(score, axis=1, keepdims=True)
            power = jnp.exp2(score - top)
            share = 1.0 / jnp.sum(power, axis=1, keepdims=True)
            power = power.astype(BF16)
            for g in range(2):
                lanes = slice(g * tokens, (g + 1) * tokens)
                shares.append(share[:, :, lanes])
                spreads.append(jnp.concatenate(
                    [power[h, :, lanes] * mask for h in range(n_h) for mask in window_masks], axis=0
                ))
                first = (2 * duo + g) * group
                stacked.append(jnp.concatenate([
                    jnp.concatenate([
                        values[first + h * HEAD_DIM : first + (h + 1) * HEAD_DIM]
                        if h == at else nothing
                        for at in range(n_h)
                    ], axis=1)
                    for h in range(n_h)
                ], axis=0))
        found = [dot(a, b) for a, b in zip(stacked, spreads)]
        found = jnp.concatenate([
            (f.reshape(n_h, HEAD_DIM, tokens) * share).reshape(group, tokens).astype(BF16)
            for f, share in zip(found, shares)
        ], axis=0)
        return dot_t(eye_t, found).astype(BF16)

    def return_copy(m, s, side):
        return remote(
            osend.at[(m * plan.sources + s) * 2 + side], oin.at[m, (my_slab * 2 + c) * plan.pairs + my_pair],
            o_s, o_r.at[m], peer(s, side),
        )

    def attend_batch(m):
        await_batch(m)
        came = frecv[m].astype(F32)
        mixed = jnp.concatenate([
            came[:, w * n_t : (w + 1) * n_t].reshape(keys, width) for w in range(WINDOWS)
        ], axis=0)
        centered = mixed - jnp.mean(mixed, axis=-1, keepdims=True)
        spread = jnp.mean(centered * centered, axis=-1, keepdims=True)
        normed = (centered * lax.rsqrt(spread + 1e-05) * gain[...]).astype(BF16)
        total = mixed + dot(attend(normed), w_out[...])
        for side in range(2):
            lanes = slice(side * half, (side + 1) * half)
            value = total[:, lanes] + bo_full[side]
            value = jnp.concatenate([
                value[w * keys : (w + 1) * keys].reshape(plan.sources, n_t, half)
                for w in range(WINDOWS)
            ], axis=1)
            value = value.astype(BF16)
            for at in range(plan.sources):
                osend[(m * plan.sources + at) * 2 + side] = value[at]

        oin[m, (my_slab * 2 + c) * plan.pairs + my_pair] = osend[(m * plan.sources + my_s) * 2 + c]
        for k in farthest_first(plan.sources):
            for side in range(2):
                return_copy(m, lax.rem(my_s + k, plan.sources), side).start()
        return_copy(m, my_s, 1 - c).start()

    loads[2].wait()
    token_row = lax.broadcasted_iota(jnp.int32, (slab, 1), 0)
    token_i = remainder(quotient(token_row, n_j), n_i)

    def bottleneck(u):
        a = lax.rem(u + 1, depth_h)
        e = lax.rem(u + 4, depth_h + 2)

        @pl.when(u == (depth_h - 3) // 2 + 1)
        def _():
            await_or_zero(((halo, 0, has_top, down), (halo, 1, has_bot, up)))
            place(0, [halo[0]] + [cells[i * depth_h - 1] for i in range(1, n_i)])
            place(depth_h + 1, [cells[i * depth_h] for i in range(1, n_i)] + [halo[1]])
            at_row = lax.broadcasted_iota(jnp.int32, edge_x.shape[1:], 0)
            for side, col in ((0, 0), (1, tile_w - 1)):
                top = halo[0].astype(F32)[col : col + 1]
                bottom = halo[1].astype(F32)[col : col + 1]
                edge_x[side] = jnp.where(at_row == 0, top, bottom).astype(BF16)

            @pl.when(has_right)
            def _():
                rightward_x.start()

            @pl.when(has_left)
            def _():
                leftward_x.start()

        depth_slab(a)
        project_slab(u, a)

        @pl.when(u == depth_h - 3)
        def _():
            await_or_zero(((colin_x, 0, has_left, rightward_x), (colin_x, 1, has_right, leftward_x)))
            expand_columns(colin_x, tile_h)

        @pl.when(u < depth_h - 1)
        def _():
            expand_slabs(e, 1)

            @pl.when((e == 0) | (e == depth_h + 1))
            def _():
                outside = jnp.where(
                    e == 0,
                    jnp.where(token_i == 0, 1 - ok_top, 0.0),
                    jnp.where(token_i == n_i - 1, 1 - ok_bot, 0.0),
                )
                exp[e, n_t : n_t + slab] = exp[e, n_t : n_t + slab] * (1 - outside)

            border_columns(e)

    lag = depth_h

    @pl.loop(0, lag + plan.batches)
    def _(t):
        @pl.when(t < depth_h)
        def _():
            bottleneck(t)

        @pl.when((t > 0) & (t <= depth_h))
        def _():
            finish(t - 1)

        @pl.when(t == lag)
        def _():
            await_weights()

        @pl.when(t >= lag)
        def _():
            attend_batch(t - lag)

    @pl.when(has_bot)
    def _():
        down.wait_send()

    @pl.when(has_top)
    def _():
        up.wait_send()

    @pl.when(has_right)
    def _():
        rightward.wait_send()
        rightward_x.wait_send()

    @pl.when(has_left)
    def _():
        leftward.wait_send()
        leftward_x.wait_send()

    for copy in weights:
        copy.wait_send()

    remote(psend, psend, p_s, p_r.at[0], partner).wait_send()
    sent = fsend.at[pl.ds(0, depth_h * plan.pairs - plan.batches)]
    remote(sent, sent, f_s, f_r.at[0], partner).wait_send()

    perm_t = one_hot(slab, slab, lambda row, column: cell_of(column) == row)

    @pl.loop(0, plan.batches)
    def _(m):
        others = oin.at[m, pl.ds(0, 2 * plan.sources - 1)]
        remote(others, others, o_s, o_r.at[m], partner).wait_recv()
        pieces = 2 * plan.pairs
        for ah in range(slabs):
            arrived = oin[m, ah * pieces : (ah + 1) * pieces].astype(F32)
            placed = dot(perm_t, arrived.reshape(slab, half).astype(BF16)).astype(BF16)
            a = lax.rem(m * slabs + ah + 1, depth_h)
            for i in range(n_i):
                out[i * depth_h + a] = placed[i * tile_w : (i + 1) * tile_w]

    sent = osend.at[pl.ds(0, plan.batches * (2 * plan.sources - 1))]
    remote(sent, sent, o_s, o_r.at[0], partner).wait_send()


def per_device(
    mesh_shape, cells, w_expand, b_expand, w_depth, b_depth, w_project, b_project, ln_gain,
    w_qkv, w_out, b_out,
):
    tile_h, tile_w, width = cells.shape
    plan = Plan(mesh_shape, tile_h, tile_w)
    inner = w_expand.shape[1]
    half = width // 2
    args = (
        cells, w_expand, b_expand[None], w_depth, b_depth[None],
        w_project, b_project[None], ln_gain[None], w_qkv.transpose(1, 0, 2), w_out, b_out[None],
    )
    dma = pltpu.SemaphoreType.DMA
    vmem = pltpu.VMEM
    n = plan
    rows_x = 16
    return pl.pallas_call(
        functools.partial(kernel, plan),
        out_shape=jax.ShapeDtypeStruct((tile_h, tile_w, half), BF16),
        in_specs=[
            pl.BlockSpec(memory_space=pl.ANY) for _ in args
        ],
        out_specs=pl.BlockSpec(memory_space=pltpu.VMEM),
        scratch_shapes=[
            vmem((1, inner), F32), vmem(w_depth.shape, BF16), vmem((1, inner), F32),
            vmem((1, width), F32), vmem((1, width), F32),
            vmem(cells.shape, BF16), vmem((n.depth_h + 2, n.slab, width), BF16),
            vmem(w_expand.shape, BF16), vmem(w_project.shape, BF16),
            vmem((3, width, width), BF16), vmem((width, width), BF16), vmem((9, inner), F32),
            vmem((n.depth_h + 2, n.slab + 2 * n.n_t, inner), F32),
            vmem((2, tile_w, width), BF16),
            vmem((2, tile_h, width), BF16),
            vmem((2, tile_h, width), BF16),
            vmem((2, rows_x, width), BF16),
            vmem((2, rows_x, width), BF16),
            vmem((2, tile_h + rows_x, inner), F32),
            vmem((n.slab, inner), BF16),
            vmem((n.depth_h, n.part, width), BF16),
            vmem((n.depth_h, n.part, width), BF16),
            vmem((n.depth_h, n.part, width), F32),
            vmem((n.depth_h * n.pairs, n.piece, width), BF16),
            vmem((n.batches, n.sources, n.piece, width), BF16),
            vmem((1, inner), F32), vmem((1, inner), F32),
            vmem((width, width), BF16),
            vmem((2, 1, half), F32),
            vmem((n.batches * n.sources * 2, n.piece, half), BF16),
            vmem((n.batches, n.sources * 2, n.piece, half), BF16),
            dma((11,)),
            dma((2,)), dma((2,)), dma((4,)), dma((4,)), dma((3,)), dma((3,)),
            dma, dma((n.depth_h,)), dma, dma((n.batches,)), dma, dma((n.batches,)),
        ],
        compiler_params=pltpu.CompilerParams(
            collective_id=0, has_side_effects=True, vmem_limit_bytes=60 << 20
        ),
    )(*args)


def solution(mesh):
    placed = (
        P(("grp", "gy"), "gx", None),
        P(None, "ch"),
        P("ch"),
        P(None, None, "ch"),
        P("ch"),
        P("ch", None),
        P(),
        P(),
        P(None, None, "ch"),
        P("ch", None),
        P("ch"),
    )
    return jax.shard_map(
        functools.partial(per_device, dict(mesh.shape)),
        mesh=mesh,
        in_specs=placed,
        out_specs=P(("grp", "gy"), "gx", "ch"),
        check_vma=False,
    )
```

```python
import functools

import jax
import jax.numpy as jnp
import numpy as np
from jax import lax
from jax.experimental import pallas as pl
from jax.experimental.pallas import tpu as pltpu
from jax.sharding import PartitionSpec as P

HEAD_DIM = 32
GRID = 8
WINDOWS = 2
MESH = pl.DeviceIdType.MESH
F32 = jnp.float32
BF16 = jnp.bfloat16


HALF_ROOT = np.float32(np.sqrt(0.5))


def gelu_scaled(t):
    return t * (HALF_ROOT + HALF_ROOT * lax.erf(t))


def dot(a, b):
    return jnp.dot(a, b, preferred_element_type=F32)


def dot_t(a, b):
    return lax.dot_general(a, b, (((1,), (1,)), ((), ())), preferred_element_type=F32)


def quotient(v, n):
    return v >> (n.bit_length() - 1) if n & (n - 1) == 0 else lax.div(v, n)


def remainder(v, n):
    return v & (n - 1) if n & (n - 1) == 0 else lax.rem(v, n)


def farthest_first(n):
    return sorted(range(1, n), key=lambda k: abs(2 * k - n))


class Plan:
    def __init__(self, mesh_shape, tile_h, tile_w):
        self.n_rows, self.n_cols = mesh_shape["gy"], mesh_shape["gx"]
        self.tile_h, self.tile_w = tile_h, tile_w
        stride_h = tile_h * self.n_rows // GRID
        stride_w = tile_w * self.n_cols // GRID
        self.depth_h, self.depth_w = min(tile_h, stride_h), min(tile_w, stride_w)
        self.steps_h, self.steps_w = stride_h // self.depth_h, stride_w // self.depth_w
        self.n_i, self.n_j = tile_h // self.depth_h, tile_w // self.depth_w
        self.ph, self.pw = GRID // self.n_i, GRID // self.n_j
        self.n_t = self.n_i * self.n_j
        self.sources = self.ph * self.pw
        half_w = self.depth_w // 2
        self.slab = self.depth_w * self.n_t
        self.part = self.slab // 2
        self.pairs = half_w // WINDOWS
        self.slabs = self.sources * WINDOWS // half_w
        self.batches = self.depth_h // self.slabs
        self.piece = WINDOWS * self.n_t
        assert self.pairs % self.pw == 0 and self.pairs // self.pw * self.slabs == self.ph
        assert self.depth_h % self.slabs == 0 and self.depth_h >= 4


def kernel(
    plan, cells_h, w_exp_h, b_exp_h, w_dep_h, b_dep_h, w_proj_h, b_proj_h, gain_h, w_qkv_h, w_out_h,
    b_out_h, out,
    b_exp, w_dep_in, b_dep, b_proj, gain, cells, ordered, w_exp, w_proj, w_qkv, w_out, w_dep,
    exp, halo, edge, colin, edge_x, colin_x, colexp, dbuf, psend, precv, acc, fsend, frecv,
    b_exp_s, b_dep_s, w_vt, bo_full, osend, oin, result,
    out_s, in_s, halo_s, halo_r, col_s, col_r, w_s, w_r, p_s, p_r, f_s, f_r, o_s, o_r,
):
    tile_h, tile_w = plan.tile_h, plan.tile_w
    depth_h, n_i, n_j, n_t = plan.depth_h, plan.n_i, plan.n_j, plan.n_t
    width = cells.shape[2]
    inner = w_exp.shape[1]
    slab, part, pw, slabs = plan.slab, plan.part, plan.pw, plan.slabs
    half = width // 2
    z, x, c = lax.axis_index("gy"), lax.axis_index("gx"), lax.axis_index("ch")
    zs, xs = lax.rem(z, plan.steps_h), lax.rem(x, plan.steps_w)
    mp, mq = lax.div(z, plan.steps_h), lax.div(x, plan.steps_w)
    my_s = mp * pw + mq
    my_slab = lax.rem(mp, slabs)
    my_pair = lax.div(mp, slabs) * pw + mq
    last_z, last_x = plan.n_rows - 1, plan.n_cols - 1
    partner = {"ch": 1 - c}
    has_top, has_bot = z > 0, z < last_z
    has_left, has_right = x > 0, x < last_x

    def peer(s, core):
        p, q = lax.div(s, pw), lax.rem(s, pw)
        return {"gy": p * plan.steps_h + zs, "gx": q * plan.steps_w + xs, "ch": core}

    def owner(ah, pair):
        return (lax.div(pair, pw) * slabs + ah) * pw + lax.rem(pair, pw)

    def remote(src, dst, send, recv, device):
        return pltpu.make_async_remote_copy(
            src_ref=src, dst_ref=dst, send_sem=send, recv_sem=recv,
            device_id=device, device_id_type=MESH,
        )

    mine = pl.ds(pl.multiple_of(c * half, half), half)
    loads = [
        pltpu.make_async_copy(src, dst, in_s.at[n])
        for n, (src, dst) in enumerate((
            (cells_h, cells), (w_exp_h, w_exp), (w_proj_h, w_proj),
            (w_qkv_h, w_qkv.at[:, :, mine]), (w_out_h, w_out.at[mine]),
            (b_exp_h, b_exp), (w_dep_h, w_dep_in), (b_dep_h, b_dep), (b_proj_h, b_proj),
            (gain_h, gain), (b_out_h, bo_full.at[c]),
        ))
    ]
    small = loads[5:]
    for load in loads[:2] + small + loads[2:3]:
        load.start()

    barrier = pltpu.get_barrier_semaphore()
    around = (
        (has_top, {"gy": jnp.maximum(z - 1, 0)}),
        (has_bot, {"gy": jnp.minimum(z + 1, last_z)}),
        (has_left, {"gx": jnp.maximum(x - 1, 0)}),
        (has_right, {"gx": jnp.minimum(x + 1, last_x)}),
    )
    count = jnp.int32(2 * plan.sources - 1)
    for there, device in around:
        @pl.when(there)
        def _():
            pl.semaphore_signal(barrier, inc=1, device_id=device, device_id_type=MESH)
        count = count + there.astype(jnp.int32)

    @pl.loop(0, 2 * plan.sources)
    def _(t):
        s, core = lax.div(t, 2), lax.rem(t, 2)

        @pl.when(jnp.logical_not((s == my_s) & (core == c)))
        def _():
            pl.semaphore_signal(barrier, inc=1, device_id=peer(s, core), device_id_type=MESH)

    down = remote(cells_h.at[tile_h - 1], halo.at[0], halo_s.at[0], halo_r.at[0], around[1][1])
    up = remote(cells_h.at[0], halo.at[1], halo_s.at[1], halo_r.at[1], around[0][1])
    rightward = remote(edge.at[1], colin.at[0], col_s.at[0], col_r.at[0], around[3][1])
    leftward = remote(edge.at[0], colin.at[1], col_s.at[1], col_r.at[1], around[2][1])
    rightward_x = remote(edge_x.at[1], colin_x.at[0], col_s.at[2], col_r.at[2], around[3][1])
    leftward_x = remote(edge_x.at[0], colin_x.at[1], col_s.at[3], col_r.at[3], around[2][1])
    weights = (
        remote(w_qkv_h, w_qkv.at[:, :, mine], w_s.at[0], w_r.at[0], partner),
        remote(w_out_h, w_out.at[mine], w_s.at[1], w_r.at[1], partner),
        remote(b_out_h, bo_full.at[c], w_s.at[2], w_r.at[2], partner),
    )

    def one_hot(rows, columns, source):
        row = lax.broadcasted_iota(jnp.int32, (rows, columns), 0)
        column = lax.broadcasted_iota(jnp.int32, (rows, columns), 1)
        return source(row, column).astype(F32).astype(BF16)

    def cell_of(row):
        b, i, j = quotient(row, n_t), quotient(remainder(row, n_t), n_j), remainder(row, n_j)
        return i * tile_w + j * plan.depth_w + b

    perm = one_hot(slab, slab, lambda row, column: cell_of(row) == column)
    picks = [
        one_hot(tile_h, tile_h * 16, lambda row, column: row * 16 + at == column) for at in (0, 15)
    ]
    loads[0].wait()

    for side, first in ((0, 0), (1, tile_w - 16)):
        border = cells[:, first : first + 16, :].reshape(tile_h * 16, width)
        edge[side] = dot(picks[side], border).astype(BF16)

    def place(e, rows):
        ordered[e] = dot(perm, jnp.concatenate(rows, axis=0)).astype(BF16)

    def place_own(e):
        place(e, [cells[i * depth_h + e - 1] for i in range(n_i)])

    ahead = 4
    for e in range(1, ahead + 1):
        place_own(e)

    lanes_e = 256

    def expand(source, lanes):
        return gelu_scaled(dot(source, w_exp[:, lanes]) * HALF_ROOT + b_exp_s[:, lanes])

    def expand_slabs(e, count):
        source = ordered[pl.ds(e, count)].reshape(count * slab, width)
        for n in range(inner // lanes_e):
            lanes = slice(n * lanes_e, (n + 1) * lanes_e)
            value = expand(source, lanes)
            for k in range(count):
                exp[e + k, n_t : n_t + slab, lanes] = value[k * slab : (k + 1) * slab]

    ok_top, ok_bot = has_top.astype(F32), has_bot.astype(F32)
    ok_left, ok_right = has_left.astype(F32), has_right.astype(F32)

    def border_columns(e):
        at = lax.broadcasted_iota(jnp.int32, (n_t, inner), 0)
        left = exp[e, slab : slab + n_t, :]
        right = exp[e, n_t : 2 * n_t, :]
        if n_t > 1:
            left = pltpu.roll(left, 1, 0)
            right = pltpu.roll(right, n_t - 1, 0)
        for i in range(n_i):
            row = i * depth_h + e - 1
            above, below = row < 0, row >= tile_h
            ok = jnp.where(above, ok_top, jnp.where(below, ok_bot, jnp.float32(1)))
            row = jnp.where(above, tile_h, jnp.where(below, tile_h + 1, row))
            left = jnp.where(at == i * n_j, colexp[0, pl.ds(row, 1), :] * (ok_left * ok), left)
            right = jnp.where(
                at == i * n_j + n_j - 1, colexp[1, pl.ds(row, 1), :] * (ok_right * ok), right
            )
        exp[e, 0:n_t, :] = left
        exp[e, n_t + slab : 2 * n_t + slab, :] = right

    pl.semaphore_wait(barrier, count)

    @pl.when(has_right)
    def _():
        rightward.start()

    @pl.when(has_left)
    def _():
        leftward.start()

    @pl.when(has_bot)
    def _():
        down.start()

    @pl.when(has_top)
    def _():
        up.start()

    for copy in weights:
        copy.start()

    for load in small:
        load.wait()
    for di in range(3):
        w_dep[3 * di : 3 * di + 3] = w_dep_in[di].astype(F32) * HALF_ROOT
    b_exp_s[...] = b_exp[...] * HALF_ROOT
    b_dep_s[...] = b_dep[...] * HALF_ROOT
    loads[1].wait()
    loads[3].start()
    loads[4].start()
    expand_slabs(1, ahead)

    @pl.loop(ahead + 1, depth_h + 1)
    def _(e):
        place_own(e)

    def await_or_zero(pairs):
        for buffer, index, there, copy in pairs:
            @pl.when(there)
            def _():
                copy.wait_recv()

            @pl.when(jnp.logical_not(there))
            def _():
                buffer[index] = jnp.zeros(buffer.shape[1:], BF16)

    await_or_zero(((colin, 0, has_left, rightward), (colin, 1, has_right, leftward)))

    def expand_columns(source, first):
        rows = source.shape[1]
        flat = source[...].reshape(2 * rows, width)
        for n in range(inner // lanes_e):
            lanes = slice(n * lanes_e, (n + 1) * lanes_e)
            value = expand(flat, lanes)
            colexp[0, first : first + rows, lanes] = value[:rows]
            colexp[1, first : first + rows, lanes] = value[rows:]

    expand_columns(colin, 0)

    @pl.loop(1, ahead + 1)
    def _(e):
        border_columns(e)

    lanes_d = 128
    strip = min(32, part)

    def partial_copy(u):
        return remote(psend.at[u], precv.at[u], p_s, p_r.at[u], partner)

    def depth_slab(a):
        for chunk in range(inner // lanes_d):
            lanes = slice(chunk * lanes_d, (chunk + 1) * lanes_d)
            for n in range(slab // strip):
                total = None
                for di in range(3):
                    rows = exp[a + di, n * strip : (n + 1) * strip + 2 * n_t, lanes]
                    for dj in range(3):
                        k = 3 * di + dj
                        term = rows[dj * n_t : dj * n_t + strip] * w_dep[k : k + 1, lanes]
                        total = term if total is None else total + term
                value = gelu_scaled(total + b_dep_s[:, lanes]).astype(BF16)
                core, place_in = divmod(n * strip, part)
                first = pl.multiple_of(jnp.where(c == core, part, 0) + place_in, strip)
                dbuf[pl.ds(first, strip), lanes] = value

    def project_slab(u, a):
        projected = dot(dbuf[...], w_proj[...])
        psend[u] = projected[:part].astype(BF16)
        partial_copy(u).start()
        own = ordered[a + 1, pl.ds(pl.multiple_of(c * part, part), part)]
        acc[u] = projected[part:] + own.astype(F32) + b_proj[...]

    def forward_copy(u, pair):
        m, ah = lax.div(u, slabs), lax.rem(u, slabs)
        s = owner(ah, pair)
        return remote(
            fsend.at[u * plan.pairs + pair], frecv.at[m, my_s], f_s, f_r.at[m], peer(s, c)
        )

    def finish(u):
        m = lax.div(u, slabs)
        partial_copy(u).wait_recv()
        mixed = (acc[u] + precv[u].astype(F32)).astype(BF16)
        for pair in range(plan.pairs):
            fsend[u * plan.pairs + pair] = mixed[pair * plan.piece : (pair + 1) * plan.piece]

        for k in farthest_first(plan.pairs):
            forward_copy(u, lax.rem(my_pair + k, plan.pairs)).start()

        @pl.when(lax.rem(u, slabs) == my_slab)
        def _():
            frecv[m, my_s] = fsend[u * plan.pairs + my_pair]

        @pl.when(lax.rem(u, slabs) != my_slab)
        def _():
            forward_copy(u, my_pair).start()

    eye = (
        lax.broadcasted_iota(jnp.int32, (half, half), 0)
        == lax.broadcasted_iota(jnp.int32, (half, half), 1)
    ).astype(F32).astype(BF16)
    def await_weights():
        loads[3].wait()
        loads[4].wait()
        for copy in weights:
            copy.wait_recv()
        w_vt[:half] = dot_t(eye, w_qkv[2, :, :half]).astype(BF16)
        w_vt[half:] = dot_t(eye, w_qkv[2, :, half:]).astype(BF16)

    def await_batch(m):
        others = frecv.at[m, pl.ds(0, plan.sources - 1)]
        remote(others, others, f_s, f_r.at[m], partner).wait_recv()

    keys = plan.sources * n_t
    tokens = WINDOWS * keys
    group = 128
    n_h = group // HEAD_DIM
    lane = lax.broadcasted_iota(jnp.int32, (1, WINDOWS * 2 * group), 1)
    head_masks = [
        (remainder(quotient(lane, HEAD_DIM), n_h) == h).astype(F32).astype(BF16) for h in range(n_h)
    ]
    lane_w = lax.div(lax.broadcasted_iota(jnp.int32, (1, tokens), 1), keys)
    window_masks = [(lane_w == w).astype(F32).astype(BF16) for w in range(WINDOWS)]
    scale = np.float32(HEAD_DIM ** (-0.5) * np.log2(np.e))
    duos = width // (2 * group)
    eye_t = eye[:tokens, :tokens]

    def attend(normed):
        query = dot(normed, w_qkv[0])
        keyset = dot(normed, w_qkv[1])
        values = dot_t(w_vt[...], normed)
        query = (query * scale).astype(BF16)
        keyset = keyset.astype(BF16)
        values = values.astype(BF16)
        blank = jnp.zeros((keys, group), BF16)
        blocks = [(w, g) for w in range(WINDOWS) for g in range(2)]
        lefts, rights = [], []
        for duo in range(duos):
            rights.append(jnp.concatenate([
                jnp.concatenate([
                    query[w * keys : (w + 1) * keys, (2 * duo + g) * group : (2 * duo + g + 1) * group]
                    if block == (w, g) else blank
                    for block in blocks
                ], axis=1)
                for g in range(2) for w in range(WINDOWS)
            ], axis=0))
            left = jnp.concatenate([
                keyset[w * keys : (w + 1) * keys, 2 * duo * group : (2 * duo + 2) * group]
                for w in range(WINDOWS)
            ], axis=1)
            lefts.append(jnp.concatenate([left * mask for mask in head_masks], axis=0))
        scores = [dot_t(left, right) for left, right in zip(lefts, rights)]
        nothing = jnp.zeros((HEAD_DIM, tokens), BF16)
        stacked, spreads, shares = [], [], []
        for duo in range(duos):
            score = scores[duo].reshape(n_h, keys, 2 * tokens)
            top = jnp.max(score, axis=1, keepdims=True)
            power = jnp.exp2(score - top)
            share = 1.0 / jnp.sum(power, axis=1, keepdims=True)
            power = power.astype(BF16)
            for g in range(2):
                lanes = slice(g * tokens, (g + 1) * tokens)
                shares.append(share[:, :, lanes])
                spreads.append(jnp.concatenate(
                    [power[h, :, lanes] * mask for h in range(n_h) for mask in window_masks], axis=0
                ))
                first = (2 * duo + g) * group
                stacked.append(jnp.concatenate([
                    jnp.concatenate([
                        values[first + h * HEAD_DIM : first + (h + 1) * HEAD_DIM]
                        if h == at else nothing
                        for at in range(n_h)
                    ], axis=1)
                    for h in range(n_h)
                ], axis=0))
        found = [dot(a, b) for a, b in zip(stacked, spreads)]
        found = jnp.concatenate([
            (f.reshape(n_h, HEAD_DIM, tokens) * share).reshape(group, tokens).astype(BF16)
            for f, share in zip(found, shares)
        ], axis=0)
        return dot_t(eye_t, found).astype(BF16)

    def return_copy(m, s, side):
        return remote(
            osend.at[(m * plan.sources + s) * 2 + side], oin.at[m, (my_slab * 2 + c) * plan.pairs + my_pair],
            o_s, o_r.at[m], peer(s, side),
        )

    def attend_batch(m):
        await_batch(m)
        came = frecv[m].astype(F32)
        mixed = jnp.concatenate([
            came[:, w * n_t : (w + 1) * n_t].reshape(keys, width) for w in range(WINDOWS)
        ], axis=0)
        centered = mixed - jnp.mean(mixed, axis=-1, keepdims=True)
        spread = jnp.mean(centered * centered, axis=-1, keepdims=True)
        normed = (centered * lax.rsqrt(spread + 1e-05) * gain[...]).astype(BF16)
        total = mixed + dot(attend(normed), w_out[...])
        for side in range(2):
            lanes = slice(side * half, (side + 1) * half)
            value = total[:, lanes] + bo_full[side]
            value = jnp.concatenate([
                value[w * keys : (w + 1) * keys].reshape(plan.sources, n_t, half)
                for w in range(WINDOWS)
            ], axis=1)
            value = value.astype(BF16)
            for at in range(plan.sources):
                osend[(m * plan.sources + at) * 2 + side] = value[at]

        oin[m, (my_slab * 2 + c) * plan.pairs + my_pair] = osend[(m * plan.sources + my_s) * 2 + c]
        for k in farthest_first(plan.sources):
            for side in range(2):
                return_copy(m, lax.rem(my_s + k, plan.sources), side).start()
        return_copy(m, my_s, 1 - c).start()

    loads[2].wait()
    token_row = lax.broadcasted_iota(jnp.int32, (slab, 1), 0)
    token_i = remainder(quotient(token_row, n_j), n_i)

    def bottleneck(u):
        a = lax.rem(u + 1, depth_h)

        @pl.when(u == (depth_h - ahead) // 2)
        def _():
            await_or_zero(((halo, 0, has_top, down), (halo, 1, has_bot, up)))
            place(0, [halo[0]] + [cells[i * depth_h - 1] for i in range(1, n_i)])
            place(depth_h + 1, [cells[i * depth_h] for i in range(1, n_i)] + [halo[1]])
            at_row = lax.broadcasted_iota(jnp.int32, edge_x.shape[1:], 0)
            for side, col in ((0, 0), (1, tile_w - 1)):
                top = halo[0].astype(F32)[col : col + 1]
                bottom = halo[1].astype(F32)[col : col + 1]
                edge_x[side] = jnp.where(at_row == 0, top, bottom).astype(BF16)

            @pl.when(has_right)
            def _():
                rightward_x.start()

            @pl.when(has_left)
            def _():
                leftward_x.start()

        depth_slab(a)
        project_slab(u, a)

    def look_ahead(u):
        e = lax.rem(u + 1 + ahead, depth_h + 2)

        @pl.when(u == depth_h - ahead)
        def _():
            await_or_zero(((colin_x, 0, has_left, rightward_x), (colin_x, 1, has_right, leftward_x)))
            expand_columns(colin_x, tile_h)

        @pl.when(u < depth_h + 2 - ahead)
        def _():
            expand_slabs(e, 1)

            @pl.when((e == 0) | (e == depth_h + 1))
            def _():
                outside = jnp.where(
                    e == 0,
                    jnp.where(token_i == 0, 1 - ok_top, 0.0),
                    jnp.where(token_i == n_i - 1, 1 - ok_bot, 0.0),
                )
                exp[e, n_t : n_t + slab] = exp[e, n_t : n_t + slab] * (1 - outside)

            border_columns(e)

    lag = depth_h

    @pl.loop(0, lag + plan.batches)
    def _(t):
        @pl.when(t < depth_h)
        def _():
            bottleneck(t)

        @pl.when(t == lag)
        def _():
            await_weights()

        @pl.when((t > 0) & (t <= depth_h))
        def _():
            finish(t - 1)

        @pl.when(t < depth_h)
        def _():
            look_ahead(t)

        @pl.when(t >= lag)
        def _():
            attend_batch(t - lag)

    @pl.when(has_bot)
    def _():
        down.wait_send()

    @pl.when(has_top)
    def _():
        up.wait_send()

    @pl.when(has_right)
    def _():
        rightward.wait_send()
        rightward_x.wait_send()

    @pl.when(has_left)
    def _():
        leftward.wait_send()
        leftward_x.wait_send()

    for copy in weights:
        copy.wait_send()

    remote(psend, psend, p_s, p_r.at[0], partner).wait_send()
    sent = fsend.at[pl.ds(0, depth_h * plan.pairs - plan.batches)]
    remote(sent, sent, f_s, f_r.at[0], partner).wait_send()

    perm_t = one_hot(slab, slab, lambda row, column: cell_of(column) == row)

    @pl.loop(0, plan.batches)
    def _(m):
        others = oin.at[m, pl.ds(0, 2 * plan.sources - 1)]
        remote(others, others, o_s, o_r.at[m], partner).wait_recv()
        pieces = 2 * plan.pairs
        for ah in range(slabs):
            arrived = oin[m, ah * pieces : (ah + 1) * pieces].astype(F32)
            placed = dot(perm_t, arrived.reshape(slab, half).astype(BF16)).astype(BF16)
            a = lax.rem(m * slabs + ah + 1, depth_h)
            for i in range(n_i):
                row = i * depth_h + a
                result[row] = placed[i * tile_w : (i + 1) * tile_w]
                pltpu.make_async_copy(result.at[row], out.at[row], out_s).start()

    sent = osend.at[pl.ds(0, plan.batches * (2 * plan.sources - 1))]
    remote(sent, sent, o_s, o_r.at[0], partner).wait_send()
    pltpu.make_async_copy(result, out, out_s).wait()


def per_device(
    mesh_shape, cells, w_expand, b_expand, w_depth, b_depth, w_project, b_project, ln_gain,
    w_qkv, w_out, b_out,
):
    tile_h, tile_w, width = cells.shape
    plan = Plan(mesh_shape, tile_h, tile_w)
    inner = w_expand.shape[1]
    half = width // 2
    args = (
        cells, w_expand, b_expand[None], w_depth, b_depth[None],
        w_project, b_project[None], ln_gain[None], w_qkv.transpose(1, 0, 2), w_out, b_out[None],
    )
    dma = pltpu.SemaphoreType.DMA
    vmem = pltpu.VMEM
    n = plan
    rows_x = 16
    return pl.pallas_call(
        functools.partial(kernel, plan),
        out_shape=jax.ShapeDtypeStruct((tile_h, tile_w, half), BF16),
        in_specs=[
            pl.BlockSpec(memory_space=pl.ANY) for _ in args
        ],
        out_specs=pl.BlockSpec(memory_space=pl.ANY),
        scratch_shapes=[
            vmem((1, inner), F32), vmem(w_depth.shape, BF16), vmem((1, inner), F32),
            vmem((1, width), F32), vmem((1, width), F32),
            vmem(cells.shape, BF16), vmem((n.depth_h + 2, n.slab, width), BF16),
            vmem(w_expand.shape, BF16), vmem(w_project.shape, BF16),
            vmem((3, width, width), BF16), vmem((width, width), BF16), vmem((9, inner), F32),
            vmem((n.depth_h + 2, n.slab + 2 * n.n_t, inner), F32),
            vmem((2, tile_w, width), BF16),
            vmem((2, tile_h, width), BF16),
            vmem((2, tile_h, width), BF16),
            vmem((2, rows_x, width), BF16),
            vmem((2, rows_x, width), BF16),
            vmem((2, tile_h + rows_x, inner), F32),
            vmem((n.slab, inner), BF16),
            vmem((n.depth_h, n.part, width), BF16),
            vmem((n.depth_h, n.part, width), BF16),
            vmem((n.depth_h, n.part, width), F32),
            vmem((n.depth_h * n.pairs, n.piece, width), BF16),
            vmem((n.batches, n.sources, n.piece, width), BF16),
            vmem((1, inner), F32), vmem((1, inner), F32),
            vmem((width, width), BF16),
            vmem((2, 1, half), F32),
            vmem((n.batches * n.sources * 2, n.piece, half), BF16),
            vmem((n.batches, n.sources * 2, n.piece, half), BF16),
            vmem((tile_h, tile_w, half), BF16),
            dma, dma((11,)),
            dma((2,)), dma((2,)), dma((4,)), dma((4,)), dma((3,)), dma((3,)),
            dma, dma((n.depth_h,)), dma, dma((n.batches,)), dma, dma((n.batches,)),
        ],
        compiler_params=pltpu.CompilerParams(
            collective_id=0, has_side_effects=True, vmem_limit_bytes=60 << 20
        ),
    )(*args)


def solution(mesh):
    placed = (
        P(("grp", "gy"), "gx", None),
        P(None, "ch"),
        P("ch"),
        P(None, None, "ch"),
        P("ch"),
        P("ch", None),
        P(),
        P(),
        P(None, None, "ch"),
        P("ch", None),
        P("ch"),
    )
    return jax.shard_map(
        functools.partial(per_device, dict(mesh.shape)),
        mesh=mesh,
        in_specs=placed,
        out_specs=P(("grp", "gy"), "gx", "ch"),
        check_vma=False,
    )
```

```python
import functools

import jax
import jax.numpy as jnp
import numpy as np
from jax import lax
from jax.experimental import pallas as pl
from jax.experimental.pallas import tpu as pltpu
from jax.sharding import PartitionSpec as P

HEAD_DIM = 32
GRID = 8
WINDOWS = 2
MESH = pl.DeviceIdType.MESH
F32 = jnp.float32
BF16 = jnp.bfloat16


HALF_ROOT = np.float32(np.sqrt(0.5))


def gelu_scaled(t):
    return t * (HALF_ROOT + HALF_ROOT * lax.erf(t))


def dot(a, b):
    return jnp.dot(a, b, preferred_element_type=F32)


def dot_t(a, b):
    return lax.dot_general(a, b, (((1,), (1,)), ((), ())), preferred_element_type=F32)


def quotient(v, n):
    return v >> (n.bit_length() - 1) if n & (n - 1) == 0 else lax.div(v, n)


def remainder(v, n):
    return v & (n - 1) if n & (n - 1) == 0 else lax.rem(v, n)


def farthest_first(n):
    return sorted(range(1, n), key=lambda k: abs(2 * k - n))


class Plan:
    def __init__(self, mesh_shape, tile_h, tile_w):
        self.n_rows, self.n_cols = mesh_shape["gy"], mesh_shape["gx"]
        self.tile_h, self.tile_w = tile_h, tile_w
        stride_h = tile_h * self.n_rows // GRID
        stride_w = tile_w * self.n_cols // GRID
        self.depth_h, self.depth_w = min(tile_h, stride_h), min(tile_w, stride_w)
        self.steps_h, self.steps_w = stride_h // self.depth_h, stride_w // self.depth_w
        self.n_i, self.n_j = tile_h // self.depth_h, tile_w // self.depth_w
        self.ph, self.pw = GRID // self.n_i, GRID // self.n_j
        self.n_t = self.n_i * self.n_j
        self.sources = self.ph * self.pw
        half_w = self.depth_w // 2
        self.slab = self.depth_w * self.n_t
        self.part = self.slab // 2
        self.pairs = half_w // WINDOWS
        self.slabs = self.sources * WINDOWS // half_w
        self.batches = self.depth_h // self.slabs
        self.piece = WINDOWS * self.n_t
        assert self.pairs % self.pw == 0 and self.pairs // self.pw * self.slabs == self.ph
        assert self.depth_h % self.slabs == 0 and self.depth_h % 2 == 0 and self.depth_h >= 8


def kernel(
    plan, cells_h, w_exp_h, b_exp_h, w_dep_h, b_dep_h, w_proj_h, b_proj_h, gain_h, w_qkv_h, w_out_h,
    b_out_h, out,
    b_exp, w_dep_in, b_dep, b_proj, gain, cells, ordered, w_exp, w_proj, w_qkv, w_out, w_dep,
    exp, halo, edge, colin, edge_x, colin_x, colexp, dbuf, psend, precv, acc, fsend, frecv,
    b_exp_s, b_dep_s, w_vt, bo_full, osend, oin, result,
    out_s, in_s, halo_s, halo_r, col_s, col_r, w_s, w_r, p_s, p_r, f_s, f_r, o_s, o_r,
):
    tile_h, tile_w = plan.tile_h, plan.tile_w
    depth_h, n_i, n_j, n_t = plan.depth_h, plan.n_i, plan.n_j, plan.n_t
    width = cells.shape[2]
    inner = w_exp.shape[1]
    slab, part, pw, slabs = plan.slab, plan.part, plan.pw, plan.slabs
    half = width // 2
    z, x, c = lax.axis_index("gy"), lax.axis_index("gx"), lax.axis_index("ch")
    zs, xs = lax.rem(z, plan.steps_h), lax.rem(x, plan.steps_w)
    mp, mq = lax.div(z, plan.steps_h), lax.div(x, plan.steps_w)
    my_s = mp * pw + mq
    my_slab = lax.rem(mp, slabs)
    my_pair = lax.div(mp, slabs) * pw + mq
    last_z, last_x = plan.n_rows - 1, plan.n_cols - 1
    partner = {"ch": 1 - c}
    has_top, has_bot = z > 0, z < last_z
    has_left, has_right = x > 0, x < last_x

    def peer(s, core):
        p, q = lax.div(s, pw), lax.rem(s, pw)
        return {"gy": p * plan.steps_h + zs, "gx": q * plan.steps_w + xs, "ch": core}

    def owner(ah, pair):
        return (lax.div(pair, pw) * slabs + ah) * pw + lax.rem(pair, pw)

    def remote(src, dst, send, recv, device):
        return pltpu.make_async_remote_copy(
            src_ref=src, dst_ref=dst, send_sem=send, recv_sem=recv,
            device_id=device, device_id_type=MESH,
        )

    mine = pl.ds(pl.multiple_of(c * half, half), half)
    loads = [
        pltpu.make_async_copy(src, dst, in_s.at[n])
        for n, (src, dst) in enumerate((
            (cells_h, cells), (w_exp_h, w_exp), (w_proj_h, w_proj),
            (w_qkv_h, w_qkv.at[:, :, mine]), (w_out_h, w_out.at[mine]),
            (b_exp_h, b_exp), (w_dep_h, w_dep_in), (b_dep_h, b_dep), (b_proj_h, b_proj),
            (gain_h, gain), (b_out_h, bo_full.at[c]),
        ))
    ]
    small = loads[5:]
    for load in loads[:2] + small + loads[2:3]:
        load.start()

    barrier = pltpu.get_barrier_semaphore()
    around = (
        (has_top, {"gy": jnp.maximum(z - 1, 0)}),
        (has_bot, {"gy": jnp.minimum(z + 1, last_z)}),
        (has_left, {"gx": jnp.maximum(x - 1, 0)}),
        (has_right, {"gx": jnp.minimum(x + 1, last_x)}),
    )
    count = jnp.int32(2 * plan.sources - 1)
    for there, device in around:
        @pl.when(there)
        def _():
            pl.semaphore_signal(barrier, inc=1, device_id=device, device_id_type=MESH)
        count = count + there.astype(jnp.int32)

    @pl.loop(0, 2 * plan.sources)
    def _(t):
        s, core = lax.div(t, 2), lax.rem(t, 2)

        @pl.when(jnp.logical_not((s == my_s) & (core == c)))
        def _():
            pl.semaphore_signal(barrier, inc=1, device_id=peer(s, core), device_id_type=MESH)

    down = remote(cells_h.at[tile_h - 1], halo.at[0], halo_s.at[0], halo_r.at[0], around[1][1])
    up = remote(cells_h.at[0], halo.at[1], halo_s.at[1], halo_r.at[1], around[0][1])
    rightward = remote(edge.at[1], colin.at[0], col_s.at[0], col_r.at[0], around[3][1])
    leftward = remote(edge.at[0], colin.at[1], col_s.at[1], col_r.at[1], around[2][1])
    rightward_x = remote(edge_x.at[1], colin_x.at[0], col_s.at[2], col_r.at[2], around[3][1])
    leftward_x = remote(edge_x.at[0], colin_x.at[1], col_s.at[3], col_r.at[3], around[2][1])
    weights = (
        remote(w_qkv_h, w_qkv.at[:, :, mine], w_s.at[0], w_r.at[0], partner),
        remote(w_out_h, w_out.at[mine], w_s.at[1], w_r.at[1], partner),
        remote(b_out_h, bo_full.at[c], w_s.at[2], w_r.at[2], partner),
    )

    def one_hot(rows, columns, source):
        row = lax.broadcasted_iota(jnp.int32, (rows, columns), 0)
        column = lax.broadcasted_iota(jnp.int32, (rows, columns), 1)
        return source(row, column).astype(F32).astype(BF16)

    def cell_of(row):
        b, i, j = quotient(row, n_t), quotient(remainder(row, n_t), n_j), remainder(row, n_j)
        return i * tile_w + j * plan.depth_w + b

    perm = one_hot(slab, slab, lambda row, column: cell_of(row) == column)
    picks = [
        one_hot(tile_h, tile_h * 16, lambda row, column: row * 16 + at == column) for at in (0, 15)
    ]
    loads[0].wait()

    for side, first in ((0, 0), (1, tile_w - 16)):
        border = cells[:, first : first + 16, :].reshape(tile_h * 16, width)
        edge[side] = dot(picks[side], border).astype(BF16)

    def place(e, rows):
        ordered[e] = dot(perm, jnp.concatenate(rows, axis=0)).astype(BF16)

    def place_own(e):
        place(e, [cells[i * depth_h + e - 1] for i in range(n_i)])

    ahead = 4
    for e in range(1, ahead + 1):
        place_own(e)

    lanes_e = 256

    def expand(source, lanes):
        return gelu_scaled(dot(source, w_exp[:, lanes]) * HALF_ROOT + b_exp_s[:, lanes])

    def expand_slabs(e, count):
        source = ordered[pl.ds(e, count)].reshape(count * slab, width)
        for n in range(inner // lanes_e):
            lanes = slice(n * lanes_e, (n + 1) * lanes_e)
            value = expand(source, lanes)
            for k in range(count):
                exp[e + k, n_t : n_t + slab, lanes] = value[k * slab : (k + 1) * slab]

    ok_top, ok_bot = has_top.astype(F32), has_bot.astype(F32)
    ok_left, ok_right = has_left.astype(F32), has_right.astype(F32)

    def border_columns(e):
        at = lax.broadcasted_iota(jnp.int32, (n_t, inner), 0)
        left = exp[e, slab : slab + n_t, :]
        right = exp[e, n_t : 2 * n_t, :]
        if n_t > 1:
            left = pltpu.roll(left, 1, 0)
            right = pltpu.roll(right, n_t - 1, 0)
        for i in range(n_i):
            row = i * depth_h + e - 1
            above, below = row < 0, row >= tile_h
            ok = jnp.where(above, ok_top, jnp.where(below, ok_bot, jnp.float32(1)))
            row = jnp.where(above, tile_h, jnp.where(below, tile_h + 1, row))
            left = jnp.where(at == i * n_j, colexp[0, pl.ds(row, 1), :] * (ok_left * ok), left)
            right = jnp.where(
                at == i * n_j + n_j - 1, colexp[1, pl.ds(row, 1), :] * (ok_right * ok), right
            )
        exp[e, 0:n_t, :] = left
        exp[e, n_t + slab : 2 * n_t + slab, :] = right

    pl.semaphore_wait(barrier, count)

    @pl.when(has_right)
    def _():
        rightward.start()

    @pl.when(has_left)
    def _():
        leftward.start()

    @pl.when(has_bot)
    def _():
        down.start()

    @pl.when(has_top)
    def _():
        up.start()

    for copy in weights:
        copy.start()

    for load in small:
        load.wait()
    for di in range(3):
        w_dep[3 * di : 3 * di + 3] = w_dep_in[di].astype(F32) * HALF_ROOT
    b_exp_s[...] = b_exp[...] * HALF_ROOT
    b_dep_s[...] = b_dep[...] * HALF_ROOT
    loads[1].wait()
    loads[3].start()
    loads[4].start()
    expand_slabs(1, ahead)

    @pl.loop(ahead + 1, depth_h + 1)
    def _(e):
        place_own(e)

    def await_or_zero(pairs):
        for buffer, index, there, copy in pairs:
            @pl.when(there)
            def _():
                copy.wait_recv()

            @pl.when(jnp.logical_not(there))
            def _():
                buffer[index] = jnp.zeros(buffer.shape[1:], BF16)

    def expand_columns(source, first):
        rows = source.shape[1]
        flat = source[...].reshape(2 * rows, width)
        for n in range(inner // lanes_e):
            lanes = slice(n * lanes_e, (n + 1) * lanes_e)
            value = expand(flat, lanes)
            colexp[0, first : first + rows, lanes] = value[:rows]
            colexp[1, first : first + rows, lanes] = value[rows:]

    lanes_d = 128
    quarter = part // 2
    some = plan.pairs // 2

    def partial_copy(u):
        return remote(psend.at[u], precv.at[u], p_s, p_r.at[u], partner)

    def slabs_of(u):
        return [2 * lax.div(u, 2) + k for k in range(2)]

    def first_row(core, outer):
        return pl.multiple_of(jnp.where(core == 0, 1 - outer, 2 + outer) * quarter, quarter)

    def depth_unit(u):
        outer = lax.rem(u, 2)
        for chunk in range(inner // lanes_d):
            lanes = slice(chunk * lanes_d, (chunk + 1) * lanes_d)
            for n, at in enumerate(slabs_of(u)):
                a = lax.rem(at + 1, depth_h)
                for core in range(2):
                    window = pl.ds(first_row(core, outer), quarter + 2 * n_t)
                    total = None
                    for di in range(3):
                        rows = exp[a + di, window, lanes]
                        for dj in range(3):
                            k = 3 * di + dj
                            term = rows[dj * n_t : dj * n_t + quarter] * w_dep[k : k + 1, lanes]
                            total = term if total is None else total + term
                    value = gelu_scaled(total + b_dep_s[:, lanes]).astype(BF16)
                    first = pl.multiple_of(jnp.where(c == core, part, 0) + n * quarter, quarter)
                    dbuf[pl.ds(first, quarter), lanes] = value

    def project_unit(u):
        projected = dot(dbuf[...], w_proj[...])
        psend[u] = projected[:part].astype(BF16)
        partial_copy(u).start()
        own = jnp.concatenate([
            ordered[lax.rem(at + 1, depth_h) + 1, pl.ds(first_row(c, lax.rem(u, 2)), quarter)]
            for at in slabs_of(u)
        ], axis=0)
        acc[u] = projected[part:] + own.astype(F32) + b_proj[...]

    def forward_copy(u, pair):
        m, ah = lax.div(u, slabs), lax.rem(u, slabs)
        s = owner(ah, pair)
        return remote(
            fsend.at[u * plan.pairs + pair], frecv.at[m, my_s], f_s, f_r.at[m], peer(s, c)
        )

    def finish(u):
        partial_copy(u).wait_recv()
        mixed = (acc[u] + precv[u].astype(F32)).astype(BF16)
        base = jnp.where(c == lax.rem(u, 2), some, 0)
        for n, at in enumerate(slabs_of(u)):
            for k in range(some):
                rows = slice((n * some + k) * plan.piece, (n * some + k + 1) * plan.piece)
                fsend[at * plan.pairs + base + k] = mixed[rows]
        for k in range(some):
            for at in slabs_of(u):
                pair = base + k
                is_mine = (lax.rem(at, slabs) == my_slab) & (pair == my_pair)

                @pl.when(is_mine)
                def _():
                    frecv[lax.div(at, slabs), my_s] = fsend[at * plan.pairs + pair]

                @pl.when(jnp.logical_not(is_mine))
                def _():
                    forward_copy(at, pair).start()

    eye = (
        lax.broadcasted_iota(jnp.int32, (half, half), 0)
        == lax.broadcasted_iota(jnp.int32, (half, half), 1)
    ).astype(F32).astype(BF16)
    def await_weights():
        loads[3].wait()
        loads[4].wait()
        for copy in weights:
            copy.wait_recv()
        w_vt[:half] = dot_t(eye, w_qkv[2, :, :half]).astype(BF16)
        w_vt[half:] = dot_t(eye, w_qkv[2, :, half:]).astype(BF16)

    def await_batch(m):
        others = frecv.at[m, pl.ds(0, plan.sources - 1)]
        remote(others, others, f_s, f_r.at[m], partner).wait_recv()

    keys = plan.sources * n_t
    tokens = WINDOWS * keys
    group = 128
    n_h = group // HEAD_DIM
    lane = lax.broadcasted_iota(jnp.int32, (1, WINDOWS * 2 * group), 1)
    head_masks = [
        (remainder(quotient(lane, HEAD_DIM), n_h) == h).astype(F32).astype(BF16) for h in range(n_h)
    ]
    lane_w = lax.div(lax.broadcasted_iota(jnp.int32, (1, tokens), 1), keys)
    window_masks = [(lane_w == w).astype(F32).astype(BF16) for w in range(WINDOWS)]
    scale = np.float32(HEAD_DIM ** (-0.5) * np.log2(np.e))
    duos = width // (2 * group)
    eye_t = eye[:tokens, :tokens]

    def attend(normed):
        query = dot(normed, w_qkv[0])
        keyset = dot(normed, w_qkv[1])
        values = dot_t(w_vt[...], normed)
        query = (query * scale).astype(BF16)
        keyset = keyset.astype(BF16)
        values = values.astype(BF16)
        blank = jnp.zeros((keys, group), BF16)
        blocks = [(w, g) for w in range(WINDOWS) for g in range(2)]
        lefts, rights = [], []
        for duo in range(duos):
            rights.append(jnp.concatenate([
                jnp.concatenate([
                    query[w * keys : (w + 1) * keys, (2 * duo + g) * group : (2 * duo + g + 1) * group]
                    if block == (w, g) else blank
                    for block in blocks
                ], axis=1)
                for g in range(2) for w in range(WINDOWS)
            ], axis=0))
            left = jnp.concatenate([
                keyset[w * keys : (w + 1) * keys, 2 * duo * group : (2 * duo + 2) * group]
                for w in range(WINDOWS)
            ], axis=1)
            lefts.append(jnp.concatenate([left * mask for mask in head_masks], axis=0))
        scores = [dot_t(left, right) for left, right in zip(lefts, rights)]
        nothing = jnp.zeros((HEAD_DIM, tokens), BF16)
        stacked, spreads, shares = [], [], []
        for duo in range(duos):
            score = scores[duo].reshape(n_h, keys, 2 * tokens)
            top = jnp.max(score, axis=1, keepdims=True)
            power = jnp.exp2(score - top)
            share = 1.0 / jnp.sum(power, axis=1, keepdims=True)
            power = power.astype(BF16)
            for g in range(2):
                lanes = slice(g * tokens, (g + 1) * tokens)
                shares.append(share[:, :, lanes])
                spreads.append(jnp.concatenate(
                    [power[h, :, lanes] * mask for h in range(n_h) for mask in window_masks], axis=0
                ))
                first = (2 * duo + g) * group
                stacked.append(jnp.concatenate([
                    jnp.concatenate([
                        values[first + h * HEAD_DIM : first + (h + 1) * HEAD_DIM]
                        if h == at else nothing
                        for at in range(n_h)
                    ], axis=1)
                    for h in range(n_h)
                ], axis=0))
        found = [dot(a, b) for a, b in zip(stacked, spreads)]
        found = jnp.concatenate([
            (f.reshape(n_h, HEAD_DIM, tokens) * share).reshape(group, tokens).astype(BF16)
            for f, share in zip(found, shares)
        ], axis=0)
        return dot_t(eye_t, found).astype(BF16)

    def return_copy(m, s, side):
        return remote(
            osend.at[(m * plan.sources + s) * 2 + side], oin.at[m, (my_slab * 2 + c) * plan.pairs + my_pair],
            o_s, o_r.at[m], peer(s, side),
        )

    def attend_batch(m):
        await_batch(m)
        came = frecv[m].astype(F32)
        mixed = jnp.concatenate([
            came[:, w * n_t : (w + 1) * n_t].reshape(keys, width) for w in range(WINDOWS)
        ], axis=0)
        centered = mixed - jnp.mean(mixed, axis=-1, keepdims=True)
        spread = jnp.mean(centered * centered, axis=-1, keepdims=True)
        normed = (centered * lax.rsqrt(spread + 1e-05) * gain[...]).astype(BF16)
        total = mixed + dot(attend(normed), w_out[...])
        for side in range(2):
            lanes = slice(side * half, (side + 1) * half)
            value = total[:, lanes] + bo_full[side]
            value = jnp.concatenate([
                value[w * keys : (w + 1) * keys].reshape(plan.sources, n_t, half)
                for w in range(WINDOWS)
            ], axis=1)
            value = value.astype(BF16)
            for at in range(plan.sources):
                osend[(m * plan.sources + at) * 2 + side] = value[at]

        oin[m, (my_slab * 2 + c) * plan.pairs + my_pair] = osend[(m * plan.sources + my_s) * 2 + c]
        for k in farthest_first(plan.sources):
            for side in range(2):
                return_copy(m, lax.rem(my_s + k, plan.sources), side).start()
        return_copy(m, my_s, 1 - c).start()

    loads[2].wait()
    token_row = lax.broadcasted_iota(jnp.int32, (slab, 1), 0)
    token_i = remainder(quotient(token_row, n_j), n_i)

    def bottleneck(u):
        @pl.when(u == (depth_h - ahead) // 2)
        def _():
            await_or_zero(((halo, 0, has_top, down), (halo, 1, has_bot, up)))
            place(0, [halo[0]] + [cells[i * depth_h - 1] for i in range(1, n_i)])
            place(depth_h + 1, [cells[i * depth_h] for i in range(1, n_i)] + [halo[1]])
            at_row = lax.broadcasted_iota(jnp.int32, edge_x.shape[1:], 0)
            for side, col in ((0, 0), (1, tile_w - 1)):
                top = halo[0].astype(F32)[col : col + 1]
                bottom = halo[1].astype(F32)[col : col + 1]
                edge_x[side] = jnp.where(at_row == 0, top, bottom).astype(BF16)

            @pl.when(has_right)
            def _():
                rightward_x.start()

            @pl.when(has_left)
            def _():
                leftward_x.start()

        depth_unit(u)
        project_unit(u)

    def look_ahead(u):
        @pl.when(u == depth_h - ahead)
        def _():
            await_or_zero(((colin_x, 0, has_left, rightward_x), (colin_x, 1, has_right, leftward_x)))
            expand_columns(colin_x, tile_h)

        @pl.loop(0, 2)
        def _(k):
            e = lax.rem(u + 1 + ahead + k, depth_h + 2)
            expand_slabs(e, 1)

            @pl.when((e == 0) | (e == depth_h + 1))
            def _():
                outside = jnp.where(
                    e == 0,
                    jnp.where(token_i == 0, 1 - ok_top, 0.0),
                    jnp.where(token_i == n_i - 1, 1 - ok_bot, 0.0),
                )
                exp[e, n_t : n_t + slab] = exp[e, n_t : n_t + slab] * (1 - outside)

            @pl.when(u > 0)
            def _():
                border_columns(e)

    def first_columns():
        await_or_zero(((colin, 0, has_left, rightward), (colin, 1, has_right, leftward)))
        expand_columns(colin, 0)

        @pl.loop(1, ahead + 3)
        def _(e):
            border_columns(e)

    lag = depth_h

    @pl.loop(0, lag + plan.batches)
    def _(t):
        @pl.when(t < depth_h)
        def _():
            bottleneck(t)

        @pl.when(t == lag)
        def _():
            await_weights()

        @pl.when((t > 1) & (t <= depth_h))
        def _():
            finish(t - 1)

        @pl.when((lax.rem(t, 2) == 0) & (t < depth_h - 2))
        def _():
            look_ahead(t)

        @pl.when(t == 0)
        def _():
            finish(t)
            first_columns()

        @pl.when(t >= lag)
        def _():
            attend_batch(t - lag)

    @pl.when(has_bot)
    def _():
        down.wait_send()

    @pl.when(has_top)
    def _():
        up.wait_send()

    @pl.when(has_right)
    def _():
        rightward.wait_send()
        rightward_x.wait_send()

    @pl.when(has_left)
    def _():
        leftward.wait_send()
        leftward_x.wait_send()

    for copy in weights:
        copy.wait_send()

    remote(psend, psend, p_s, p_r.at[0], partner).wait_send()
    sent = fsend.at[pl.ds(0, depth_h * plan.pairs - plan.batches)]
    remote(sent, sent, f_s, f_r.at[0], partner).wait_send()

    perm_t = one_hot(slab, slab, lambda row, column: cell_of(column) == row)

    @pl.loop(0, plan.batches)
    def _(m):
        others = oin.at[m, pl.ds(0, 2 * plan.sources - 1)]
        remote(others, others, o_s, o_r.at[m], partner).wait_recv()
        pieces = 2 * plan.pairs
        for ah in range(slabs):
            arrived = oin[m, ah * pieces : (ah + 1) * pieces].astype(F32)
            placed = dot(perm_t, arrived.reshape(slab, half).astype(BF16)).astype(BF16)
            a = lax.rem(m * slabs + ah + 1, depth_h)
            for i in range(n_i):
                row = i * depth_h + a
                result[row] = placed[i * tile_w : (i + 1) * tile_w]
                pltpu.make_async_copy(result.at[row], out.at[row], out_s).start()

    sent = osend.at[pl.ds(0, plan.batches * (2 * plan.sources - 1))]
    remote(sent, sent, o_s, o_r.at[0], partner).wait_send()
    pltpu.make_async_copy(result, out, out_s).wait()


def per_device(
    mesh_shape, cells, w_expand, b_expand, w_depth, b_depth, w_project, b_project, ln_gain,
    w_qkv, w_out, b_out,
):
    tile_h, tile_w, width = cells.shape
    plan = Plan(mesh_shape, tile_h, tile_w)
    inner = w_expand.shape[1]
    half = width // 2
    args = (
        cells, w_expand, b_expand[None], w_depth, b_depth[None],
        w_project, b_project[None], ln_gain[None], w_qkv.transpose(1, 0, 2), w_out, b_out[None],
    )
    dma = pltpu.SemaphoreType.DMA
    vmem = pltpu.VMEM
    n = plan
    rows_x = 16
    return pl.pallas_call(
        functools.partial(kernel, plan),
        out_shape=jax.ShapeDtypeStruct((tile_h, tile_w, half), BF16),
        in_specs=[
            pl.BlockSpec(memory_space=pl.ANY) for _ in args
        ],
        out_specs=pl.BlockSpec(memory_space=pl.ANY),
        scratch_shapes=[
            vmem((1, inner), F32), vmem(w_depth.shape, BF16), vmem((1, inner), F32),
            vmem((1, width), F32), vmem((1, width), F32),
            vmem(cells.shape, BF16), vmem((n.depth_h + 2, n.slab, width), BF16),
            vmem(w_expand.shape, BF16), vmem(w_project.shape, BF16),
            vmem((3, width, width), BF16), vmem((width, width), BF16), vmem((9, inner), F32),
            vmem((n.depth_h + 2, n.slab + 2 * n.n_t, inner), F32),
            vmem((2, tile_w, width), BF16),
            vmem((2, tile_h, width), BF16),
            vmem((2, tile_h, width), BF16),
            vmem((2, rows_x, width), BF16),
            vmem((2, rows_x, width), BF16),
            vmem((2, tile_h + rows_x, inner), F32),
            vmem((n.slab, inner), BF16),
            vmem((n.depth_h, n.part, width), BF16),
            vmem((n.depth_h, n.part, width), BF16),
            vmem((n.depth_h, n.part, width), F32),
            vmem((n.depth_h * n.pairs, n.piece, width), BF16),
            vmem((n.batches, n.sources, n.piece, width), BF16),
            vmem((1, inner), F32), vmem((1, inner), F32),
            vmem((width, width), BF16),
            vmem((2, 1, half), F32),
            vmem((n.batches * n.sources * 2, n.piece, half), BF16),
            vmem((n.batches, n.sources * 2, n.piece, half), BF16),
            vmem((tile_h, tile_w, half), BF16),
            dma, dma((11,)),
            dma((2,)), dma((2,)), dma((4,)), dma((4,)), dma((3,)), dma((3,)),
            dma, dma((n.depth_h,)), dma, dma((n.batches,)), dma, dma((n.batches,)),
        ],
        compiler_params=pltpu.CompilerParams(
            collective_id=0, has_side_effects=True, vmem_limit_bytes=60 << 20
        ),
    )(*args)


def solution(mesh):
    placed = (
        P(("grp", "gy"), "gx", None),
        P(None, "ch"),
        P("ch"),
        P(None, None, "ch"),
        P("ch"),
        P("ch", None),
        P(),
        P(),
        P(None, None, "ch"),
        P("ch", None),
        P("ch"),
    )
    return jax.shard_map(
        functools.partial(per_device, dict(mesh.shape)),
        mesh=mesh,
        in_specs=placed,
        out_specs=P(("grp", "gy"), "gx", "ch"),
        check_vma=False,
    )
```

```python
import functools

import jax
import jax.numpy as jnp
import numpy as np
from jax import lax
from jax.experimental import pallas as pl
from jax.experimental.pallas import tpu as pltpu
from jax.sharding import PartitionSpec as P

HEAD_DIM = 32
GRID = 8
WINDOWS = 2
MESH = pl.DeviceIdType.MESH
F32 = jnp.float32
BF16 = jnp.bfloat16


HALF_ROOT = np.float32(np.sqrt(0.5))


def gelu_scaled(t):
    return t * (HALF_ROOT + HALF_ROOT * lax.erf(t))


def dot(a, b):
    return jnp.dot(a, b, preferred_element_type=F32)


def dot_t(a, b):
    return lax.dot_general(a, b, (((1,), (1,)), ((), ())), preferred_element_type=F32)


def quotient(v, n):
    return v >> (n.bit_length() - 1) if n & (n - 1) == 0 else lax.div(v, n)


def remainder(v, n):
    return v & (n - 1) if n & (n - 1) == 0 else lax.rem(v, n)


def farthest_first(n):
    return sorted(range(1, n), key=lambda k: abs(2 * k - n))


class Plan:
    def __init__(self, mesh_shape, tile_h, tile_w):
        self.n_rows, self.n_cols = mesh_shape["gy"], mesh_shape["gx"]
        self.tile_h, self.tile_w = tile_h, tile_w
        stride_h = tile_h * self.n_rows // GRID
        stride_w = tile_w * self.n_cols // GRID
        self.depth_h, self.depth_w = min(tile_h, stride_h), min(tile_w, stride_w)
        self.steps_h, self.steps_w = stride_h // self.depth_h, stride_w // self.depth_w
        self.n_i, self.n_j = tile_h // self.depth_h, tile_w // self.depth_w
        self.ph, self.pw = GRID // self.n_i, GRID // self.n_j
        self.n_t = self.n_i * self.n_j
        self.sources = self.ph * self.pw
        half_w = self.depth_w // 2
        self.slab = self.depth_w * self.n_t
        self.part = self.slab // 2
        self.pairs = half_w // WINDOWS
        self.slabs = self.sources * WINDOWS // half_w
        self.batches = self.depth_h // self.slabs
        self.piece = WINDOWS * self.n_t
        assert self.pairs % self.pw == 0 and self.pairs // self.pw * self.slabs == self.ph
        assert self.depth_h % self.slabs == 0 and self.depth_h % 2 == 0 and self.depth_h >= 8


def kernel(
    plan, cells_h, w_exp_h, b_exp_h, w_dep_h, b_dep_h, w_proj_h, b_proj_h, gain_h, w_qkv_h, w_out_h,
    b_out_h, out,
    b_exp, w_dep_in, b_dep, b_proj, gain, cells, ordered, w_exp, w_proj, w_qkv, w_out, w_dep,
    exp, halo, edge, colin, edge_x, colin_x, colexp, dbuf, psend, precv, acc, fsend, frecv,
    b_exp_s, b_dep_s, w_vt, bo_full, osend, oin, result,
    out_s, in_s, halo_s, halo_r, col_s, col_r, w_s, w_r, p_s, p_r, f_s, f_r, o_s, o_r,
):
    tile_h, tile_w = plan.tile_h, plan.tile_w
    depth_h, n_i, n_j, n_t = plan.depth_h, plan.n_i, plan.n_j, plan.n_t
    width = cells.shape[2]
    inner = w_exp.shape[1]
    slab, part, pw, slabs = plan.slab, plan.part, plan.pw, plan.slabs
    half = width // 2
    z, x, c = lax.axis_index("gy"), lax.axis_index("gx"), lax.axis_index("ch")
    zs, xs = lax.rem(z, plan.steps_h), lax.rem(x, plan.steps_w)
    mp, mq = lax.div(z, plan.steps_h), lax.div(x, plan.steps_w)
    my_s = mp * pw + mq
    my_slab = lax.rem(mp, slabs)
    my_pair = lax.div(mp, slabs) * pw + mq
    last_z, last_x = plan.n_rows - 1, plan.n_cols - 1
    partner = {"ch": 1 - c}
    has_top, has_bot = z > 0, z < last_z
    has_left, has_right = x > 0, x < last_x

    def peer(s, core):
        p, q = lax.div(s, pw), lax.rem(s, pw)
        return {"gy": p * plan.steps_h + zs, "gx": q * plan.steps_w + xs, "ch": core}

    def owner(ah, pair):
        return (lax.div(pair, pw) * slabs + ah) * pw + lax.rem(pair, pw)

    def remote(src, dst, send, recv, device):
        return pltpu.make_async_remote_copy(
            src_ref=src, dst_ref=dst, send_sem=send, recv_sem=recv,
            device_id=device, device_id_type=MESH,
        )

    mine = pl.ds(pl.multiple_of(c * half, half), half)
    loads = [
        pltpu.make_async_copy(src, dst, in_s.at[n])
        for n, (src, dst) in enumerate((
            (cells_h, cells), (w_exp_h, w_exp), (w_proj_h, w_proj),
            (w_qkv_h, w_qkv.at[:, :, mine]), (w_out_h, w_out.at[mine]),
            (b_exp_h, b_exp), (w_dep_h, w_dep_in), (b_dep_h, b_dep), (b_proj_h, b_proj),
            (gain_h, gain), (b_out_h, bo_full.at[c]),
        ))
    ]
    small = loads[5:]
    for load in loads[:2] + small + loads[2:3]:
        load.start()

    barrier = pltpu.get_barrier_semaphore()
    around = (
        (has_top, {"gy": jnp.maximum(z - 1, 0)}),
        (has_bot, {"gy": jnp.minimum(z + 1, last_z)}),
        (has_left, {"gx": jnp.maximum(x - 1, 0)}),
        (has_right, {"gx": jnp.minimum(x + 1, last_x)}),
    )
    count = jnp.int32(2 * plan.sources - 1)
    for there, device in around:
        @pl.when(there)
        def _():
            pl.semaphore_signal(barrier, inc=1, device_id=device, device_id_type=MESH)
        count = count + there.astype(jnp.int32)

    def greet(s, core):
        pl.semaphore_signal(barrier, inc=1, device_id=peer(s, core), device_id_type=MESH)

    greet(my_s, 1 - c)
    for k in farthest_first(plan.sources):
        for core in range(2):
            greet(lax.rem(my_s + k, plan.sources), core)

    down = remote(cells_h.at[tile_h - 1], halo.at[0], halo_s.at[0], halo_r.at[0], around[1][1])
    up = remote(cells_h.at[0], halo.at[1], halo_s.at[1], halo_r.at[1], around[0][1])
    rightward = remote(edge.at[1], colin.at[0], col_s.at[0], col_r.at[0], around[3][1])
    leftward = remote(edge.at[0], colin.at[1], col_s.at[1], col_r.at[1], around[2][1])
    rightward_x = remote(edge_x.at[1], colin_x.at[0], col_s.at[2], col_r.at[2], around[3][1])
    leftward_x = remote(edge_x.at[0], colin_x.at[1], col_s.at[3], col_r.at[3], around[2][1])
    weights = (
        remote(w_qkv_h, w_qkv.at[:, :, mine], w_s.at[0], w_r.at[0], partner),
        remote(w_out_h, w_out.at[mine], w_s.at[1], w_r.at[1], partner),
        remote(b_out_h, bo_full.at[c], w_s.at[2], w_r.at[2], partner),
    )

    def one_hot(rows, columns, source):
        row = lax.broadcasted_iota(jnp.int32, (rows, columns), 0)
        column = lax.broadcasted_iota(jnp.int32, (rows, columns), 1)
        return source(row, column).astype(F32).astype(BF16)

    def cell_of(row):
        b, i, j = quotient(row, n_t), quotient(remainder(row, n_t), n_j), remainder(row, n_j)
        return i * tile_w + j * plan.depth_w + b

    perm = one_hot(slab, slab, lambda row, column: cell_of(row) == column)
    picks = [
        one_hot(tile_h, tile_h * 16, lambda row, column: row * 16 + at == column) for at in (0, 15)
    ]
    loads[0].wait()

    for side, first in ((0, 0), (1, tile_w - 16)):
        border = cells[:, first : first + 16, :].reshape(tile_h * 16, width)
        edge[side] = dot(picks[side], border).astype(BF16)

    def place(e, rows):
        ordered[e] = dot(perm, jnp.concatenate(rows, axis=0)).astype(BF16)

    def place_own(e):
        place(e, [cells[i * depth_h + e - 1] for i in range(n_i)])

    ahead = 4
    for e in range(1, ahead + 1):
        place_own(e)

    lanes_e = 256

    def expand(source, lanes):
        return gelu_scaled(dot(source, w_exp[:, lanes]) * HALF_ROOT + b_exp_s[:, lanes])

    def expand_slabs(e, count):
        source = ordered[pl.ds(e, count)].reshape(count * slab, width)
        for n in range(inner // lanes_e):
            lanes = slice(n * lanes_e, (n + 1) * lanes_e)
            value = expand(source, lanes)
            for k in range(count):
                exp[e + k, n_t : n_t + slab, lanes] = value[k * slab : (k + 1) * slab]

    ok_top, ok_bot = has_top.astype(F32), has_bot.astype(F32)
    ok_left, ok_right = has_left.astype(F32), has_right.astype(F32)

    def border_columns(e):
        at = lax.broadcasted_iota(jnp.int32, (n_t, inner), 0)
        left = exp[e, slab : slab + n_t, :]
        right = exp[e, n_t : 2 * n_t, :]
        if n_t > 1:
            left = pltpu.roll(left, 1, 0)
            right = pltpu.roll(right, n_t - 1, 0)
        for i in range(n_i):
            row = i * depth_h + e - 1
            above, below = row < 0, row >= tile_h
            ok = jnp.where(above, ok_top, jnp.where(below, ok_bot, jnp.float32(1)))
            row = jnp.where(above, tile_h, jnp.where(below, tile_h + 1, row))
            left = jnp.where(at == i * n_j, colexp[0, pl.ds(row, 1), :] * (ok_left * ok), left)
            right = jnp.where(
                at == i * n_j + n_j - 1, colexp[1, pl.ds(row, 1), :] * (ok_right * ok), right
            )
        exp[e, 0:n_t, :] = left
        exp[e, n_t + slab : 2 * n_t + slab, :] = right

    pl.semaphore_wait(barrier, count)

    @pl.when(has_right)
    def _():
        rightward.start()

    @pl.when(has_left)
    def _():
        leftward.start()

    @pl.when(has_bot)
    def _():
        down.start()

    @pl.when(has_top)
    def _():
        up.start()

    for copy in weights:
        copy.start()

    for load in small:
        load.wait()
    for di in range(3):
        w_dep[3 * di : 3 * di + 3] = w_dep_in[di].astype(F32) * HALF_ROOT
    b_exp_s[...] = b_exp[...] * HALF_ROOT
    b_dep_s[...] = b_dep[...] * HALF_ROOT
    loads[1].wait()
    loads[3].start()
    loads[4].start()
    expand_slabs(1, ahead)

    @pl.loop(ahead + 1, depth_h + 1)
    def _(e):
        place_own(e)

    def await_or_zero(pairs):
        for buffer, index, there, copy in pairs:
            @pl.when(there)
            def _():
                copy.wait_recv()

            @pl.when(jnp.logical_not(there))
            def _():
                buffer[index] = jnp.zeros(buffer.shape[1:], BF16)

    def expand_columns(source, first):
        rows = source.shape[1]
        flat = source[...].reshape(2 * rows, width)
        for n in range(inner // lanes_e):
            lanes = slice(n * lanes_e, (n + 1) * lanes_e)
            value = expand(flat, lanes)
            colexp[0, first : first + rows, lanes] = value[:rows]
            colexp[1, first : first + rows, lanes] = value[rows:]

    lanes_d = 128
    quarter = part // 2
    some = plan.pairs // 2

    def partial_copy(u):
        return remote(psend.at[u], precv.at[u], p_s, p_r.at[u], partner)

    def slabs_of(u):
        return [2 * lax.div(u, 2) + k for k in range(2)]

    def first_row(core, outer):
        return pl.multiple_of(jnp.where(core == 0, 1 - outer, 2 + outer) * quarter, quarter)

    def depth_unit(u):
        outer = lax.rem(u, 2)
        for chunk in range(inner // lanes_d):
            lanes = slice(chunk * lanes_d, (chunk + 1) * lanes_d)
            for n, at in enumerate(slabs_of(u)):
                a = lax.rem(at + 1, depth_h)
                for core in range(2):
                    window = pl.ds(first_row(core, outer), quarter + 2 * n_t)
                    total = None
                    for di in range(3):
                        rows = exp[a + di, window, lanes]
                        for dj in range(3):
                            k = 3 * di + dj
                            term = rows[dj * n_t : dj * n_t + quarter] * w_dep[k : k + 1, lanes]
                            total = term if total is None else total + term
                    value = gelu_scaled(total + b_dep_s[:, lanes]).astype(BF16)
                    first = pl.multiple_of(jnp.where(c == core, part, 0) + n * quarter, quarter)
                    dbuf[pl.ds(first, quarter), lanes] = value

    def project_unit(u):
        projected = dot(dbuf[...], w_proj[...])
        psend[u] = projected[:part].astype(BF16)
        partial_copy(u).start()
        own = jnp.concatenate([
            ordered[lax.rem(at + 1, depth_h) + 1, pl.ds(first_row(c, lax.rem(u, 2)), quarter)]
            for at in slabs_of(u)
        ], axis=0)
        acc[u] = projected[part:] + own.astype(F32) + b_proj[...]

    def forward_copy(u, pair):
        m, ah = lax.div(u, slabs), lax.rem(u, slabs)
        s = owner(ah, pair)
        return remote(
            fsend.at[u * plan.pairs + pair], frecv.at[m, my_s], f_s, f_r.at[m], peer(s, c)
        )

    def finish(u):
        partial_copy(u).wait_recv()
        mixed = (acc[u] + precv[u].astype(F32)).astype(BF16)
        base = jnp.where(c == lax.rem(u, 2), some, 0)
        for n, at in enumerate(slabs_of(u)):
            for k in range(some):
                rows = slice((n * some + k) * plan.piece, (n * some + k + 1) * plan.piece)
                fsend[at * plan.pairs + base + k] = mixed[rows]
        for k in range(some):
            for at in slabs_of(u):
                pair = base + k
                is_mine = (lax.rem(at, slabs) == my_slab) & (pair == my_pair)

                @pl.when(is_mine)
                def _():
                    frecv[lax.div(at, slabs), my_s] = fsend[at * plan.pairs + pair]

                @pl.when(jnp.logical_not(is_mine))
                def _():
                    forward_copy(at, pair).start()

    eye = (
        lax.broadcasted_iota(jnp.int32, (half, half), 0)
        == lax.broadcasted_iota(jnp.int32, (half, half), 1)
    ).astype(F32).astype(BF16)
    def await_weights():
        loads[3].wait()
        loads[4].wait()
        for copy in weights:
            copy.wait_recv()
        w_vt[:half] = dot_t(eye, w_qkv[2, :, :half]).astype(BF16)
        w_vt[half:] = dot_t(eye, w_qkv[2, :, half:]).astype(BF16)

    def await_batch(m):
        others = frecv.at[m, pl.ds(0, plan.sources - 1)]
        remote(others, others, f_s, f_r.at[m], partner).wait_recv()

    keys = plan.sources * n_t
    tokens = WINDOWS * keys
    group = 128
    n_h = group // HEAD_DIM
    lane = lax.broadcasted_iota(jnp.int32, (1, WINDOWS * 2 * group), 1)
    head_masks = [
        (remainder(quotient(lane, HEAD_DIM), n_h) == h).astype(F32).astype(BF16) for h in range(n_h)
    ]
    lane_w = lax.div(lax.broadcasted_iota(jnp.int32, (1, tokens), 1), keys)
    window_masks = [(lane_w == w).astype(F32).astype(BF16) for w in range(WINDOWS)]
    scale = np.float32(HEAD_DIM ** (-0.5) * np.log2(np.e))
    duos = width // (2 * group)
    eye_t = eye[:tokens, :tokens]

    def attend(normed):
        query = dot(normed, w_qkv[0])
        keyset = dot(normed, w_qkv[1])
        values = dot_t(w_vt[...], normed)
        query = (query * scale).astype(BF16)
        keyset = keyset.astype(BF16)
        values = values.astype(BF16)
        blank = jnp.zeros((keys, group), BF16)
        blocks = [(w, g) for w in range(WINDOWS) for g in range(2)]
        lefts, rights = [], []
        for duo in range(duos):
            rights.append(jnp.concatenate([
                jnp.concatenate([
                    query[w * keys : (w + 1) * keys, (2 * duo + g) * group : (2 * duo + g + 1) * group]
                    if block == (w, g) else blank
                    for block in blocks
                ], axis=1)
                for g in range(2) for w in range(WINDOWS)
            ], axis=0))
            left = jnp.concatenate([
                keyset[w * keys : (w + 1) * keys, 2 * duo * group : (2 * duo + 2) * group]
                for w in range(WINDOWS)
            ], axis=1)
            lefts.append(jnp.concatenate([left * mask for mask in head_masks], axis=0))
        scores = [dot_t(left, right) for left, right in zip(lefts, rights)]
        nothing = jnp.zeros((HEAD_DIM, tokens), BF16)
        stacked, spreads, shares = [], [], []
        for duo in range(duos):
            score = scores[duo].reshape(n_h, keys, 2 * tokens)
            top = jnp.max(score, axis=1, keepdims=True)
            power = jnp.exp2(score - top)
            share = 1.0 / jnp.sum(power, axis=1, keepdims=True)
            power = power.astype(BF16)
            for g in range(2):
                lanes = slice(g * tokens, (g + 1) * tokens)
                shares.append(share[:, :, lanes])
                spreads.append(jnp.concatenate(
                    [power[h, :, lanes] * mask for h in range(n_h) for mask in window_masks], axis=0
                ))
                first = (2 * duo + g) * group
                stacked.append(jnp.concatenate([
                    jnp.concatenate([
                        values[first + h * HEAD_DIM : first + (h + 1) * HEAD_DIM]
                        if h == at else nothing
                        for at in range(n_h)
                    ], axis=1)
                    for h in range(n_h)
                ], axis=0))
        found = [dot(a, b) for a, b in zip(stacked, spreads)]
        found = jnp.concatenate([
            (f.reshape(n_h, HEAD_DIM, tokens) * share).reshape(group, tokens).astype(BF16)
            for f, share in zip(found, shares)
        ], axis=0)
        return dot_t(eye_t, found).astype(BF16)

    def return_copy(m, s, side):
        return remote(
            osend.at[(m * plan.sources + s) * 2 + side], oin.at[m, (my_slab * 2 + c) * plan.pairs + my_pair],
            o_s, o_r.at[m], peer(s, side),
        )

    def attend_batch(m):
        await_batch(m)
        came = frecv[m].astype(F32)
        mixed = jnp.concatenate([
            came[:, w * n_t : (w + 1) * n_t].reshape(keys, width) for w in range(WINDOWS)
        ], axis=0)
        centered = mixed - jnp.mean(mixed, axis=-1, keepdims=True)
        spread = jnp.mean(centered * centered, axis=-1, keepdims=True)
        normed = (centered * lax.rsqrt(spread + 1e-05) * gain[...]).astype(BF16)
        total = mixed + dot(attend(normed), w_out[...])
        for side in range(2):
            lanes = slice(side * half, (side + 1) * half)
            value = total[:, lanes] + bo_full[side]
            value = jnp.concatenate([
                value[w * keys : (w + 1) * keys].reshape(plan.sources, n_t, half)
                for w in range(WINDOWS)
            ], axis=1)
            value = value.astype(BF16)
            for at in range(plan.sources):
                osend[(m * plan.sources + at) * 2 + side] = value[at]

        oin[m, (my_slab * 2 + c) * plan.pairs + my_pair] = osend[(m * plan.sources + my_s) * 2 + c]
        for k in farthest_first(plan.sources):
            for side in range(2):
                return_copy(m, lax.rem(my_s + k, plan.sources), side).start()
        return_copy(m, my_s, 1 - c).start()

    loads[2].wait()
    token_row = lax.broadcasted_iota(jnp.int32, (slab, 1), 0)
    token_i = remainder(quotient(token_row, n_j), n_i)

    def bottleneck(u):
        @pl.when(u == (depth_h - ahead) // 2)
        def _():
            await_or_zero(((halo, 0, has_top, down), (halo, 1, has_bot, up)))
            place(0, [halo[0]] + [cells[i * depth_h - 1] for i in range(1, n_i)])
            place(depth_h + 1, [cells[i * depth_h] for i in range(1, n_i)] + [halo[1]])
            at_row = lax.broadcasted_iota(jnp.int32, edge_x.shape[1:], 0)
            for side, col in ((0, 0), (1, tile_w - 1)):
                top = halo[0].astype(F32)[col : col + 1]
                bottom = halo[1].astype(F32)[col : col + 1]
                edge_x[side] = jnp.where(at_row == 0, top, bottom).astype(BF16)

            @pl.when(has_right)
            def _():
                rightward_x.start()

            @pl.when(has_left)
            def _():
                leftward_x.start()

        depth_unit(u)
        project_unit(u)

    def look_ahead(u):
        @pl.when(u == depth_h - ahead)
        def _():
            await_or_zero(((colin_x, 0, has_left, rightward_x), (colin_x, 1, has_right, leftward_x)))
            expand_columns(colin_x, tile_h)

        @pl.when(u < depth_h - ahead)
        def _():
            expand_slabs(u + 1 + ahead, 2)

        @pl.when(u == depth_h - ahead)
        def _():
            for e in (0, depth_h + 1):
                expand_slabs(e, 1)

        @pl.loop(0, 2)
        def _(k):
            e = lax.rem(u + 1 + ahead + k, depth_h + 2)

            @pl.when((e == 0) | (e == depth_h + 1))
            def _():
                outside = jnp.where(
                    e == 0,
                    jnp.where(token_i == 0, 1 - ok_top, 0.0),
                    jnp.where(token_i == n_i - 1, 1 - ok_bot, 0.0),
                )
                exp[e, n_t : n_t + slab] = exp[e, n_t : n_t + slab] * (1 - outside)

            @pl.when(u > 0)
            def _():
                border_columns(e)

    def first_columns():
        await_or_zero(((colin, 0, has_left, rightward), (colin, 1, has_right, leftward)))
        expand_columns(colin, 0)

        @pl.loop(1, ahead + 3)
        def _(e):
            border_columns(e)

    lag = depth_h

    @pl.loop(0, lag + plan.batches)
    def _(t):
        @pl.when(t < depth_h)
        def _():
            bottleneck(t)

        @pl.when(t == lag)
        def _():
            await_weights()

        @pl.when((t > 1) & (t <= depth_h))
        def _():
            finish(t - 1)

        @pl.when((lax.rem(t, 2) == 0) & (t < depth_h - 2))
        def _():
            look_ahead(t)

        @pl.when(t == 0)
        def _():
            finish(t)
            first_columns()

        @pl.when(t >= lag)
        def _():
            attend_batch(t - lag)

    @pl.when(has_bot)
    def _():
        down.wait_send()

    @pl.when(has_top)
    def _():
        up.wait_send()

    @pl.when(has_right)
    def _():
        rightward.wait_send()
        rightward_x.wait_send()

    @pl.when(has_left)
    def _():
        leftward.wait_send()
        leftward_x.wait_send()

    for copy in weights:
        copy.wait_send()

    remote(psend, psend, p_s, p_r.at[0], partner).wait_send()
    sent = fsend.at[pl.ds(0, depth_h * plan.pairs - plan.batches)]
    remote(sent, sent, f_s, f_r.at[0], partner).wait_send()

    perm_t = one_hot(slab, slab, lambda row, column: cell_of(column) == row)

    @pl.loop(0, plan.batches)
    def _(m):
        others = oin.at[m, pl.ds(0, 2 * plan.sources - 1)]
        remote(others, others, o_s, o_r.at[m], partner).wait_recv()
        pieces = 2 * plan.pairs
        for ah in range(slabs):
            arrived = oin[m, ah * pieces : (ah + 1) * pieces].astype(F32)
            placed = dot(perm_t, arrived.reshape(slab, half).astype(BF16)).astype(BF16)
            a = lax.rem(m * slabs + ah + 1, depth_h)
            for i in range(n_i):
                row = i * depth_h + a
                result[row] = placed[i * tile_w : (i + 1) * tile_w]
                pltpu.make_async_copy(result.at[row], out.at[row], out_s).start()

    sent = osend.at[pl.ds(0, plan.batches * (2 * plan.sources - 1))]
    remote(sent, sent, o_s, o_r.at[0], partner).wait_send()
    pltpu.make_async_copy(result, out, out_s).wait()


def per_device(
    mesh_shape, cells, w_expand, b_expand, w_depth, b_depth, w_project, b_project, ln_gain,
    w_qkv, w_out, b_out,
):
    tile_h, tile_w, width = cells.shape
    plan = Plan(mesh_shape, tile_h, tile_w)
    inner = w_expand.shape[1]
    half = width // 2
    args = (
        cells, w_expand, b_expand[None], w_depth, b_depth[None],
        w_project, b_project[None], ln_gain[None], w_qkv.transpose(1, 0, 2), w_out, b_out[None],
    )
    dma = pltpu.SemaphoreType.DMA
    vmem = pltpu.VMEM
    n = plan
    rows_x = 16
    return pl.pallas_call(
        functools.partial(kernel, plan),
        out_shape=jax.ShapeDtypeStruct((tile_h, tile_w, half), BF16),
        in_specs=[
            pl.BlockSpec(memory_space=pl.ANY) for _ in args
        ],
        out_specs=pl.BlockSpec(memory_space=pl.ANY),
        scratch_shapes=[
            vmem((1, inner), F32), vmem(w_depth.shape, BF16), vmem((1, inner), F32),
            vmem((1, width), F32), vmem((1, width), F32),
            vmem(cells.shape, BF16), vmem((n.depth_h + 2, n.slab, width), BF16),
            vmem(w_expand.shape, BF16), vmem(w_project.shape, BF16),
            vmem((3, width, width), BF16), vmem((width, width), BF16), vmem((9, inner), F32),
            vmem((n.depth_h + 2, n.slab + 2 * n.n_t, inner), F32),
            vmem((2, tile_w, width), BF16),
            vmem((2, tile_h, width), BF16),
            vmem((2, tile_h, width), BF16),
            vmem((2, rows_x, width), BF16),
            vmem((2, rows_x, width), BF16),
            vmem((2, tile_h + rows_x, inner), F32),
            vmem((n.slab, inner), BF16),
            vmem((n.depth_h, n.part, width), BF16),
            vmem((n.depth_h, n.part, width), BF16),
            vmem((n.depth_h, n.part, width), F32),
            vmem((n.depth_h * n.pairs, n.piece, width), BF16),
            vmem((n.batches, n.sources, n.piece, width), BF16),
            vmem((1, inner), F32), vmem((1, inner), F32),
            vmem((width, width), BF16),
            vmem((2, 1, half), F32),
            vmem((n.batches * n.sources * 2, n.piece, half), BF16),
            vmem((n.batches, n.sources * 2, n.piece, half), BF16),
            vmem((tile_h, tile_w, half), BF16),
            dma, dma((11,)),
            dma((2,)), dma((2,)), dma((4,)), dma((4,)), dma((3,)), dma((3,)),
            dma, dma((n.depth_h,)), dma, dma((n.batches,)), dma, dma((n.batches,)),
        ],
        compiler_params=pltpu.CompilerParams(
            collective_id=0, has_side_effects=True, vmem_limit_bytes=60 << 20
        ),
    )(*args)


def solution(mesh):
    placed = (
        P(("grp", "gy"), "gx", None),
        P(None, "ch"),
        P("ch"),
        P(None, None, "ch"),
        P("ch"),
        P("ch", None),
        P(),
        P(),
        P(None, None, "ch"),
        P("ch", None),
        P("ch"),
    )
    return jax.shard_map(
        functools.partial(per_device, dict(mesh.shape)),
        mesh=mesh,
        in_specs=placed,
        out_specs=P(("grp", "gy"), "gx", "ch"),
        check_vma=False,
    )
```

```python
import functools

import jax
import jax.numpy as jnp
import numpy as np
from jax import lax
from jax.experimental import pallas as pl
from jax.experimental.pallas import tpu as pltpu
from jax.sharding import PartitionSpec as P

HEAD_DIM = 32
GRID = 8
WINDOWS = 2
MESH = pl.DeviceIdType.MESH
F32 = jnp.float32
BF16 = jnp.bfloat16


HALF_ROOT = np.float32(np.sqrt(0.5))


def gelu_scaled(t):
    return t * (HALF_ROOT + HALF_ROOT * lax.erf(t))


def dot(a, b):
    return jnp.dot(a, b, preferred_element_type=F32)


def dot_t(a, b):
    return lax.dot_general(a, b, (((1,), (1,)), ((), ())), preferred_element_type=F32)


def quotient(v, n):
    return v >> (n.bit_length() - 1) if n & (n - 1) == 0 else lax.div(v, n)


def remainder(v, n):
    return v & (n - 1) if n & (n - 1) == 0 else lax.rem(v, n)


def farthest_first(n):
    return sorted(range(1, n), key=lambda k: abs(2 * k - n))


class Plan:
    def __init__(self, mesh_shape, tile_h, tile_w):
        self.n_rows, self.n_cols = mesh_shape["gy"], mesh_shape["gx"]
        self.tile_h, self.tile_w = tile_h, tile_w
        stride_h = tile_h * self.n_rows // GRID
        stride_w = tile_w * self.n_cols // GRID
        self.depth_h, self.depth_w = min(tile_h, stride_h), min(tile_w, stride_w)
        self.steps_h, self.steps_w = stride_h // self.depth_h, stride_w // self.depth_w
        self.n_i, self.n_j = tile_h // self.depth_h, tile_w // self.depth_w
        self.ph, self.pw = GRID // self.n_i, GRID // self.n_j
        self.n_t = self.n_i * self.n_j
        self.sources = self.ph * self.pw
        half_w = self.depth_w // 2
        self.slab = self.depth_w * self.n_t
        self.part = self.slab // 2
        self.pairs = half_w // WINDOWS
        self.slabs = self.sources * WINDOWS // half_w
        self.batches = self.depth_h // self.slabs
        self.piece = WINDOWS * self.n_t
        assert self.pairs % self.pw == 0 and self.pairs // self.pw * self.slabs == self.ph
        assert self.depth_h % self.slabs == 0 and self.depth_h % 2 == 0 and self.depth_h >= 8


def kernel(
    plan, cells_h, w_exp_h, b_exp_h, w_dep_h, b_dep_h, w_proj_h, b_proj_h, gain_h, w_qkv_h, w_out_h,
    b_out_h, out,
    b_exp, w_dep_in, b_dep, b_proj, gain, cells, ordered, w_exp, w_proj, w_qkv, w_out, w_dep,
    exp, halo, edge, colin, edge_x, colin_x, colexp, dbuf, psend, precv, acc, fsend, frecv,
    b_exp_s, b_dep_s, w_vt, bo_full, osend, oin, result,
    out_s, in_s, halo_s, halo_r, col_s, col_r, w_s, w_r, p_s, p_r, f_s, f_r, o_s, o_r,
):
    tile_h, tile_w = plan.tile_h, plan.tile_w
    depth_h, n_i, n_j, n_t = plan.depth_h, plan.n_i, plan.n_j, plan.n_t
    width = cells.shape[2]
    inner = w_exp.shape[1]
    slab, part, pw, slabs = plan.slab, plan.part, plan.pw, plan.slabs
    half = width // 2
    z, x, c = lax.axis_index("gy"), lax.axis_index("gx"), lax.axis_index("ch")
    zs, xs = lax.rem(z, plan.steps_h), lax.rem(x, plan.steps_w)
    mp, mq = lax.div(z, plan.steps_h), lax.div(x, plan.steps_w)
    my_s = mp * pw + mq
    my_slab = lax.rem(mp, slabs)
    my_pair = lax.div(mp, slabs) * pw + mq
    last_z, last_x = plan.n_rows - 1, plan.n_cols - 1
    partner = {"ch": 1 - c}
    has_top, has_bot = z > 0, z < last_z
    has_left, has_right = x > 0, x < last_x

    def peer(s, core):
        p, q = lax.div(s, pw), lax.rem(s, pw)
        return {"gy": p * plan.steps_h + zs, "gx": q * plan.steps_w + xs, "ch": core}

    def owner(ah, pair):
        return (lax.div(pair, pw) * slabs + ah) * pw + lax.rem(pair, pw)

    def remote(src, dst, send, recv, device):
        return pltpu.make_async_remote_copy(
            src_ref=src, dst_ref=dst, send_sem=send, recv_sem=recv,
            device_id=device, device_id_type=MESH,
        )

    mine = pl.ds(pl.multiple_of(c * half, half), half)
    loads = [
        pltpu.make_async_copy(src, dst, in_s.at[n])
        for n, (src, dst) in enumerate((
            (cells_h, cells), (w_exp_h, w_exp), (w_proj_h, w_proj),
            (w_qkv_h, w_qkv.at[:, :, mine]), (w_out_h, w_out.at[mine]),
            (b_exp_h, b_exp), (w_dep_h, w_dep_in), (b_dep_h, b_dep), (b_proj_h, b_proj),
            (gain_h, gain), (b_out_h, bo_full.at[c]),
        ))
    ]
    small = loads[5:]
    for load in loads[:2] + small + loads[2:3]:
        load.start()

    barrier = pltpu.get_barrier_semaphore()
    around = (
        (has_top, {"gy": jnp.maximum(z - 1, 0)}),
        (has_bot, {"gy": jnp.minimum(z + 1, last_z)}),
        (has_left, {"gx": jnp.maximum(x - 1, 0)}),
        (has_right, {"gx": jnp.minimum(x + 1, last_x)}),
    )
    count = jnp.int32(2 * plan.sources - 1)
    for there, device in around:
        @pl.when(there)
        def _():
            pl.semaphore_signal(barrier, inc=1, device_id=device, device_id_type=MESH)
        count = count + there.astype(jnp.int32)

    def greet(s, core):
        pl.semaphore_signal(barrier, inc=1, device_id=peer(s, core), device_id_type=MESH)

    greet(my_s, 1 - c)
    for k in farthest_first(plan.sources):
        for core in range(2):
            greet(lax.rem(my_s + k, plan.sources), core)

    down = remote(cells_h.at[tile_h - 1], halo.at[0], halo_s.at[0], halo_r.at[0], around[1][1])
    up = remote(cells_h.at[0], halo.at[1], halo_s.at[1], halo_r.at[1], around[0][1])
    rightward = remote(edge.at[1], colin.at[0], col_s.at[0], col_r.at[0], around[3][1])
    leftward = remote(edge.at[0], colin.at[1], col_s.at[1], col_r.at[1], around[2][1])
    rightward_x = remote(edge_x.at[1], colin_x.at[0], col_s.at[2], col_r.at[2], around[3][1])
    leftward_x = remote(edge_x.at[0], colin_x.at[1], col_s.at[3], col_r.at[3], around[2][1])
    weights = (
        remote(w_qkv_h, w_qkv.at[:, :, mine], w_s.at[0], w_r.at[0], partner),
        remote(w_out_h, w_out.at[mine], w_s.at[1], w_r.at[1], partner),
        remote(b_out_h, bo_full.at[c], w_s.at[2], w_r.at[2], partner),
    )

    def one_hot(rows, columns, source):
        row = lax.broadcasted_iota(jnp.int32, (rows, columns), 0)
        column = lax.broadcasted_iota(jnp.int32, (rows, columns), 1)
        return source(row, column).astype(F32).astype(BF16)

    def cell_of(row):
        b, i, j = quotient(row, n_t), quotient(remainder(row, n_t), n_j), remainder(row, n_j)
        return i * tile_w + j * plan.depth_w + b

    perm = one_hot(slab, slab, lambda row, column: cell_of(row) == column)
    picks = [
        one_hot(tile_h, tile_h * 16, lambda row, column: row * 16 + at == column) for at in (0, 15)
    ]
    loads[0].wait()

    for side, first in ((0, 0), (1, tile_w - 16)):
        border = cells[:, first : first + 16, :].reshape(tile_h * 16, width)
        edge[side] = dot(picks[side], border).astype(BF16)

    def place(e, rows):
        ordered[e] = dot(perm, jnp.concatenate(rows, axis=0)).astype(BF16)

    def place_own(e):
        place(e, [cells[i * depth_h + e - 1] for i in range(n_i)])

    ahead = 4
    for e in range(1, ahead + 1):
        place_own(e)

    lanes_e = 256

    def expand(source, lanes):
        return gelu_scaled(dot(source, w_exp[:, lanes]) * HALF_ROOT + b_exp_s[:, lanes])

    def expand_slabs(e, count):
        source = ordered[pl.ds(e, count)].reshape(count * slab, width)
        for n in range(inner // lanes_e):
            lanes = slice(n * lanes_e, (n + 1) * lanes_e)
            value = expand(source, lanes)
            for k in range(count):
                exp[e + k, n_t : n_t + slab, lanes] = value[k * slab : (k + 1) * slab]

    ok_top, ok_bot = has_top.astype(F32), has_bot.astype(F32)
    ok_left, ok_right = has_left.astype(F32), has_right.astype(F32)

    def border_columns(e):
        at = lax.broadcasted_iota(jnp.int32, (n_t, inner), 0)
        left = exp[e, slab : slab + n_t, :]
        right = exp[e, n_t : 2 * n_t, :]
        if n_t > 1:
            left = pltpu.roll(left, 1, 0)
            right = pltpu.roll(right, n_t - 1, 0)
        for i in range(n_i):
            row = i * depth_h + e - 1
            above, below = row < 0, row >= tile_h
            ok = jnp.where(above, ok_top, jnp.where(below, ok_bot, jnp.float32(1)))
            row = jnp.where(above, tile_h, jnp.where(below, tile_h + 1, row))
            left = jnp.where(at == i * n_j, colexp[0, pl.ds(row, 1), :] * (ok_left * ok), left)
            right = jnp.where(
                at == i * n_j + n_j - 1, colexp[1, pl.ds(row, 1), :] * (ok_right * ok), right
            )
        exp[e, 0:n_t, :] = left
        exp[e, n_t + slab : 2 * n_t + slab, :] = right

    pl.semaphore_wait(barrier, count)

    @pl.when(has_right)
    def _():
        rightward.start()

    @pl.when(has_left)
    def _():
        leftward.start()

    @pl.when(has_bot)
    def _():
        down.start()

    @pl.when(has_top)
    def _():
        up.start()

    for copy in weights:
        copy.start()

    for load in small:
        load.wait()
    for di in range(3):
        w_dep[3 * di : 3 * di + 3] = w_dep_in[di].astype(F32) * HALF_ROOT
    b_exp_s[...] = b_exp[...] * HALF_ROOT
    b_dep_s[...] = b_dep[...] * HALF_ROOT
    loads[1].wait()
    loads[3].start()
    loads[4].start()
    expand_slabs(1, ahead)

    @pl.loop(ahead + 1, depth_h + 1)
    def _(e):
        place_own(e)

    def await_or_zero(pairs):
        for buffer, index, there, copy in pairs:
            @pl.when(there)
            def _():
                copy.wait_recv()

            @pl.when(jnp.logical_not(there))
            def _():
                buffer[index] = jnp.zeros(buffer.shape[1:], BF16)

    def expand_columns(source, first):
        rows = source.shape[1]
        flat = source[...].reshape(2 * rows, width)
        for n in range(inner // lanes_e):
            lanes = slice(n * lanes_e, (n + 1) * lanes_e)
            value = expand(flat, lanes)
            colexp[0, first : first + rows, lanes] = value[:rows]
            colexp[1, first : first + rows, lanes] = value[rows:]

    lanes_d = 128
    quarter = part // 2
    some = plan.pairs // 2

    def partial_copy(u):
        return remote(psend.at[u], precv.at[u], p_s, p_r.at[u], partner)

    def slabs_of(u):
        return [2 * lax.div(u, 2) + k for k in range(2)]

    def first_row(core, outer):
        return pl.multiple_of(jnp.where(core == 0, 1 - outer, 2 + outer) * quarter, quarter)

    def depth_unit(u):
        outer = lax.rem(u, 2)
        for chunk in range(inner // lanes_d):
            lanes = slice(chunk * lanes_d, (chunk + 1) * lanes_d)
            for n, at in enumerate(slabs_of(u)):
                a = lax.rem(at + 1, depth_h)
                for core in range(2):
                    window = pl.ds(first_row(core, outer), quarter + 2 * n_t)
                    total = None
                    for di in range(3):
                        rows = exp[a + di, window, lanes]
                        for dj in range(3):
                            k = 3 * di + dj
                            term = rows[dj * n_t : dj * n_t + quarter] * w_dep[k : k + 1, lanes]
                            total = term if total is None else total + term
                    value = gelu_scaled(total + b_dep_s[:, lanes]).astype(BF16)
                    first = pl.multiple_of(jnp.where(c == core, part, 0) + n * quarter, quarter)
                    dbuf[pl.ds(first, quarter), lanes] = value

    def project_unit(u):
        projected = dot(dbuf[...], w_proj[...])
        psend[u] = projected[:part].astype(BF16)
        partial_copy(u).start()
        own = jnp.concatenate([
            ordered[lax.rem(at + 1, depth_h) + 1, pl.ds(first_row(c, lax.rem(u, 2)), quarter)]
            for at in slabs_of(u)
        ], axis=0)
        acc[u] = projected[part:] + own.astype(F32) + b_proj[...]

    def forward_copy(u, pair):
        m, ah = lax.div(u, slabs), lax.rem(u, slabs)
        s = owner(ah, pair)
        return remote(
            fsend.at[u * plan.pairs + pair], frecv.at[m, my_s], f_s, f_r.at[m], peer(s, c)
        )

    def finish(u):
        partial_copy(u).wait_recv()
        mixed = (acc[u] + precv[u].astype(F32)).astype(BF16)
        base = jnp.where(c == lax.rem(u, 2), some, 0)
        for n, at in enumerate(slabs_of(u)):
            for k in range(some):
                rows = slice((n * some + k) * plan.piece, (n * some + k + 1) * plan.piece)
                fsend[at * plan.pairs + base + k] = mixed[rows]
        for k in range(some):
            for at in slabs_of(u):
                pair = base + k
                is_mine = (lax.rem(at, slabs) == my_slab) & (pair == my_pair)

                @pl.when(is_mine)
                def _():
                    frecv[lax.div(at, slabs), my_s] = fsend[at * plan.pairs + pair]

                @pl.when(jnp.logical_not(is_mine))
                def _():
                    forward_copy(at, pair).start()

    eye = (
        lax.broadcasted_iota(jnp.int32, (half, half), 0)
        == lax.broadcasted_iota(jnp.int32, (half, half), 1)
    ).astype(F32).astype(BF16)
    def await_weights():
        loads[3].wait()
        loads[4].wait()
        for copy in weights:
            copy.wait_recv()
        w_vt[:half] = dot_t(eye, w_qkv[2, :, :half]).astype(BF16)
        w_vt[half:] = dot_t(eye, w_qkv[2, :, half:]).astype(BF16)

    def await_batch(m):
        others = frecv.at[m, pl.ds(0, plan.sources - 1)]
        remote(others, others, f_s, f_r.at[m], partner).wait_recv()

    keys = plan.sources * n_t
    tokens = WINDOWS * keys
    group = 128
    n_h = group // HEAD_DIM
    lane = lax.broadcasted_iota(jnp.int32, (1, WINDOWS * 2 * group), 1)
    head_masks = [
        (remainder(quotient(lane, HEAD_DIM), n_h) == h).astype(F32).astype(BF16) for h in range(n_h)
    ]
    lane_w = lax.div(lax.broadcasted_iota(jnp.int32, (1, tokens), 1), keys)
    window_masks = [(lane_w == w).astype(F32).astype(BF16) for w in range(WINDOWS)]
    scale = np.float32(HEAD_DIM ** (-0.5) * np.log2(np.e))
    duos = width // (2 * group)
    eye_t = eye[:tokens, :tokens]

    def attend(normed):
        query = dot(normed, w_qkv[0])
        keyset = dot(normed, w_qkv[1])
        values = dot_t(w_vt[...], normed)
        query = (query * scale).astype(BF16)
        keyset = keyset.astype(BF16)
        values = values.astype(BF16)
        blank = jnp.zeros((keys, group), BF16)
        blocks = [(w, g) for w in range(WINDOWS) for g in range(2)]
        lefts, rights = [], []
        for duo in range(duos):
            rights.append(jnp.concatenate([
                jnp.concatenate([
                    query[w * keys : (w + 1) * keys, (2 * duo + g) * group : (2 * duo + g + 1) * group]
                    if block == (w, g) else blank
                    for block in blocks
                ], axis=1)
                for g in range(2) for w in range(WINDOWS)
            ], axis=0))
            left = jnp.concatenate([
                keyset[w * keys : (w + 1) * keys, 2 * duo * group : (2 * duo + 2) * group]
                for w in range(WINDOWS)
            ], axis=1)
            lefts.append(jnp.concatenate([left * mask for mask in head_masks], axis=0))
        scores = [dot_t(left, right) for left, right in zip(lefts, rights)]
        nothing = jnp.zeros((HEAD_DIM, tokens), BF16)
        stacked, spreads, shares = [], [], []
        for duo in range(duos):
            score = scores[duo].reshape(n_h, keys, 2 * tokens)
            top = jnp.max(score, axis=1, keepdims=True)
            power = jnp.exp2(score - top)
            share = 1.0 / jnp.sum(power, axis=1, keepdims=True)
            power = power.astype(BF16)
            for g in range(2):
                lanes = slice(g * tokens, (g + 1) * tokens)
                shares.append(share[:, :, lanes])
                spreads.append(jnp.concatenate(
                    [power[h, :, lanes] * mask for h in range(n_h) for mask in window_masks], axis=0
                ))
                first = (2 * duo + g) * group
                stacked.append(jnp.concatenate([
                    jnp.concatenate([
                        values[first + h * HEAD_DIM : first + (h + 1) * HEAD_DIM]
                        if h == at else nothing
                        for at in range(n_h)
                    ], axis=1)
                    for h in range(n_h)
                ], axis=0))
        found = [dot(a, b) for a, b in zip(stacked, spreads)]
        found = jnp.concatenate([
            (f.reshape(n_h, HEAD_DIM, tokens) * share).reshape(group, tokens).astype(BF16)
            for f, share in zip(found, shares)
        ], axis=0)
        return dot_t(eye_t, found).astype(BF16)

    def return_copy(m, s, side):
        return remote(
            osend.at[(m * plan.sources + s) * 2 + side], oin.at[m, (my_slab * 2 + c) * plan.pairs + my_pair],
            o_s, o_r.at[m], peer(s, side),
        )

    def attend_batch(m):
        await_batch(m)
        came = frecv[m].astype(F32)
        mixed = jnp.concatenate([
            came[:, w * n_t : (w + 1) * n_t].reshape(keys, width) for w in range(WINDOWS)
        ], axis=0)
        centered = mixed - jnp.mean(mixed, axis=-1, keepdims=True)
        spread = jnp.mean(centered * centered, axis=-1, keepdims=True)
        normed = (centered * lax.rsqrt(spread + 1e-05) * gain[...]).astype(BF16)
        total = mixed + dot(attend(normed), w_out[...])
        for side in range(2):
            lanes = slice(side * half, (side + 1) * half)
            value = total[:, lanes] + bo_full[side]
            value = jnp.concatenate([
                value[w * keys : (w + 1) * keys].reshape(plan.sources, n_t, half)
                for w in range(WINDOWS)
            ], axis=1)
            value = value.astype(BF16)
            for at in range(plan.sources):
                osend[(m * plan.sources + at) * 2 + side] = value[at]

        oin[m, (my_slab * 2 + c) * plan.pairs + my_pair] = osend[(m * plan.sources + my_s) * 2 + c]
        for k in farthest_first(plan.sources):
            for side in range(2):
                return_copy(m, lax.rem(my_s + k, plan.sources), side).start()
        return_copy(m, my_s, 1 - c).start()

    loads[2].wait()
    token_row = lax.broadcasted_iota(jnp.int32, (slab, 1), 0)
    token_i = remainder(quotient(token_row, n_j), n_i)

    def bottleneck(u):
        @pl.when(u == (depth_h - ahead) // 2)
        def _():
            await_or_zero(((halo, 0, has_top, down), (halo, 1, has_bot, up)))
            place(0, [halo[0]] + [cells[i * depth_h - 1] for i in range(1, n_i)])
            place(depth_h + 1, [cells[i * depth_h] for i in range(1, n_i)] + [halo[1]])
            at_row = lax.broadcasted_iota(jnp.int32, edge_x.shape[1:], 0)
            for side, col in ((0, 0), (1, tile_w - 1)):
                top = halo[0].astype(F32)[col : col + 1]
                bottom = halo[1].astype(F32)[col : col + 1]
                edge_x[side] = jnp.where(at_row == 0, top, bottom).astype(BF16)

            @pl.when(has_right)
            def _():
                rightward_x.start()

            @pl.when(has_left)
            def _():
                leftward_x.start()

        depth_unit(u)
        project_unit(u)

    def look_ahead(u):
        @pl.when(u == depth_h - ahead)
        def _():
            await_or_zero(((colin_x, 0, has_left, rightward_x), (colin_x, 1, has_right, leftward_x)))
            expand_columns(colin_x, tile_h)

        @pl.when(u < depth_h - ahead)
        def _():
            expand_slabs(u + 1 + ahead, 2)

        @pl.when(u == depth_h - ahead)
        def _():
            for e in (0, depth_h + 1):
                expand_slabs(e, 1)

        @pl.loop(0, 2)
        def _(k):
            e = lax.rem(u + 1 + ahead + k, depth_h + 2)

            @pl.when((e == 0) | (e == depth_h + 1))
            def _():
                outside = jnp.where(
                    e == 0,
                    jnp.where(token_i == 0, 1 - ok_top, 0.0),
                    jnp.where(token_i == n_i - 1, 1 - ok_bot, 0.0),
                )
                exp[e, n_t : n_t + slab] = exp[e, n_t : n_t + slab] * (1 - outside)

            @pl.when(u > 0)
            def _():
                border_columns(e)

    def first_columns():
        await_or_zero(((colin, 0, has_left, rightward), (colin, 1, has_right, leftward)))
        expand_columns(colin, 0)

        @pl.loop(1, ahead + 3)
        def _(e):
            border_columns(e)

    lag = depth_h

    @pl.loop(0, lag + plan.batches)
    def _(t):
        @pl.when(t < depth_h)
        def _():
            bottleneck(t)

        @pl.when(t == lag)
        def _():
            await_weights()

        @pl.when((t > 1) & (t <= depth_h))
        def _():
            finish(t - 1)

        @pl.when((lax.rem(t, 2) == 0) & (t < depth_h - 2))
        def _():
            look_ahead(t)

        @pl.when(t == 0)
        def _():
            finish(t)
            first_columns()

        @pl.when(t >= lag)
        def _():
            attend_batch(t - lag)

    @pl.when(has_bot)
    def _():
        down.wait_send()

    @pl.when(has_top)
    def _():
        up.wait_send()

    @pl.when(has_right)
    def _():
        rightward.wait_send()
        rightward_x.wait_send()

    @pl.when(has_left)
    def _():
        leftward.wait_send()
        leftward_x.wait_send()

    for copy in weights:
        copy.wait_send()

    remote(psend, psend, p_s, p_r.at[0], partner).wait_send()
    sent = fsend.at[pl.ds(0, depth_h * plan.pairs - plan.batches)]
    remote(sent, sent, f_s, f_r.at[0], partner).wait_send()

    perm_t = one_hot(slab, slab, lambda row, column: cell_of(column) == row)

    @pl.loop(0, plan.batches)
    def _(m):
        others = oin.at[m, pl.ds(0, 2 * plan.sources - 1)]
        remote(others, others, o_s, o_r.at[m], partner).wait_recv()
        pieces = 2 * plan.pairs
        arrived = jnp.concatenate([
            oin[m, ah * pieces : (ah + 1) * pieces].astype(F32).reshape(slab, half).astype(BF16)
            for ah in range(slabs)
        ], axis=1)
        placed = dot(perm_t, arrived).astype(BF16)
        for ah in range(slabs):
            a = lax.rem(m * slabs + ah + 1, depth_h)
            for i in range(n_i):
                row = i * depth_h + a
                cell_rows = slice(i * tile_w, (i + 1) * tile_w)
                result[row] = placed[cell_rows, ah * half : (ah + 1) * half]
                pltpu.make_async_copy(result.at[row], out.at[row], out_s).start()

    sent = osend.at[pl.ds(0, plan.batches * (2 * plan.sources - 1))]
    remote(sent, sent, o_s, o_r.at[0], partner).wait_send()
    pltpu.make_async_copy(result, out, out_s).wait()


def per_device(
    mesh_shape, cells, w_expand, b_expand, w_depth, b_depth, w_project, b_project, ln_gain,
    w_qkv, w_out, b_out,
):
    tile_h, tile_w, width = cells.shape
    plan = Plan(mesh_shape, tile_h, tile_w)
    inner = w_expand.shape[1]
    half = width // 2
    args = (
        cells, w_expand, b_expand[None], w_depth, b_depth[None],
        w_project, b_project[None], ln_gain[None], w_qkv.transpose(1, 0, 2), w_out, b_out[None],
    )
    dma = pltpu.SemaphoreType.DMA
    vmem = pltpu.VMEM
    n = plan
    rows_x = 16
    return pl.pallas_call(
        functools.partial(kernel, plan),
        out_shape=jax.ShapeDtypeStruct((tile_h, tile_w, half), BF16),
        in_specs=[
            pl.BlockSpec(memory_space=pl.ANY) for _ in args
        ],
        out_specs=pl.BlockSpec(memory_space=pl.ANY),
        scratch_shapes=[
            vmem((1, inner), F32), vmem(w_depth.shape, BF16), vmem((1, inner), F32),
            vmem((1, width), F32), vmem((1, width), F32),
            vmem(cells.shape, BF16), vmem((n.depth_h + 2, n.slab, width), BF16),
            vmem(w_expand.shape, BF16), vmem(w_project.shape, BF16),
            vmem((3, width, width), BF16), vmem((width, width), BF16), vmem((9, inner), F32),
            vmem((n.depth_h + 2, n.slab + 2 * n.n_t, inner), F32),
            vmem((2, tile_w, width), BF16),
            vmem((2, tile_h, width), BF16),
            vmem((2, tile_h, width), BF16),
            vmem((2, rows_x, width), BF16),
            vmem((2, rows_x, width), BF16),
            vmem((2, tile_h + rows_x, inner), F32),
            vmem((n.slab, inner), BF16),
            vmem((n.depth_h, n.part, width), BF16),
            vmem((n.depth_h, n.part, width), BF16),
            vmem((n.depth_h, n.part, width), F32),
            vmem((n.depth_h * n.pairs, n.piece, width), BF16),
            vmem((n.batches, n.sources, n.piece, width), BF16),
            vmem((1, inner), F32), vmem((1, inner), F32),
            vmem((width, width), BF16),
            vmem((2, 1, half), F32),
            vmem((n.batches * n.sources * 2, n.piece, half), BF16),
            vmem((n.batches, n.sources * 2, n.piece, half), BF16),
            vmem((tile_h, tile_w, half), BF16),
            dma, dma((11,)),
            dma((2,)), dma((2,)), dma((4,)), dma((4,)), dma((3,)), dma((3,)),
            dma, dma((n.depth_h,)), dma, dma((n.batches,)), dma, dma((n.batches,)),
        ],
        compiler_params=pltpu.CompilerParams(
            collective_id=0, has_side_effects=True, vmem_limit_bytes=60 << 20
        ),
    )(*args)


def solution(mesh):
    placed = (
        P(("grp", "gy"), "gx", None),
        P(None, "ch"),
        P("ch"),
        P(None, None, "ch"),
        P("ch"),
        P("ch", None),
        P(),
        P(),
        P(None, None, "ch"),
        P("ch", None),
        P("ch"),
    )
    return jax.shard_map(
        functools.partial(per_device, dict(mesh.shape)),
        mesh=mesh,
        in_specs=placed,
        out_specs=P(("grp", "gy"), "gx", "ch"),
        check_vma=False,
    )
```
